32 devices in a mesh: seq: 8 (over y, x, core), head: 4 (over z).
Axes of the slice: x: 2, y: 2, z: 4, core: 2. Of those that a mesh axis runs over, the one named last changes fastest.
Arguments:
- tokens: bfloat16 [2048, 2048], P('seq'), may hold values from -18 to 18
- qkv_weight: bfloat16 [3, 2048, 2048], P(None, None, 'head'), may hold values from -1 to 1
- beta_logit: float32 [16, 2048], P('head', 'seq'), may hold values from -5.8 to -3.5
- log_decay: float32 [16, 2048], P('head', 'seq'), may hold values from -1 to 0
- out_grad: bfloat16 [2048, 2048], P('seq', 'head'), may hold values from -24 to 24
Outputs:
- input_grad: bfloat16 [2048, 2048], P('seq', 'head')
The draws below stay inside these ranges and needn't reach their ends.
All inputs are finite; a program needn't handle non-finite values.
Results may differ from the reference program's by a relative error of at most 0.008.
Values may be sent and summed in bfloat16 or wider, within the bound.
No kernel may reach another device: no remote copies, remote signals or barrier semaphores. Data moves between devices by JAX's collectives and lax.ppermute only.
A program may use at most 64 MiB of HBM per device.

```python
import math
import jax
import jax.numpy as jnp
from jax import lax

D = 2048
HEADS = 16
DK = 128
TOK_DEV = 256
TOKENS = 2048


def draw_tokens(key, part):
    streams = jax.random.split(key, 2)
    scales = jnp.exp(jax.random.uniform(streams[0], (TOKENS, 1), jnp.float32, math.log(0.3), math.log(3.0)))
    entries = jnp.clip(jax.random.normal(streams[1], (TOKENS, D), jnp.float32), -6.0, 6.0)
    return (scales * entries).astype(jnp.bfloat16)


def draw_qkv_weight(key, part):
    streams = jax.random.split(key, 2)
    column_scales = jnp.exp(jax.random.uniform(streams[0], (3, 1, HEADS * DK), jnp.float32, math.log(0.32), math.log(3.2)))
    base = jnp.clip(jax.random.normal(streams[1], (3, D, HEADS * DK), jnp.float32), -2.5, 2.5)
    return (base * column_scales / math.sqrt(D)).astype(jnp.bfloat16)


def draw_log_decay(key, part):
    streams = jax.random.split(key, 7)
    share = 0.5
    slow_heads = jax.random.uniform(streams[0], (HEADS, 1), jnp.float32) < share
    fast_rate = jnp.exp(jax.random.uniform(streams[1], (HEADS, 1), jnp.float32, math.log(1.0 / 50.0), math.log(1.0 / 30.0)))
    slow_rate = jnp.exp(jax.random.uniform(streams[2], (HEADS, 1), jnp.float32, math.log(0.05), math.log(0.3))) / TOKENS
    forget_factors = jnp.where(slow_heads, slow_rate, fast_rate)
    piece_scaling_factor = jnp.exp(jax.random.uniform(streams[3], (HEADS, TOKENS // TOK_DEV), jnp.float32, math.log(0.5), math.log(2.0)))
    piece_scaling_factor = jnp.repeat(piece_scaling_factor, TOK_DEV, axis=1)
    element_scaling_factor = jax.random.uniform(streams[4], (HEADS, TOKENS), jnp.float32, 0.5, 1.5)
    element_slots = jax.random.randint(streams[5], (2, 1), 0, TOKENS)
    element_offsets = jnp.arange(TOKENS)[None, :]
    piece_groupings = jnp.sum((element_offsets == element_slots).astype(jnp.float32), axis=0)[None, :]
    objective_scores = jax.random.uniform(streams[6], (HEADS, TOKENS), jnp.float32, 0.22, 0.4)
    return -forget_factors * piece_scaling_factor * element_scaling_factor - piece_groupings * objective_scores


def block_scale(rng, dims, shards, smallest, largest):
    def one(position, blocks):
        heights = jax.random.uniform(jax.random.fold_in(jax.random.fold_in(rng, 6), position), (blocks,), jnp.float32, smallest / len(shards), largest / len(shards))
        return jnp.repeat(jnp.exp(heights), dims[position] // blocks).reshape((-1,) + (1,) * (len(dims) - position - 1))

    level = one(*shards[0])
    for cut in shards[1:]:
        level = level * one(*cut)
    return level


def scatter_about(rng, dims, deviation, limit, cuts=(), kind=jnp.bfloat16):
    values = deviation * jax.random.normal(rng, dims, jnp.float32)
    if cuts:
        values = values * block_scale(rng, dims, cuts, -0.22, 0.18)
    return jnp.clip(values, -limit, limit).astype(kind)


def setup_inputs(seed: int = 0) -> dict:
    streams_of = jax.random.split(jax.random.key(seed), 6)
    return {
        "tokens": draw_tokens(jax.random.fold_in(streams_of[5], 71), 0),
        "qkv_weight": draw_qkv_weight(jax.random.fold_in(streams_of[5], 71), 0),
        "beta_logit": jnp.clip(-5.8 + 2.3000002 * jax.random.uniform(streams_of[2], (HEADS, TOKENS), jnp.float32) ** block_scale(streams_of[2], (HEADS, TOKENS), ((0, 4), (1, 8)), -0.2, 0.2), -5.8, -3.5),
        "log_decay": draw_log_decay(jax.random.fold_in(streams_of[5], 71), 0),
        "out_grad": scatter_about(streams_of[4], (TOKENS, HEADS * DK), 4.0, 24.0, ((0, 8), (1, 4))),
    }


HIGH = lax.Precision.HIGHEST
block_tokens = 64

def unit_rows(tensor):
    return tensor * lax.rsqrt(lax.optimization_barrier(jnp.sum(tensor * tensor, axis=-1, keepdims=True)) + 1e-06)

def head_grad(queries, key_rows, values, log_decay, strengths, cotangent):
    length, head_width = queries.shape
    block_size = min(block_tokens, length)
    blocks = length // block_size

    def advance(memory, inputs):
        query_row, key_row, value_row, decay_row, strength_row = inputs
        kept = jnp.exp(decay_row) * memory
        recall = jnp.dot(key_row, kept, precision=HIGH)
        memory = kept + strength_row * jnp.outer(key_row, value_row - recall)
        return (memory, jnp.dot(query_row, memory, precision=HIGH))

    def run_block(memory, inputs):
        return lax.scan(advance, memory, inputs)
    checked = jax.checkpoint(run_block)

    def forward(query_in, key_in, value_in):
        unit_query = unit_rows(query_in)
        unit_key = unit_rows(key_in)
        pieces = (unit_query, unit_key, value_in, log_decay, strengths)
        blocked = tuple((tensor.reshape((blocks, block_size) + tensor.shape[1:]) for tensor in pieces))
        zeroed = jnp.zeros((head_width, head_width), jnp.float32)
        _, results = lax.scan(checked, zeroed, blocked)
        return results.reshape(length, head_width)
    _, pullback = jax.vjp(forward, queries, key_rows, values)
    return pullback(cotangent)

def reference(tokens, qkv_weight, beta_logit, log_decay, out_grad):
    total_rows = tokens.shape[0]
    heads = beta_logit.shape[0]
    head_width = qkv_weight.shape[-1] // heads

    def per_head(tensor):
        return tensor.reshape(total_rows, heads, head_width).transpose(1, 0, 2)
    projected = [per_head(jnp.dot(tokens, qkv_weight[member], preferred_element_type=jnp.float32)) for member in range(3)]
    strengths = jax.nn.sigmoid(beta_logit)
    cotangent = per_head(out_grad.astype(jnp.float32))

    def one_head(pieces):
        return head_grad(pieces[0], pieces[1], pieces[2], pieces[3], pieces[4], pieces[5])
    grads = lax.map(one_head, (projected[0], projected[1], projected[2], log_decay, strengths, cotangent))
    result = jnp.zeros((total_rows, tokens.shape[1]), jnp.float32)
    for member in range(3):
        flat = grads[member].transpose(1, 0, 2).reshape(total_rows, heads * head_width)
        weight_full = qkv_weight[member].astype(jnp.float32)
        result = result + jnp.dot(flat, weight_full.T, precision=HIGH)
    return result.astype(jnp.bfloat16)
```

```python
import functools

import jax
import jax.numpy as jnp
from jax import lax
from jax.experimental import pallas as pl
from jax.experimental.pallas import tpu as pltpu
from jax.sharding import PartitionSpec as P

F32 = jnp.float32
BF16 = jnp.bfloat16
HIGH = lax.Precision.HIGHEST
FAR = -1e30
BASE = 64


def nn(a, b):
    return lax.dot_general(a, b, (((1,), (0,)), ((), ())), preferred_element_type=F32)


def nt(a, b):
    return lax.dot_general(a, b, (((1,), (1,)), ((), ())), preferred_element_type=F32)


def fine(a, b, dims=(1, 0)):
    return lax.dot_general(
        a, b, (((dims[0],), (dims[1],)), ((), ())), precision=HIGH, preferred_element_type=F32
    )


def grid_ids(size):
    rows = lax.broadcasted_iota(jnp.int32, (size, size), 0)
    cols = lax.broadcasted_iota(jnp.int32, (size, size), 1)
    return rows, cols


def gates(logit, decay):
    size = decay.shape[1]
    rows, cols = grid_ids(size)
    lower = jnp.where(rows >= cols, 1.0, 0.0).astype(F32)
    eye = jnp.where(rows == cols, 1.0, 0.0).astype(F32)
    strength = 1.0 / (1.0 + jnp.exp(-logit))
    run_row = fine(decay, lower, (1, 1))
    run_col = fine(lower, decay, (1, 1))
    strength_col = fine(eye, strength, (1, 1))
    return strength, strength_col, run_row, run_col


def unit_rows(tensor):
    scale = lax.rsqrt(jnp.sum(tensor * tensor, axis=-1, keepdims=True) + 1e-06)
    return tensor * scale, scale


def unit_lower_inverse(couplings, rows, cols):
    size = couplings[0].shape[0]
    base = min(BASE, size)
    same = (rows // base) == (cols // base)
    power = [jnp.where(same, a, 0.0).astype(BF16) for a in couplings]
    rest = [-jnp.where(same, a, 0.0) for a in couplings]
    reach = 2
    if reach < base:
        power = [nn(a, a) for a in power]
    while reach < base:
        narrow = [a.astype(BF16) for a in power]
        rest = [n + p + nn(n.astype(BF16), b) for n, p, b in zip(rest, power, narrow)]
        reach *= 2
        if reach < base:
            power = [nn(b, b) for b in narrow]
    while base < size:
        wide = 2 * base
        off = jnp.logical_and((rows // wide) == (cols // wide), (rows // base) != (cols // base))
        outer = [jnp.where(off, a, 0.0) for a in couplings]
        narrow = [n.astype(BF16) for n in rest]
        half = [a + nn(a.astype(BF16), n) for a, n in zip(outer, narrow)]
        rest = [n - (y + nn(b, y.astype(BF16))) for n, b, y in zip(rest, narrow, half)]
        base = wide
    return rest


def prepare_kernel(
    heads, half, tok_ref, w_ref, logit_ref, decay_ref, og_ref,
    proj_ref, u_ref, wk_ref, dbt_ref, ktt_ref, keep_ref, send_ref,
    value_scr, pay_scr,
):
    member = pl.program_id(0)
    result = nn(tok_ref[...], w_ref[0])

    @pl.when(member < 2)
    def _():
        proj_ref[member] = result

    @pl.when(member == 2)
    def _():
        value_scr[...] = result
        size = tok_ref.shape[0]
        width = w_ref.shape[2] // heads
        rows, cols = grid_ids(size)
        causal = rows >= cols
        strict = rows > cols
        strength, strength_col, run_row, run_col = gates(logit_ref[...], decay_ref[...])
        every = range(heads)
        spans = [slice(h * width, (h + 1) * width) for h in every]
        queries = [unit_rows(proj_ref[0, :, s])[0] for s in spans]
        keys = [unit_rows(proj_ref[1, :, s])[0] for s in spans]
        key_b = [k.astype(BF16) for k in keys]
        query_b = [q.astype(BF16) for q in queries]
        gamma = [
            jnp.exp(jnp.where(causal, run_col[:, h : h + 1] - run_row[h : h + 1, :], FAR))
            for h in every
        ]
        couplings = [
            jnp.where(strict, strength_col[:, h : h + 1] * gamma[h] * nt(key_b[h], key_b[h]), 0.0)
            for h in every
        ]
        scores = [(gamma[h] * nt(query_b[h], key_b[h])).astype(BF16) for h in every]
        inverse = [n.astype(BF16) for n in unit_lower_inverse(couplings, rows, cols)]
        last = [run_col[size - 1 : size, h : h + 1] for h in every]
        open_col = [jnp.exp(run_col[:, h : h + 1]) for h in every]
        fade_row = [jnp.exp(last[h] - run_row[h : h + 1, :]) for h in every]
        write_key = [strength_col[:, h : h + 1] * open_col[h] * keys[h] for h in every]
        right = [
            jnp.concatenate(
                [strength_col[:, h : h + 1] * value_scr[:, spans[h]], write_key[h]], axis=1
            )
            for h in every
        ]
        solved = [right[h] + nn(inverse[h], right[h].astype(BF16)) for h in every]
        grad_t = [og_ref[:, s].astype(F32).T.astype(BF16) for s in spans]
        fade_t = [keys[h].T * fade_row[h] for h in every]
        left = [jnp.concatenate([nn(grad_t[h], scores[h]), fade_t[h]], axis=0) for h in every]
        back = [left[h] + nn(left[h].astype(BF16), inverse[h]) for h in every]
        e_rows, e_cols = grid_ids(width)
        for h in every:
            state = nn(fade_t[h].astype(BF16), solved[h].astype(BF16))
            unit = jnp.where(e_rows == e_cols, jnp.exp(last[h]), 0.0)
            seed = nn(grad_t[h], (open_col[h] * queries[h]).astype(BF16)) - nn(
                back[h][:width].astype(BF16), write_key[h].astype(BF16)
            )
            pay_scr[h, 0] = (unit - state[:, width:]).astype(BF16)
            pay_scr[h, 1] = state[:, :width].astype(BF16)
            pay_scr[h, 2] = seed.astype(BF16)
            u_ref[h] = solved[h][:, :width]
            wk_ref[h] = solved[h][:, width:].astype(BF16)
            dbt_ref[h] = back[h][:width]
            ktt_ref[h] = back[h][width:].astype(BF16)
        if half:
            core = lax.rem(lax.axis_index("seq"), 2)
            keep_ref[...] = pay_scr[pl.ds(core * half, half)]
            send_ref[...] = pay_scr[pl.ds((1 - core) * half, half)]
        else:
            keep_ref[...] = pay_scr[...]
            send_ref[...] = pay_scr[...]


def prepare(tokens, weights, logit, decay, out_grad, half):
    heads, size = logit.shape
    members, depth, columns = weights.shape
    width = columns // heads
    part = half or heads
    whole = lambda *shape: pl.BlockSpec(shape, lambda p: (0,) * len(shape))
    return pl.pallas_call(
        functools.partial(prepare_kernel, heads, half),
        grid=(members,),
        in_specs=[
            whole(size, depth),
            pl.BlockSpec((1, depth, columns), lambda p: (p, 0, 0)),
            whole(heads, size),
            whole(heads, size),
            whole(size, columns),
        ],
        out_specs=[
            whole(2, size, columns),
            whole(heads, size, width),
            whole(heads, size, width),
            whole(heads, width, size),
            whole(heads, width, size),
            whole(part, 3, width, width),
            whole(part, 3, width, width),
        ],
        out_shape=[
            jax.ShapeDtypeStruct((2, size, columns), F32),
            jax.ShapeDtypeStruct((heads, size, width), F32),
            jax.ShapeDtypeStruct((heads, size, width), BF16),
            jax.ShapeDtypeStruct((heads, width, size), F32),
            jax.ShapeDtypeStruct((heads, width, size), BF16),
            jax.ShapeDtypeStruct((part, 3, width, width), BF16),
            jax.ShapeDtypeStruct((part, 3, width, width), BF16),
        ],
        scratch_shapes=[
            pltpu.VMEM((size, columns), F32),
            pltpu.VMEM((heads, 3, width, width), BF16),
        ],
        name="prepare",
    )(tokens, weights, logit, decay, out_grad)


def pair_kernel(levels, keep_ref, recv_ref, *pay_refs):
    place = lax.axis_index("seq")
    first = lax.rem(place, 2) == 0
    chip = place // 2
    for h in range(keep_ref.shape[0]):
        mine = [keep_ref[h, i].astype(F32) for i in range(3)]
        other = [recv_ref[h, i].astype(F32) for i in range(3)]
        early = [jnp.where(first, a, b) for a, b in zip(mine, other)]
        late = [jnp.where(first, b, a) for a, b in zip(mine, other)]
        joint = fine(late[0], early[0]).astype(BF16)
        up = (fine(late[0], early[1]) + late[1]).astype(BF16)
        down = (fine(late[2], early[0]) + early[2]).astype(BF16)
        for level in range(levels):
            upward = lax.rem(chip // (1 << level), 2) == 0
            pay_refs[level][h, 0] = joint
            pay_refs[level][h, 1] = jnp.where(upward, up.astype(F32), down.astype(F32)).astype(BF16)


def join_pair(keep, recv, levels):
    half, _, width, _ = keep.shape
    shape = jax.ShapeDtypeStruct((half, 2, width, width), BF16)
    return pl.pallas_call(
        functools.partial(pair_kernel, levels), out_shape=[shape] * levels, name="join_pair"
    )(keep, recv)


def scan_kernel(chips, keep_ref, recv_ref, *refs):
    got_refs, (own_ref, send_ref, store, state) = refs[: chips - 1], refs[chips - 1 :]
    place = lax.axis_index("seq")
    first = lax.rem(place, 2) == 0
    chip = place // 2
    half = keep_ref.shape[0]
    for d in range(1, chips):
        store[d] = got_refs[d - 1][...]
    state[...] = jnp.zeros_like(state)

    def forward(j, carry):
        d = j ^ chip
        for h in range(half):
            state[h, 0] = fine(store[d, h, 0].astype(F32), state[h, 0]) + store[d, h, 1].astype(F32)
        return carry

    def backward(i, carry):
        d = (chips - 1 - i) ^ chip
        for h in range(half):
            state[h, 1] = fine(state[h, 1], store[d, h, 0].astype(F32)) + store[d, h, 1].astype(F32)
        return carry

    lax.fori_loop(0, chip, forward, 0)
    lax.fori_loop(0, chips - 1 - chip, backward, 0)
    for h in range(half):
        mine = [keep_ref[h, i].astype(F32) for i in range(3)]
        other = [recv_ref[h, i].astype(F32) for i in range(3)]
        early = [jnp.where(first, a, b) for a, b in zip(mine, other)]
        late = [jnp.where(first, b, a) for a, b in zip(mine, other)]
        enter = state[h, 0]
        leave = state[h, 1]
        middle = fine(early[0], enter) + early[1]
        inner = fine(leave, late[0]) + late[2]
        own_ref[h, 0] = jnp.where(first, enter, middle).astype(BF16)
        own_ref[h, 1] = jnp.where(first, inner, leave).astype(BF16)
        send_ref[h, 0] = jnp.where(first, middle, enter).astype(BF16)
        send_ref[h, 1] = jnp.where(first, leave, inner).astype(BF16)


def scan_chips(keep, recv, got):
    half, _, width, _ = keep.shape
    chips = len(got) + 1
    shape = jax.ShapeDtypeStruct((half, 2, width, width), BF16)
    return pl.pallas_call(
        functools.partial(scan_kernel, chips),
        out_shape=[shape, shape],
        scratch_shapes=[
            pltpu.VMEM((chips, half, 2, width, width), BF16),
            pltpu.VMEM((half, 2, width, width), F32),
        ],
        name="scan_chips",
    )(keep, recv, *got)


def finish_kernel(
    heads, half, order_ref, w_ref, proj_ref, u_ref, wk_ref, dbt_ref, ktt_ref, logit_ref, decay_ref,
    og_ref, own_ref, recv_ref, out_ref, grad_scr, edge_scr,
):
    @pl.when(pl.program_id(0) == 0)
    def _():
        size = og_ref.shape[0]
        width = og_ref.shape[1] // heads
        if half:
            core = lax.rem(lax.axis_index("seq"), 2)
            edge_scr[pl.ds(core * half, half)] = own_ref[...]
            edge_scr[pl.ds((1 - core) * half, half)] = recv_ref[...]
        else:
            edge_scr[...] = own_ref[...]
        rows, cols = grid_ids(size)
        strength, strength_col, run_row, run_col = gates(logit_ref[...], decay_ref[...])
        every = range(heads)
        spans = [slice(h * width, (h + 1) * width) for h in every]
        last = [run_col[size - 1 : size, h : h + 1] for h in every]
        beta = [strength_col[:, h : h + 1] for h in every]
        beta_row = [strength[h : h + 1, :] for h in every]
        open_col = [jnp.exp(run_col[:, h : h + 1]) for h in every]
        fade_col = [jnp.exp(last[h] - run_col[:, h : h + 1]) for h in every]
        gap = [run_col[:, h : h + 1] - run_row[h : h + 1, :] for h in every]
        gamma = [jnp.exp(jnp.where(rows >= cols, gap[h], FAR)) for h in every]
        gamma_t = [jnp.exp(jnp.where(rows <= cols, -gap[h], FAR)) for h in every]
        query = [unit_rows(proj_ref[0, :, s]) for s in spans]
        key = [unit_rows(proj_ref[1, :, s]) for s in spans]
        query_b = [q[0].astype(BF16) for q in query]
        key_b = [k[0].astype(BF16) for k in key]
        grad = [og_ref[:, s] for s in spans]
        grad_t = [g.astype(F32).T.astype(BF16) for g in grad]
        update = [(u_ref[h] - nn(wk_ref[h], edge_scr[h, 0])).astype(BF16) for h in every]
        delta_t = [dbt_ref[h] + nn(edge_scr[h, 1], ktt_ref[h]) for h in every]
        delta = [d.T for d in delta_t]
        delta_b = [d.astype(BF16) for d in delta]
        for h in every:
            lanes = nt(jnp.concatenate([grad[h], delta_b[h]], axis=0), update[h])
            turned = nn(update[h], jnp.concatenate([grad_t[h], delta_t[h].astype(BF16)], axis=1))
            attend = (gamma[h] * lanes[:size]).astype(BF16)
            attend_t = (gamma_t[h] * turned[:, :size]).astype(BF16)
            mix = jnp.where(rows > cols, beta[h] * gamma[h] * lanes[size:], 0.0) + jnp.where(
                rows < cols, beta_row[h] * gamma_t[h] * turned[:, size:], 0.0
            )
            edge = nt(jnp.concatenate([grad[h], delta_b[h]], axis=0), edge_scr[h, 0])
            dq = open_col[h] * edge[:size] + nn(attend, key_b[h])
            dk = (
                nn(attend_t, query_b[h])
                - nn(mix.astype(BF16), key_b[h])
                + fade_col[h] * nn(update[h], edge_scr[h, 1])
                - beta[h] * open_col[h] * edge[size:]
            )
            for slot, (unit, scale), slope in ((0, query[h], dq), (1, key[h], dk)):
                along = jnp.sum(unit * slope, axis=-1, keepdims=True)
                grad_scr[slot, :, spans[h]] = (scale * (slope - unit * along)).astype(BF16)
            grad_scr[2, :, spans[h]] = (beta[h] * delta[h]).astype(BF16)

    total = nt(grad_scr[0], w_ref[0])
    for member in range(1, w_ref.shape[0]):
        total = total + nt(grad_scr[member], w_ref[member])
    out_ref[0] = total


def finish(weights, proj, u, wk, dbt, ktt, logit, decay, out_grad, own, recv, half):
    heads, size = logit.shape
    members, depth, columns = weights.shape
    width = columns // heads
    parts = lax.axis_size("head")
    step = depth // parts
    place = lax.axis_index("head")
    order = lax.rem(place + jnp.arange(parts, dtype=jnp.int32), parts)
    whole = lambda *shape: pl.BlockSpec(shape, lambda p, order: (0,) * len(shape))
    return pl.pallas_call(
        functools.partial(finish_kernel, heads, half),
        grid_spec=pltpu.PrefetchScalarGridSpec(
            num_scalar_prefetch=1,
            grid=(parts,),
            in_specs=[
                pl.BlockSpec((members, step, columns), lambda p, order: (0, order[p], 0)),
                whole(*proj.shape),
                whole(*u.shape),
                whole(*wk.shape),
                whole(*dbt.shape),
                whole(*ktt.shape),
                whole(*logit.shape),
                whole(*decay.shape),
                whole(*out_grad.shape),
                whole(*own.shape),
                whole(*recv.shape),
            ],
            out_specs=pl.BlockSpec((1, size, step), lambda p, order: (p, 0, 0)),
            scratch_shapes=[
                pltpu.VMEM((3, size, columns), BF16),
                pltpu.VMEM((heads, 2, width, width), BF16),
            ],
        ),
        out_shape=jax.ShapeDtypeStruct((parts, size, step), F32),
        name="finish",
    )(order, weights, proj, u, wk, dbt, ktt, logit, decay, out_grad, own, recv)


def swap(value, axis, count, mask):
    return lax.ppermute(value, axis, [(i, i ^ mask) for i in range(count)])


def edges_by_pairs(keep, send, count):
    chips = count // 2
    levels = chips.bit_length() - 1
    recv = swap(send, "seq", count, 1)
    pays = join_pair(keep, recv, levels)
    got = [swap(pays[d.bit_length() - 1], "seq", count, 2 * d) for d in range(1, chips)]
    own, away = scan_chips(keep, recv, got)
    return own, swap(away, "seq", count, 1)


def edges_by_gather(keep, count):
    place = lax.axis_index("seq")
    gathered = lax.all_gather(keep, "seq")
    product = functools.partial(jnp.einsum, "hij,hjk->hik", precision=HIGH)

    def take(j):
        return lax.dynamic_index_in_dim(gathered, j, 0, False).astype(F32)

    def forward(j, state):
        part = take(j)
        return product(part[:, 0], state) + part[:, 1]

    def backward(i, state):
        part = take(count - 1 - i)
        return product(state, part[:, 0]) + part[:, 2]

    vacant = jnp.zeros(keep.shape[:1] + keep.shape[2:], F32)
    enter = lax.fori_loop(0, place, forward, vacant)
    leave = lax.fori_loop(0, count - 1 - place, backward, vacant)
    own = jnp.stack([enter, leave], axis=1).astype(BF16)
    return own, own


def sum_over_heads(blocks):
    count = lax.axis_size("head")
    right = left = None
    for turn in range(count - 1):
        onward = blocks[count - 1 - turn]
        back = blocks[turn + 1]
        if turn:
            onward = onward + right.astype(F32)
            back = back + left.astype(F32)
        right = lax.ppermute(
            onward.astype(BF16), "head", [(i, i + 1) for i in range(min(turn + 1, count - 1))]
        )
        left = lax.ppermute(
            back.astype(BF16), "head", [(count - 1 - i, count - 2 - i) for i in range(min(turn + 1, count - 1))]
        )
    total = blocks[0]
    if count > 1:
        total = total + right.astype(F32) + left.astype(F32)
    return total.astype(BF16)


def on_device(tokens, qkv_weight, beta_logit, log_decay, out_grad):
    heads = beta_logit.shape[0]
    count = lax.axis_size("seq")
    paired = heads % 2 == 0 and count > 2 and count & (count - 1) == 0 and count <= 8
    half = heads // 2 if paired else 0
    proj, u, wk, dbt, ktt, keep, send = prepare(
        tokens, qkv_weight, beta_logit, log_decay, out_grad, half
    )
    if paired:
        own, recv = edges_by_pairs(keep, send, count)
    else:
        own, recv = edges_by_gather(keep, count)
    blocks = finish(
        qkv_weight, proj, u, wk, dbt, ktt, beta_logit, log_decay, out_grad, own, recv, half
    )
    return sum_over_heads(blocks)


def solution(mesh):
    return jax.shard_map(
        on_device,
        mesh=mesh,
        in_specs=(
            P("seq", None),
            P(None, None, "head"),
            P("head", "seq"),
            P("head", "seq"),
            P("seq", "head"),
        ),
        out_specs=P("seq", "head"),
        check_vma=False,
    )
```

```python
import functools

import jax
import jax.numpy as jnp
from jax import lax
from jax.experimental import pallas as pl
from jax.experimental.pallas import tpu as pltpu
from jax.sharding import PartitionSpec as P

F32 = jnp.float32
BF16 = jnp.bfloat16
HIGH = lax.Precision.HIGHEST
FAR = -1e30


def nn(a, b):
    return lax.dot_general(a, b, (((1,), (0,)), ((), ())), preferred_element_type=F32)


def nt(a, b):
    return lax.dot_general(a, b, (((1,), (1,)), ((), ())), preferred_element_type=F32)


def fine(a, b, dims=(1, 0)):
    return lax.dot_general(
        a, b, (((dims[0],), (dims[1],)), ((), ())), precision=HIGH, preferred_element_type=F32
    )


def grid_ids(size):
    rows = lax.broadcasted_iota(jnp.int32, (size, size), 0)
    cols = lax.broadcasted_iota(jnp.int32, (size, size), 1)
    return rows, cols


def exact_terms(value):
    high = value.astype(BF16)
    left = value - high.astype(F32)
    mid = left.astype(BF16)
    return high, mid, (left - mid.astype(F32)).astype(BF16)


def gates(logit, decay):
    heads, size = decay.shape
    rows, cols = grid_ids(size)
    upper = jnp.where(rows <= cols, 1.0, 0.0).astype(BF16)
    high, mid, low = exact_terms(decay)
    run = nn(high, upper) + nn(mid, upper) + nn(low, upper)
    lanes = [run, 1.0 / (1.0 + jnp.exp(-logit))]
    spare = -2 * heads % 8
    if spare:
        lanes.append(jnp.zeros((spare, size), F32))
    lanes = jnp.concatenate(lanes, axis=0)
    return lanes, lanes.T


def unit_rows(tensor):
    scale = lax.rsqrt(jnp.sum(tensor * tensor, axis=-1, keepdims=True) + 1e-06)
    return tensor * scale, scale


def unit_lower_inverse(couplings):
    size = couplings[0].shape[0]
    base = size // 4
    lane_block = lax.broadcasted_iota(jnp.int32, (base, size), 1) // base
    on = [lane_block == b for b in range(4)]
    odd = lane_block % 2 == 1
    masks = [jnp.where(o, 1.0, 0.0).astype(BF16) for o in on]
    none = jnp.zeros((base, size), BF16)

    def strip(a, b):
        return a[b * base : (b + 1) * base]

    def spread(x):
        return jnp.concatenate([x * m for m in masks], axis=0)

    flat = [sum(jnp.where(on[b], strip(a, b), 0.0) for b in range(4)) for a in couplings]
    rest = [-x for x in flat]
    power = flat
    reach = 1
    while 2 * reach < base:
        narrow = [p.astype(BF16) for p in power]
        if reach == 1:
            power = [nn(p, spread(p)) for p in narrow]
        else:
            both = [
                nn(jnp.concatenate([n.astype(BF16), p], axis=0), spread(p))
                for n, p in zip(rest, narrow)
            ]
            rest = [n + p + x[:base] for n, p, x in zip(rest, power, both)]
            power = [x[base:] for x in both]
        reach *= 2
    if reach > 1:
        narrow = [p.astype(BF16) for p in power]
        rest = [n + p + nn(n.astype(BF16), spread(b)) for n, p, b in zip(rest, power, narrow)]

    outer = [jnp.where(on[0], strip(a, 1), 0.0) + jnp.where(on[2], strip(a, 3), 0.0) for a in couplings]
    wide = [n.astype(BF16) for n in rest]
    half = [g + nn(g.astype(BF16), spread(n)) for g, n in zip(outer, wide)]
    half_b = [y.astype(BF16) for y in half]
    late = [jnp.where(odd, n, 0.0) for n in rest]
    cross = [
        y + nn(l.astype(BF16), jnp.concatenate([none, b * masks[0], none, b * masks[2]], axis=0))
        for y, l, b in zip(half, late, half_b)
    ]
    below = [l - z for l, z in zip(late, cross)]
    above = [jnp.where(odd, 0.0, n) for n in rest]
    mid = size // 2
    early = [jnp.concatenate([t[:, :mid], b[:, :mid]], axis=0).astype(BF16) for t, b in zip(above, below)]
    later = [jnp.concatenate([t[:, mid:], b[:, mid:]], axis=0).astype(BF16) for t, b in zip(above, below)]
    corner = [a[mid:, :mid] for a in couplings]
    half = [c + nn(c.astype(BF16), e) for c, e in zip(corner, early)]
    cross = [y + nn(l, y.astype(BF16)) for y, l in zip(half, later)]
    blank = jnp.zeros((mid, mid), BF16)
    return [
        jnp.concatenate(
            [
                jnp.concatenate([e, blank], axis=1),
                jnp.concatenate([(-z).astype(BF16), l], axis=1),
            ],
            axis=0,
        )
        for e, z, l in zip(early, cross, later)
    ]


def prepare_kernel(
    half, pieces, tok_hbm, w_hbm, logit_ref, decay_ref, og_ref,
    unit_ref, scale_ref, lane_ref, col_ref, u_ref, wk_ref, dbt_ref, ktt_ref, gt_ref, keep_ref, send_ref,
    tok_scr, w_scr, value_scr, pay_scr, tok_sem, w_sem,
):
    heads, size = decay_ref.shape
    members, depth, columns = w_scr.shape
    width = columns // heads
    chunk = depth // pieces
    members_in_turn = (1, 2, 0)

    def part(i):
        return pl.ds(i * chunk, chunk)

    tok_copies = [
        pltpu.make_async_copy(tok_hbm.at[:, part(i)], tok_scr.at[:, part(i)], tok_sem.at[i])
        for i in range(pieces)
    ]
    w_copies = [
        [
            pltpu.make_async_copy(w_hbm.at[p, part(i)], w_scr.at[p, part(i)], w_sem.at[p, i])
            for i in range(pieces)
        ]
        for p in range(members)
    ]
    for turn, p in enumerate(members_in_turn):
        for i in range(pieces):
            if turn == 0:
                tok_copies[i].start()
            w_copies[p][i].start()

    lanes, cols_of = gates(logit_ref[...], decay_ref[...])
    lane_ref[...] = lanes
    col_ref[...] = cols_of
    every = range(heads)
    spans = [slice(h * width, (h + 1) * width) for h in every]
    for h in every:
        gt_ref[h] = og_ref[:, spans[h]].astype(F32).T.astype(BF16)

    for turn, p in enumerate(members_in_turn):
        total = None
        for i in range(pieces):
            if turn == 0:
                tok_copies[i].wait()
            w_copies[p][i].wait()
            here = slice(i * chunk, (i + 1) * chunk)
            result = nn(tok_scr[:, here], w_scr[p, here])
            total = result if total is None else total + result
        if p == 2:
            value_scr[...] = total
        else:
            for h in every:
                unit, scale = unit_rows(total[:, spans[h]])
                unit_ref[p, :, spans[h]] = unit
                scale_ref[:, p * heads + h : p * heads + h + 1] = scale

    rows, cols = grid_ids(size)
    causal = rows >= cols
    strict = rows > cols
    run_col = [cols_of[:, h : h + 1] for h in every]
    run_row = [lanes[h : h + 1, :] for h in every]
    beta = [cols_of[:, heads + h : heads + h + 1] for h in every]
    keys = [unit_ref[1, :, s] for s in spans]
    key_b = [k.astype(BF16) for k in keys]
    gamma = [jnp.exp(jnp.where(causal, run_col[h] - run_row[h], FAR)) for h in every]
    couplings = [
        jnp.where(strict, beta[h] * gamma[h] * nt(key_b[h], key_b[h]), 0.0) for h in every
    ]
    queries = [unit_ref[0, :, s] for s in spans]
    scores = [(gamma[h] * nt(queries[h].astype(BF16), key_b[h])).astype(BF16) for h in every]
    inverse = unit_lower_inverse(couplings)
    last = [run_col[h][size - 1 : size, :] for h in every]
    open_col = [jnp.exp(run_col[h]) for h in every]
    fade_row = [jnp.exp(last[h] - run_row[h]) for h in every]
    write_key = [beta[h] * open_col[h] * keys[h] for h in every]
    right = [
        jnp.concatenate([beta[h] * value_scr[:, spans[h]], write_key[h]], axis=1) for h in every
    ]
    solved = [right[h] + nn(inverse[h], right[h].astype(BF16)) for h in every]
    fade_t = [keys[h].T * fade_row[h] for h in every]
    left = [jnp.concatenate([nn(gt_ref[h], scores[h]), fade_t[h]], axis=0) for h in every]
    back = [left[h] + nn(left[h].astype(BF16), inverse[h]) for h in every]
    e_rows, e_cols = grid_ids(width)
    for h in every:
        fade_hi = fade_t[h].astype(BF16)
        fade_lo = (fade_t[h] - fade_hi.astype(F32)).astype(BF16)
        solved_hi = solved[h].astype(BF16)
        solved_lo = (solved[h][:, :width] - solved_hi[:, :width].astype(F32)).astype(BF16)
        state = nn(fade_hi, solved_hi)
        fill = state[:, :width] + nn(fade_lo, solved_hi[:, :width]) + nn(fade_hi, solved_lo)
        unit = jnp.where(e_rows == e_cols, jnp.exp(last[h]), 0.0)
        seed = nn(gt_ref[h], (open_col[h] * queries[h]).astype(BF16)) - nn(
            back[h][:width].astype(BF16), write_key[h].astype(BF16)
        )
        pay_scr[h, 0] = (unit - state[:, width:]).astype(BF16)
        pay_scr[h, 1] = fill.astype(BF16)
        pay_scr[h, 2] = seed.astype(BF16)
        u_ref[h] = solved[h][:, :width]
        wk_ref[h] = solved_hi[:, width:]
        dbt_ref[h] = back[h][:width]
        ktt_ref[h] = back[h][width:].astype(BF16)
    if half:
        core = lax.rem(lax.axis_index("seq"), 2)
        keep_ref[...] = pay_scr[pl.ds(core * half, half)]
        send_ref[...] = pay_scr[pl.ds((1 - core) * half, half)]
    else:
        keep_ref[...] = pay_scr[...]
        send_ref[...] = pay_scr[...]


def here():
    return pl.BlockSpec(memory_space=pltpu.VMEM)


def away():
    return pl.BlockSpec(memory_space=pl.ANY)


def limit(mebibytes):
    return pltpu.CompilerParams(vmem_limit_bytes=mebibytes * 2**20)


def prepare(tokens, weights, logit, decay, out_grad, half):
    heads, size = logit.shape
    members, depth, columns = weights.shape
    width = columns // heads
    part = half or heads
    pieces = 4 if depth % 512 == 0 else 1
    gate_rows = 2 * heads + -2 * heads % 8
    shapes = [
        ((2, size, columns), F32),
        ((size, 2 * heads), F32),
        ((gate_rows, size), F32),
        ((size, gate_rows), F32),
        ((heads, size, width), F32),
        ((heads, size, width), BF16),
        ((heads, width, size), F32),
        ((heads, width, size), BF16),
        ((heads, width, size), BF16),
        ((part, 3, width, width), BF16),
        ((part, 3, width, width), BF16),
    ]
    return pl.pallas_call(
        functools.partial(prepare_kernel, half, pieces),
        in_specs=[away(), away(), here(), here(), here()],
        out_specs=[here()] * len(shapes),
        out_shape=[jax.ShapeDtypeStruct(*s) for s in shapes],
        scratch_shapes=[
            pltpu.VMEM((size, depth), BF16),
            pltpu.VMEM((members, depth, columns), BF16),
            pltpu.VMEM((size, columns), F32),
            pltpu.VMEM((heads, 3, width, width), BF16),
            pltpu.SemaphoreType.DMA((pieces,)),
            pltpu.SemaphoreType.DMA((members, pieces)),
        ],
        compiler_params=limit(36),
        name="prepare",
    )(tokens, weights, logit, decay, out_grad)


def weigh_kernel(heads, lane_ref, col_ref, gamma_ref, turned_ref, strong_ref, strong_t_ref):
    size = lane_ref.shape[1]
    rows, cols = grid_ids(size)
    for h in range(heads):
        gap = col_ref[:, h : h + 1] - lane_ref[h : h + 1, :]
        gamma = jnp.exp(jnp.where(rows >= cols, gap, FAR))
        turned = jnp.exp(jnp.where(rows <= cols, -gap, FAR))
        gamma_ref[h] = gamma
        turned_ref[h] = turned
        beta = col_ref[:, heads + h : heads + h + 1]
        beta_row = lane_ref[heads + h : heads + h + 1, :]
        strong_ref[h] = jnp.where(rows > cols, beta * gamma, 0.0)
        strong_t_ref[h] = jnp.where(rows < cols, beta_row * turned, 0.0)


def weigh(lanes, cols, heads):
    size = lanes.shape[1]
    shape = jax.ShapeDtypeStruct((heads, size, size), F32)
    return pl.pallas_call(
        functools.partial(weigh_kernel, heads),
        in_specs=[here()] * 2,
        out_specs=[here()] * 4,
        out_shape=[shape] * 4,
        compiler_params=limit(8),
        name="weigh",
    )(lanes, cols)


def pair_kernel(levels, keep_ref, recv_ref, *pay_refs):
    place = lax.axis_index("seq")
    first = lax.rem(place, 2) == 0
    chip = place // 2

    def join(early, late):
        width = early.shape[-1]
        for h in range(keep_ref.shape[0]):
            ahead = nn(late[h, 0], jnp.concatenate([early[h, 1], early[h, 0]], axis=1))
            up = ahead[:, :width] + late[h, 1].astype(F32)
            down = nn(late[h, 2], early[h, 0]) + early[h, 2].astype(F32)
            joint = ahead[:, width:].astype(BF16)
            for level in range(levels):
                upward = lax.rem(chip // (1 << level), 2) == 0
                pay_refs[level][h, 0] = joint
                pay_refs[level][h, 1] = jnp.where(upward, up, down).astype(BF16)

    @pl.when(first)
    def _():
        join(keep_ref, recv_ref)

    @pl.when(jnp.logical_not(first))
    def _():
        join(recv_ref, keep_ref)


def join_pair(keep, recv, levels):
    half, _, width, _ = keep.shape
    shape = jax.ShapeDtypeStruct((half, 2, width, width), BF16)
    return pl.pallas_call(
        functools.partial(pair_kernel, levels),
        in_specs=[here()] * 2,
        out_specs=[here()] * levels,
        out_shape=[shape] * levels,
        compiler_params=limit(8),
        name="join_pair",
    )(keep, recv)


def two_terms(value):
    high = value.astype(BF16)
    return high, (value - high.astype(F32)).astype(BF16)


def scan_kernel(keep_ref, recv_ref, near_ref, far_ref, cross_ref, own_ref, send_ref, enter, leave):
    place = lax.axis_index("seq")
    first = lax.rem(place, 2) == 0
    chip = place // 2
    low = lax.rem(chip, 2) == 1
    high = chip // 2 == 1
    every = range(keep_ref.shape[0])

    def pairs(one, two):
        for h in every:

            @pl.when(high)
            def _():
                enter[h] = nn(two[h, 0], one[h, 1]) + two[h, 1].astype(F32)
                leave[h] = jnp.zeros_like(leave[h])

            @pl.when(jnp.logical_not(high))
            def _():
                leave[h] = nn(two[h, 1], one[h, 0]) + one[h, 1].astype(F32)
                enter[h] = jnp.zeros_like(enter[h])

    @pl.when(low)
    def _():
        pairs(cross_ref, far_ref)
        for h in every:
            top, rest = two_terms(enter[h])
            enter[h] = nn(near_ref[h, 0], top) + nn(near_ref[h, 0], rest) + near_ref[h, 1].astype(F32)

    @pl.when(jnp.logical_not(low))
    def _():
        pairs(far_ref, cross_ref)
        for h in every:
            top, rest = two_terms(leave[h])
            leave[h] = nn(top, near_ref[h, 0]) + nn(rest, near_ref[h, 0]) + near_ref[h, 1].astype(F32)

    def within(early, late, early_out, late_out):
        for h in every:
            top, rest = two_terms(enter[h])
            back, tail = two_terms(leave[h])
            middle = nn(early[h, 0], top) + nn(early[h, 0], rest) + early[h, 1].astype(F32)
            inner = nn(back, late[h, 0]) + nn(tail, late[h, 0]) + late[h, 2].astype(F32)
            early_out[h, 0] = top
            early_out[h, 1] = inner.astype(BF16)
            late_out[h, 0] = middle.astype(BF16)
            late_out[h, 1] = back

    @pl.when(first)
    def _():
        within(keep_ref, recv_ref, own_ref, send_ref)

    @pl.when(jnp.logical_not(first))
    def _():
        within(recv_ref, keep_ref, send_ref, own_ref)


def scan_chips(keep, recv, near, far, cross):
    half, _, width, _ = keep.shape
    shape = jax.ShapeDtypeStruct((half, 2, width, width), BF16)
    return pl.pallas_call(
        scan_kernel,
        in_specs=[here()] * 5,
        out_specs=[here()] * 2,
        out_shape=[shape] * 2,
        scratch_shapes=[pltpu.VMEM((half, width, width), F32)] * 2,
        compiler_params=limit(8),
        name="scan_chips",
    )(keep, recv, near, far, cross)


def part_at(slot, count):
    place = lax.axis_index("head")
    if count != 4:
        return lax.rem(place + slot + 1, count)
    if slot == 0:
        return 3 - place
    if slot == 3:
        return place
    low, high = ((2, 0), (3, 1)) if slot == 1 else ((1, 3), (0, 2))
    ends = jnp.where(place == 0, low[0], low[1])
    return jnp.where(place < 2, ends, jnp.where(place == 2, high[0], high[1]))


def fetch(w_hbm, w_scr, sem, slot, count):
    step = w_hbm.shape[1] // count
    start = pl.multiple_of(part_at(slot, count) * step, step)
    return pltpu.make_async_copy(w_hbm.at[:, pl.ds(start, step)], w_scr, sem)


def grads_kernel(
    half, count, w_hbm, unit_ref, scale_ref, col_ref, u_ref, wk_ref, dbt_ref, ktt_ref, gt_ref, og_ref,
    gamma_ref, turned_ref, strong_ref, strong_t_ref, own_ref, recv_ref,
    grad_ref, out_ref, w_scr, edge_scr, sem,
):
    heads, size, width = u_ref.shape
    copy = fetch(w_hbm, w_scr, sem, 0, count)
    copy.start()
    if half:
        core = lax.rem(lax.axis_index("seq"), 2)
        edge_scr[pl.ds(core * half, half)] = own_ref[...]
        edge_scr[pl.ds((1 - core) * half, half)] = recv_ref[...]
    else:
        edge_scr[...] = own_ref[...]
    every = range(heads)
    spans = [slice(h * width, (h + 1) * width) for h in every]
    run_col = [col_ref[:, h : h + 1] for h in every]
    beta = [col_ref[:, heads + h : heads + h + 1] for h in every]
    open_col = [jnp.exp(run_col[h]) for h in every]
    fade_col = [jnp.exp(run_col[h][size - 1 : size, :] - run_col[h]) for h in every]
    update = [(u_ref[h] - nn(wk_ref[h], edge_scr[h, 0])).astype(BF16) for h in every]
    delta_t = [dbt_ref[h] + nn(edge_scr[h, 1], ktt_ref[h]) for h in every]
    delta = [d.T for d in delta_t]
    for h in every:
        span = spans[h]
        rows = jnp.concatenate([og_ref[:, span], delta[h].astype(BF16)], axis=0)
        lanes = nt(rows, update[h])
        turned = nn(update[h], jnp.concatenate([gt_ref[h], delta_t[h].astype(BF16)], axis=1))
        attend = (gamma_ref[h] * lanes[:size]).astype(BF16)
        attend_t = (turned_ref[h] * turned[:, :size]).astype(BF16)
        mix = (strong_ref[h] * lanes[size:] + strong_t_ref[h] * turned[:, size:]).astype(BF16)
        edge = nt(rows, edge_scr[h, 0])
        query = unit_ref[0, :, span]
        key = unit_ref[1, :, span]
        key_b = key.astype(BF16)
        dq = open_col[h] * edge[:size] + nn(attend, key_b)
        dk = (
            nn(attend_t, query.astype(BF16))
            - nn(mix, key_b)
            + fade_col[h] * nn(update[h], edge_scr[h, 1])
            - beta[h] * open_col[h] * edge[size:]
        )
        for slot, unit, slope in ((0, query, dq), (1, key, dk)):
            scale = scale_ref[:, slot * heads + h : slot * heads + h + 1]
            along = jnp.sum(unit * slope, axis=-1, keepdims=True)
            grad_ref[slot, :, span] = (scale * (slope - unit * along)).astype(BF16)
        grad_ref[2, :, span] = (beta[h] * delta[h]).astype(BF16)
    copy.wait()
    out_ref[...] = spread_grads(grad_ref, w_scr).astype(out_ref.dtype)


def spread_grads(grad_ref, w_ref):
    total = nt(grad_ref[0], w_ref[0])
    for member in range(1, grad_ref.shape[0]):
        total = total + nt(grad_ref[member], w_ref[member])
    return total


def grads(weights, prepared, out_grad, weighed, own, recv, half):
    unit, scale, col, u, wk, dbt, ktt, gt = prepared
    heads, size, width = u.shape
    members, depth, columns = weights.shape
    count = lax.axis_size("head")
    step = depth // count
    return pl.pallas_call(
        functools.partial(grads_kernel, half, count),
        in_specs=[away()] + [here()] * 15,
        out_specs=[here()] * 2,
        out_shape=[
            jax.ShapeDtypeStruct((members, size, columns), BF16),
            jax.ShapeDtypeStruct((size, step), BF16),
        ],
        scratch_shapes=[
            pltpu.VMEM((members, step, columns), BF16),
            pltpu.VMEM((heads, 2, width, width), BF16),
            pltpu.SemaphoreType.DMA(()),
        ],
        compiler_params=limit(24),
        name="grads",
    )(weights, unit, scale, col, u, wk, dbt, ktt, gt, out_grad, *weighed, own, recv)


def others_kernel(count, w_hbm, grad_ref, *refs):
    outs, (w_scr, sem) = refs[: count - 1], refs[count - 1 :]
    copies = [fetch(w_hbm, w_scr.at[i], sem.at[i], i + 1, count) for i in range(count - 1)]
    for copy in copies:
        copy.start()
    for i, copy in enumerate(copies):
        copy.wait()
        outs[i][...] = spread_grads(grad_ref, w_scr.at[i]).astype(outs[i].dtype)


def others(weights, grad):
    members, depth, columns = weights.shape
    size = grad.shape[1]
    count = lax.axis_size("head")
    step = depth // count
    kinds = [BF16] + [F32] * 2 if count == 4 else [BF16] * (count - 2) + [F32]
    return pl.pallas_call(
        functools.partial(others_kernel, count),
        in_specs=[away(), here()],
        out_specs=[here()] * (count - 1),
        out_shape=[jax.ShapeDtypeStruct((size, step), k) for k in kinds],
        scratch_shapes=[
            pltpu.VMEM((count - 1, members, step, columns), BF16),
            pltpu.SemaphoreType.DMA((count - 1,)),
        ],
        compiler_params=limit(24),
        name="others",
    )(weights, grad)


def swap(value, axis, count, mask):
    return lax.ppermute(value, axis, [(i, i ^ mask) for i in range(count)])


def edges_by_pairs(keep, send, count):
    recv = swap(send, "seq", count, 1)
    low, high = join_pair(keep, recv, 2)
    near = swap(low, "seq", count, 2)
    far = swap(high, "seq", count, 4)
    cross = swap(high, "seq", count, 6)
    own, other = scan_chips(keep, recv, near, far, cross)
    return own, swap(other, "seq", count, 1)


def edges_by_gather(keep, count):
    place = lax.axis_index("seq")
    gathered = lax.all_gather(keep, "seq")
    product = functools.partial(jnp.einsum, "hij,hjk->hik", precision=HIGH)

    def take(j):
        return lax.dynamic_index_in_dim(gathered, j, 0, False).astype(F32)

    def forward(j, state):
        part = take(j)
        return product(part[:, 0], state) + part[:, 1]

    def backward(i, state):
        part = take(count - 1 - i)
        return product(state, part[:, 0]) + part[:, 2]

    vacant = jnp.zeros(keep.shape[:1] + keep.shape[2:], F32)
    enter = lax.fori_loop(0, place, forward, vacant)
    leave = lax.fori_loop(0, count - 1 - place, backward, vacant)
    own = jnp.stack([enter, leave], axis=1).astype(BF16)
    return own, own


def sum_on_line(blocks):
    count = lax.axis_size("head")
    right = left = None
    for turn in range(count - 1):
        onward = blocks[count - 1 - turn]
        back = blocks[turn + 1]
        if turn:
            onward = (onward.astype(F32) + right.astype(F32)).astype(BF16)
            back = (back.astype(F32) + left.astype(F32)).astype(BF16)
        right = lax.ppermute(onward, "head", [(i, i + 1) for i in range(turn + 1)])
        left = lax.ppermute(back, "head", [(count - 1 - i, count - 2 - i) for i in range(turn + 1)])
    total = blocks[0]
    if count > 1:
        total = total + right.astype(F32) + left.astype(F32)
    return total.astype(BF16)


def sum_of_four(end, first, joint, own):
    outer = lax.ppermute(end, "head", [(0, 1), (3, 2)])
    inner = lax.ppermute(end, "head", [(1, 2), (2, 1)])
    ring = lax.ppermute(first, "head", [(0, 2), (2, 3), (3, 1), (1, 0)])
    joint = (joint + outer.astype(F32)).astype(BF16)
    joint = lax.ppermute(joint, "head", [(0, 1), (1, 3), (3, 2), (2, 0)])
    total = own + inner.astype(F32) + ring.astype(F32) + joint.astype(F32)
    return total.astype(BF16)


def on_device(tokens, qkv_weight, beta_logit, log_decay, out_grad):
    heads = beta_logit.shape[0]
    count = lax.axis_size("seq")
    paired = heads % 2 == 0 and count == 8
    half = heads // 2 if paired else 0
    unit, scale, lanes, col, u, wk, dbt, ktt, gt, keep, send = prepare(
        tokens, qkv_weight, beta_logit, log_decay, out_grad, half
    )
    if paired:
        own, recv = edges_by_pairs(keep, send, count)
    else:
        own, recv = edges_by_gather(keep, count)
    weighed = weigh(lanes, col, heads)
    prepared = (unit, scale, col, u, wk, dbt, ktt, gt)
    grad, end = grads(qkv_weight, prepared, out_grad, weighed, own, recv, half)
    rest = others(qkv_weight, grad)
    if lax.axis_size("head") == 4:
        return sum_of_four(end, *rest)
    return sum_on_line([rest[-1], end, *rest[:-1]])


def solution(mesh):
    return jax.shard_map(
        on_device,
        mesh=mesh,
        in_specs=(
            P("seq", None),
            P(None, None, "head"),
            P("head", "seq"),
            P("head", "seq"),
            P("seq", "head"),
        ),
        out_specs=P("seq", "head"),
        check_vma=False,
    )
```

```python
import functools

import jax
import jax.numpy as jnp
from jax import lax
from jax.experimental import pallas as pl
from jax.experimental.pallas import tpu as pltpu
from jax.sharding import PartitionSpec as P

F32 = jnp.float32
BF16 = jnp.bfloat16
HIGH = lax.Precision.HIGHEST
FAR = -1e30


def nn(a, b):
    return lax.dot_general(a, b, (((1,), (0,)), ((), ())), preferred_element_type=F32)


def nt(a, b):
    return lax.dot_general(a, b, (((1,), (1,)), ((), ())), preferred_element_type=F32)


def fine(a, b, dims=(1, 0)):
    return lax.dot_general(
        a, b, (((dims[0],), (dims[1],)), ((), ())), precision=HIGH, preferred_element_type=F32
    )


def grid_ids(size):
    rows = lax.broadcasted_iota(jnp.int32, (size, size), 0)
    cols = lax.broadcasted_iota(jnp.int32, (size, size), 1)
    return rows, cols


def exact_terms(value):
    high = value.astype(BF16)
    left = value - high.astype(F32)
    mid = left.astype(BF16)
    return high, mid, (left - mid.astype(F32)).astype(BF16)


def gates(logit, decay):
    heads, size = decay.shape
    rows, cols = grid_ids(size)
    upper = jnp.where(rows <= cols, 1.0, 0.0).astype(BF16)
    high, mid, low = exact_terms(decay)
    run = nn(high, upper) + nn(mid, upper) + nn(low, upper)
    lanes = [run, 1.0 / (1.0 + jnp.exp(-logit))]
    spare = -2 * heads % 8
    if spare:
        lanes.append(jnp.zeros((spare, size), F32))
    lanes = jnp.concatenate(lanes, axis=0)
    return lanes, lanes.T


def unit_rows(tensor):
    scale = lax.rsqrt(jnp.sum(tensor * tensor, axis=-1, keepdims=True) + 1e-06)
    return tensor * scale, scale


def unit_lower_inverse(couplings):
    size = couplings[0].shape[0]
    base = size // 4
    lane_block = lax.broadcasted_iota(jnp.int32, (base, size), 1) // base
    on = [lane_block == b for b in range(4)]
    odd = lane_block % 2 == 1
    masks = [jnp.where(o, 1.0, 0.0).astype(BF16) for o in on]
    none = jnp.zeros((base, size), BF16)

    def strip(a, b):
        return a[b * base : (b + 1) * base]

    def spread(x):
        return jnp.concatenate([x * m for m in masks], axis=0)

    flat = [sum(jnp.where(on[b], strip(a, b), 0.0) for b in range(4)) for a in couplings]
    rest = [-x for x in flat]
    power = flat
    reach = 1
    while 2 * reach < base:
        narrow = [p.astype(BF16) for p in power]
        if reach == 1:
            power = [nn(p, spread(p)) for p in narrow]
        else:
            both = [
                nn(jnp.concatenate([n.astype(BF16), p], axis=0), spread(p))
                for n, p in zip(rest, narrow)
            ]
            rest = [n + p + x[:base] for n, p, x in zip(rest, power, both)]
            power = [x[base:] for x in both]
        reach *= 2
    if reach > 1:
        narrow = [p.astype(BF16) for p in power]
        rest = [n + p + nn(n.astype(BF16), spread(b)) for n, p, b in zip(rest, power, narrow)]

    outer = [jnp.where(on[0], strip(a, 1), 0.0) + jnp.where(on[2], strip(a, 3), 0.0) for a in couplings]
    wide = [n.astype(BF16) for n in rest]
    half = [g + nn(g.astype(BF16), spread(n)) for g, n in zip(outer, wide)]
    half_b = [y.astype(BF16) for y in half]
    late = [jnp.where(odd, n, 0.0) for n in rest]
    cross = [
        y + nn(l.astype(BF16), jnp.concatenate([none, b * masks[0], none, b * masks[2]], axis=0))
        for y, l, b in zip(half, late, half_b)
    ]
    below = [l - z for l, z in zip(late, cross)]
    above = [jnp.where(odd, 0.0, n) for n in rest]
    mid = size // 2
    early = [jnp.concatenate([t[:, :mid], b[:, :mid]], axis=0).astype(BF16) for t, b in zip(above, below)]
    later = [jnp.concatenate([t[:, mid:], b[:, mid:]], axis=0).astype(BF16) for t, b in zip(above, below)]
    corner = [a[mid:, :mid] for a in couplings]
    half = [c + nn(c.astype(BF16), e) for c, e in zip(corner, early)]
    cross = [y + nn(l, y.astype(BF16)) for y, l in zip(half, later)]
    blank = jnp.zeros((mid, mid), BF16)
    return [
        jnp.concatenate(
            [
                jnp.concatenate([e, blank], axis=1),
                jnp.concatenate([(-z).astype(BF16), l], axis=1),
            ],
            axis=0,
        )
        for e, z, l in zip(early, cross, later)
    ]


def prepare_kernel(
    half, pieces, tok_hbm, w_hbm, logit_hbm, decay_hbm, og_hbm,
    w_ref, og_ref, unit_ref, scale_ref, lane_ref, col_ref, u_ref, wk_ref, dbt_ref, ktt_ref, gt_ref,
    keep_ref, send_ref,
    tok_scr, logit_ref, decay_ref, value_scr, pay_scr, tok_sem, w_sem, more_sem,
):
    heads, size = decay_ref.shape
    members, depth, columns = w_ref.shape
    width = columns // heads
    chunk = depth // pieces
    members_in_turn = (1, 2, 0)

    def part(i):
        return pl.ds(i * chunk, chunk)

    tok_copies = [
        pltpu.make_async_copy(tok_hbm.at[:, part(i)], tok_scr.at[:, part(i)], tok_sem.at[i])
        for i in range(pieces)
    ]
    w_copies = [
        [
            pltpu.make_async_copy(w_hbm.at[p, part(i)], w_ref.at[p, part(i)], w_sem.at[p, i])
            for i in range(pieces)
        ]
        for p in range(members)
    ]
    small = [(logit_hbm, logit_ref), (decay_hbm, decay_ref), (og_hbm, og_ref)]
    small = [pltpu.make_async_copy(a, b, more_sem.at[i]) for i, (a, b) in enumerate(small)]
    for copy in small[:2]:
        copy.start()
    for turn, p in enumerate(members_in_turn):
        for i in range(pieces):
            if turn == 0:
                tok_copies[i].start()
            w_copies[p][i].start()
            if turn == 0 and i == 0:
                small[2].start()
    for copy in small[:2]:
        copy.wait()

    lanes, cols_of = gates(logit_ref[...], decay_ref[...])
    lane_ref[...] = lanes
    col_ref[...] = cols_of
    every = range(heads)
    spans = [slice(h * width, (h + 1) * width) for h in every]
    for turn, p in enumerate(members_in_turn):
        total = None
        for i in range(pieces):
            if turn == 0:
                tok_copies[i].wait()
            w_copies[p][i].wait()
            here = slice(i * chunk, (i + 1) * chunk)
            result = nn(tok_scr[:, here], w_ref[p, here])
            total = result if total is None else total + result
        if p == 2:
            value_scr[...] = total
        else:
            for h in every:
                unit, scale = unit_rows(total[:, spans[h]])
                unit_ref[p, :, spans[h]] = unit
                scale_ref[:, p * heads + h : p * heads + h + 1] = scale

    small[2].wait()
    for h in every:
        gt_ref[h] = og_ref[:, spans[h]].astype(F32).T.astype(BF16)
    rows, cols = grid_ids(size)
    causal = rows >= cols
    strict = rows > cols
    run_col = [cols_of[:, h : h + 1] for h in every]
    run_row = [lanes[h : h + 1, :] for h in every]
    beta = [cols_of[:, heads + h : heads + h + 1] for h in every]
    keys = [unit_ref[1, :, s] for s in spans]
    key_b = [k.astype(BF16) for k in keys]
    gamma = [jnp.exp(jnp.where(causal, run_col[h] - run_row[h], FAR)) for h in every]
    couplings = [
        jnp.where(strict, beta[h] * gamma[h] * nt(key_b[h], key_b[h]), 0.0) for h in every
    ]
    queries = [unit_ref[0, :, s] for s in spans]
    scores = [(gamma[h] * nt(queries[h].astype(BF16), key_b[h])).astype(BF16) for h in every]
    inverse = unit_lower_inverse(couplings)
    last = [run_col[h][size - 1 : size, :] for h in every]
    open_col = [jnp.exp(run_col[h]) for h in every]
    fade_row = [jnp.exp(last[h] - run_row[h]) for h in every]
    write_key = [beta[h] * open_col[h] * keys[h] for h in every]
    right = [
        jnp.concatenate([beta[h] * value_scr[:, spans[h]], write_key[h]], axis=1) for h in every
    ]
    solved = [right[h] + nn(inverse[h], right[h].astype(BF16)) for h in every]
    fade_t = [keys[h].T * fade_row[h] for h in every]
    left = [jnp.concatenate([nn(gt_ref[h], scores[h]), fade_t[h]], axis=0) for h in every]
    back = [left[h] + nn(left[h].astype(BF16), inverse[h]) for h in every]
    e_rows, e_cols = grid_ids(width)
    for h in every:
        fade_hi = fade_t[h].astype(BF16)
        fade_lo = (fade_t[h] - fade_hi.astype(F32)).astype(BF16)
        solved_hi = solved[h].astype(BF16)
        solved_lo = (solved[h][:, :width] - solved_hi[:, :width].astype(F32)).astype(BF16)
        state = nn(fade_hi, solved_hi)
        fill = state[:, :width] + nn(fade_lo, solved_hi[:, :width]) + nn(fade_hi, solved_lo)
        unit = jnp.where(e_rows == e_cols, jnp.exp(last[h]), 0.0)
        seed = nn(gt_ref[h], (open_col[h] * queries[h]).astype(BF16)) - nn(
            back[h][:width].astype(BF16), write_key[h].astype(BF16)
        )
        pay_scr[h, 0] = (unit - state[:, width:]).astype(BF16)
        pay_scr[h, 1] = fill.astype(BF16)
        pay_scr[h, 2] = seed.astype(BF16)
        u_ref[h] = solved[h][:, :width]
        wk_ref[h] = solved_hi[:, width:]
        dbt_ref[h] = back[h][:width]
        ktt_ref[h] = back[h][width:].astype(BF16)
    if half:
        core = lax.rem(lax.axis_index("seq"), 2)
        keep_ref[...] = pay_scr[pl.ds(core * half, half)]
        send_ref[...] = pay_scr[pl.ds((1 - core) * half, half)]
    else:
        keep_ref[...] = pay_scr[...]
        send_ref[...] = pay_scr[...]


def here():
    return pl.BlockSpec(memory_space=pltpu.VMEM)


def away():
    return pl.BlockSpec(memory_space=pltpu.HBM)


def limit(mebibytes):
    return pltpu.CompilerParams(vmem_limit_bytes=mebibytes * 2**20)


def prepare(tokens, weights, logit, decay, out_grad, half):
    heads, size = logit.shape
    members, depth, columns = weights.shape
    width = columns // heads
    part = half or heads
    pieces = 4 if depth % 512 == 0 else 1
    gate_rows = 2 * heads + -2 * heads % 8
    shapes = [
        ((members, depth, columns), BF16),
        ((size, columns), BF16),
        ((2, size, columns), F32),
        ((size, 2 * heads), F32),
        ((gate_rows, size), F32),
        ((size, gate_rows), F32),
        ((heads, size, width), F32),
        ((heads, size, width), BF16),
        ((heads, width, size), F32),
        ((heads, width, size), BF16),
        ((heads, width, size), BF16),
        ((part, 3, width, width), BF16),
        ((part, 3, width, width), BF16),
    ]
    return pl.pallas_call(
        functools.partial(prepare_kernel, half, pieces),
        in_specs=[away()] * 5,
        out_specs=[here()] * len(shapes),
        out_shape=[jax.ShapeDtypeStruct(*s) for s in shapes],
        scratch_shapes=[
            pltpu.VMEM((size, depth), BF16),
            pltpu.VMEM((heads, size), F32),
            pltpu.VMEM((heads, size), F32),
            pltpu.VMEM((size, columns), F32),
            pltpu.VMEM((heads, 3, width, width), BF16),
            pltpu.SemaphoreType.DMA((pieces,)),
            pltpu.SemaphoreType.DMA((members, pieces)),
            pltpu.SemaphoreType.DMA((3,)),
        ],
        compiler_params=limit(28),
        name="prepare",
    )(*(pltpu.with_memory_space_constraint(x, pltpu.HBM) for x in (tokens, weights, logit, decay, out_grad)))


def weigh_kernel(heads, lane_ref, col_ref, gamma_ref, turned_ref, strong_ref, strong_t_ref):
    size = lane_ref.shape[1]
    rows, cols = grid_ids(size)
    for h in range(heads):
        gap = col_ref[:, h : h + 1] - lane_ref[h : h + 1, :]
        gamma = jnp.exp(jnp.where(rows >= cols, gap, FAR))
        turned = jnp.exp(jnp.where(rows <= cols, -gap, FAR))
        gamma_ref[h] = gamma
        turned_ref[h] = turned
        beta = col_ref[:, heads + h : heads + h + 1]
        beta_row = lane_ref[heads + h : heads + h + 1, :]
        strong_ref[h] = jnp.where(rows > cols, beta * gamma, 0.0)
        strong_t_ref[h] = jnp.where(rows < cols, beta_row * turned, 0.0)


def weigh(lanes, cols, heads):
    size = lanes.shape[1]
    shape = jax.ShapeDtypeStruct((heads, size, size), F32)
    return pl.pallas_call(
        functools.partial(weigh_kernel, heads),
        in_specs=[here()] * 2,
        out_specs=[here()] * 4,
        out_shape=[shape] * 4,
        compiler_params=limit(8),
        name="weigh",
    )(lanes, cols)


def pair_kernel(keep_ref, recv_ref, pay_ref):
    place = lax.axis_index("seq")
    first = lax.rem(place, 2) == 0
    chip = place // 2

    def join(early, late):
        width = early.shape[-1]
        for h in range(keep_ref.shape[0]):
            ahead = nn(late[h, 0], jnp.concatenate([early[h, 1], early[h, 0]], axis=1))
            up = ahead[:, :width] + late[h, 1].astype(F32)
            down = nn(late[h, 2], early[h, 0]) + early[h, 2].astype(F32)
            joint = ahead[:, width:].astype(BF16)
            for target in range(pay_ref.shape[0]):
                pay_ref[target, h, 0] = joint
                pay_ref[target, h, 1] = jnp.where(chip < target, up, down).astype(BF16)

    @pl.when(first)
    def _():
        join(keep_ref, recv_ref)

    @pl.when(jnp.logical_not(first))
    def _():
        join(recv_ref, keep_ref)


def join_pair(keep, recv, chips):
    half, _, width, _ = keep.shape
    return pl.pallas_call(
        pair_kernel,
        in_specs=[here()] * 2,
        out_specs=here(),
        out_shape=jax.ShapeDtypeStruct((chips, half, 2, width, width), BF16),
        compiler_params=limit(8),
        name="join_pair",
    )(keep, recv)


def two_terms(value):
    high = value.astype(BF16)
    return high, (value - high.astype(F32)).astype(BF16)


def scan_kernel(keep_ref, recv_ref, got_ref, own_ref, send_ref, enter, leave):
    place = lax.axis_index("seq")
    first = lax.rem(place, 2) == 0
    chip = place // 2
    low = lax.rem(chip, 2) == 1
    high = chip // 2 == 1
    every = range(keep_ref.shape[0])
    near_ref, far_ref, cross_ref = (got_ref.at[chip ^ i] for i in (1, 2, 3))

    def pairs(one, two):
        for h in every:

            @pl.when(high)
            def _():
                enter[h] = nn(two[h, 0], one[h, 1]) + two[h, 1].astype(F32)
                leave[h] = jnp.zeros_like(leave[h])

            @pl.when(jnp.logical_not(high))
            def _():
                leave[h] = nn(two[h, 1], one[h, 0]) + one[h, 1].astype(F32)
                enter[h] = jnp.zeros_like(enter[h])

    @pl.when(low)
    def _():
        pairs(cross_ref, far_ref)
        for h in every:
            top, rest = two_terms(enter[h])
            enter[h] = nn(near_ref[h, 0], top) + nn(near_ref[h, 0], rest) + near_ref[h, 1].astype(F32)

    @pl.when(jnp.logical_not(low))
    def _():
        pairs(far_ref, cross_ref)
        for h in every:
            top, rest = two_terms(leave[h])
            leave[h] = nn(top, near_ref[h, 0]) + nn(rest, near_ref[h, 0]) + near_ref[h, 1].astype(F32)

    def within(early, late, early_out, late_out):
        for h in every:
            top, rest = two_terms(enter[h])
            back, tail = two_terms(leave[h])
            middle = nn(early[h, 0], top) + nn(early[h, 0], rest) + early[h, 1].astype(F32)
            inner = nn(back, late[h, 0]) + nn(tail, late[h, 0]) + late[h, 2].astype(F32)
            early_out[h, 0] = top
            early_out[h, 1] = inner.astype(BF16)
            late_out[h, 0] = middle.astype(BF16)
            late_out[h, 1] = back

    @pl.when(first)
    def _():
        within(keep_ref, recv_ref, own_ref, send_ref)

    @pl.when(jnp.logical_not(first))
    def _():
        within(recv_ref, keep_ref, send_ref, own_ref)


def scan_chips(keep, recv, got):
    half, _, width, _ = keep.shape
    shape = jax.ShapeDtypeStruct((half, 2, width, width), BF16)
    return pl.pallas_call(
        scan_kernel,
        in_specs=[here()] * 3,
        out_specs=[here()] * 2,
        out_shape=[shape] * 2,
        scratch_shapes=[pltpu.VMEM((half, width, width), F32)] * 2,
        compiler_params=limit(8),
        name="scan_chips",
    )(keep, recv, got)


def part_at(slot, count):
    place = lax.axis_index("head")
    if count != 4:
        return lax.rem(place + slot + 1, count)
    if slot == 0:
        return 3 - place
    if slot == 3:
        return place
    low, high = ((2, 0), (3, 1)) if slot == 1 else ((1, 3), (0, 2))
    ends = jnp.where(place == 0, low[0], low[1])
    return jnp.where(place < 2, ends, jnp.where(place == 2, high[0], high[1]))


def grads_kernel(
    half, count, w_ref, unit_ref, scale_ref, col_ref, u_ref, wk_ref, dbt_ref, ktt_ref, gt_ref, og_ref,
    gamma_ref, turned_ref, strong_ref, strong_t_ref, own_ref, recv_ref,
    grad_ref, out_ref, edge_scr,
):
    heads, size, width = u_ref.shape
    if half:
        core = lax.rem(lax.axis_index("seq"), 2)
        edge_scr[pl.ds(core * half, half)] = own_ref[...]
        edge_scr[pl.ds((1 - core) * half, half)] = recv_ref[...]
    else:
        edge_scr[...] = own_ref[...]
    every = range(heads)
    spans = [slice(h * width, (h + 1) * width) for h in every]
    run_col = [col_ref[:, h : h + 1] for h in every]
    beta = [col_ref[:, heads + h : heads + h + 1] for h in every]
    open_col = [jnp.exp(run_col[h]) for h in every]
    fade_col = [jnp.exp(run_col[h][size - 1 : size, :] - run_col[h]) for h in every]
    update = [(u_ref[h] - nn(wk_ref[h], edge_scr[h, 0])).astype(BF16) for h in every]
    delta_t = [dbt_ref[h] + nn(edge_scr[h, 1], ktt_ref[h]) for h in every]
    delta = [d.T for d in delta_t]
    for h in every:
        span = spans[h]
        rows = jnp.concatenate([og_ref[:, span], delta[h].astype(BF16)], axis=0)
        lanes = nt(rows, update[h])
        turned = nn(update[h], jnp.concatenate([gt_ref[h], delta_t[h].astype(BF16)], axis=1))
        attend = (gamma_ref[h] * lanes[:size]).astype(BF16)
        attend_t = (turned_ref[h] * turned[:, :size]).astype(BF16)
        mix = (strong_ref[h] * lanes[size:] + strong_t_ref[h] * turned[:, size:]).astype(BF16)
        edge = nt(rows, edge_scr[h, 0])
        query = unit_ref[0, :, span]
        key = unit_ref[1, :, span]
        key_b = key.astype(BF16)
        dq = open_col[h] * edge[:size] + nn(attend, key_b)
        dk = (
            nn(attend_t, query.astype(BF16))
            - nn(mix, key_b)
            + fade_col[h] * nn(update[h], edge_scr[h, 1])
            - beta[h] * open_col[h] * edge[size:]
        )
        for slot, unit, slope in ((0, query, dq), (1, key, dk)):
            scale = scale_ref[:, slot * heads + h : slot * heads + h + 1]
            along = jnp.sum(unit * slope, axis=-1, keepdims=True)
            grad_ref[slot, :, span] = (scale * (slope - unit * along)).astype(BF16)
        grad_ref[2, :, span] = (beta[h] * delta[h]).astype(BF16)
    out_ref[...] = spread_grads(grad_ref, w_ref, 0, count).astype(out_ref.dtype)


def spread_grads(grad_ref, w_ref, slot, count):
    step = w_ref.shape[1] // count
    rows = pl.ds(pl.multiple_of(part_at(slot, count) * step, step), step)
    total = nt(grad_ref[0], w_ref[0, rows])
    for member in range(1, grad_ref.shape[0]):
        total = total + nt(grad_ref[member], w_ref[member, rows])
    return total


def grads(weights, prepared, out_grad, weighed, own, recv, half):
    unit, scale, col, u, wk, dbt, ktt, gt = prepared
    heads, size, width = u.shape
    members, depth, columns = weights.shape
    count = lax.axis_size("head")
    step = depth // count
    return pl.pallas_call(
        functools.partial(grads_kernel, half, count),
        in_specs=[here()] * 16,
        out_specs=[here()] * 2,
        out_shape=[
            jax.ShapeDtypeStruct((members, size, columns), BF16),
            jax.ShapeDtypeStruct((size, step), BF16),
        ],
        scratch_shapes=[
            pltpu.VMEM((heads, 2, width, width), BF16),
        ],
        compiler_params=limit(24),
        name="grads",
    )(weights, unit, scale, col, u, wk, dbt, ktt, gt, out_grad, *weighed, own, recv)


def others_kernel(count, w_ref, grad_ref, *outs):
    for i, out_ref in enumerate(outs):
        out_ref[...] = spread_grads(grad_ref, w_ref, i + 1, count).astype(out_ref.dtype)


def others(weights, grad):
    members, depth, columns = weights.shape
    size = grad.shape[1]
    count = lax.axis_size("head")
    step = depth // count
    kinds = [BF16] + [F32] * 2 if count == 4 else [BF16] * (count - 2) + [F32]
    return pl.pallas_call(
        functools.partial(others_kernel, count),
        in_specs=[here()] * 2,
        out_specs=[here()] * (count - 1),
        out_shape=[jax.ShapeDtypeStruct((size, step), k) for k in kinds],
        compiler_params=limit(16),
        name="others",
    )(weights, grad)


def swap(value, axis, count, mask):
    return lax.ppermute(value, axis, [(i, i ^ mask) for i in range(count)])


def edges_by_pairs(keep, send, count):
    recv = swap(send, "seq", count, 1)
    pay = join_pair(keep, recv, count // 2)
    same = [list(range(core, count, 2)) for core in range(2)]
    got = lax.all_to_all(pay, "seq", 0, 0, axis_index_groups=same)
    own, other = scan_chips(keep, recv, got)
    return own, swap(other, "seq", count, 1)


def edges_by_gather(keep, count):
    place = lax.axis_index("seq")
    gathered = lax.all_gather(keep, "seq")
    product = functools.partial(jnp.einsum, "hij,hjk->hik", precision=HIGH)

    def take(j):
        return lax.dynamic_index_in_dim(gathered, j, 0, False).astype(F32)

    def forward(j, state):
        part = take(j)
        return product(part[:, 0], state) + part[:, 1]

    def backward(i, state):
        part = take(count - 1 - i)
        return product(state, part[:, 0]) + part[:, 2]

    vacant = jnp.zeros(keep.shape[:1] + keep.shape[2:], F32)
    enter = lax.fori_loop(0, place, forward, vacant)
    leave = lax.fori_loop(0, count - 1 - place, backward, vacant)
    own = jnp.stack([enter, leave], axis=1).astype(BF16)
    return own, own


def sum_on_line(blocks):
    count = lax.axis_size("head")
    right = left = None
    for turn in range(count - 1):
        onward = blocks[count - 1 - turn]
        back = blocks[turn + 1]
        if turn:
            onward = (onward.astype(F32) + right.astype(F32)).astype(BF16)
            back = (back.astype(F32) + left.astype(F32)).astype(BF16)
        right = lax.ppermute(onward, "head", [(i, i + 1) for i in range(turn + 1)])
        left = lax.ppermute(back, "head", [(count - 1 - i, count - 2 - i) for i in range(turn + 1)])
    total = blocks[0]
    if count > 1:
        total = total + right.astype(F32) + left.astype(F32)
    return total.astype(BF16)


def sum_of_four(end, first, joint, own):
    outer = lax.ppermute(end, "head", [(0, 1), (3, 2)])
    inner = lax.ppermute(end, "head", [(1, 2), (2, 1)])
    ring = lax.ppermute(first, "head", [(0, 2), (2, 3), (3, 1), (1, 0)])
    joint = (joint + outer.astype(F32)).astype(BF16)
    joint = lax.ppermute(joint, "head", [(0, 1), (1, 3), (3, 2), (2, 0)])
    total = own + inner.astype(F32) + ring.astype(F32) + joint.astype(F32)
    return total.astype(BF16)


def on_device(tokens, qkv_weight, beta_logit, log_decay, out_grad):
    heads = beta_logit.shape[0]
    count = lax.axis_size("seq")
    paired = heads % 2 == 0 and count == 8
    half = heads // 2 if paired else 0
    held, kept_grad, unit, scale, lanes, col, u, wk, dbt, ktt, gt, keep, send = prepare(
        tokens, qkv_weight, beta_logit, log_decay, out_grad, half
    )
    if paired:
        own, recv = edges_by_pairs(keep, send, count)
    else:
        own, recv = edges_by_gather(keep, count)
    weighed = weigh(lanes, col, heads)
    prepared = (unit, scale, col, u, wk, dbt, ktt, gt)
    grad, end = grads(held, prepared, kept_grad, weighed, own, recv, half)
    rest = others(held, grad)
    if lax.axis_size("head") == 4:
        return sum_of_four(end, *rest)
    return sum_on_line([rest[-1], end, *rest[:-1]])


def solution(mesh):
    return jax.shard_map(
        on_device,
        mesh=mesh,
        in_specs=(
            P("seq", None),
            P(None, None, "head"),
            P("head", "seq"),
            P("head", "seq"),
            P("seq", "head"),
        ),
        out_specs=P("seq", "head"),
        check_vma=False,
    )
```

```python
import functools

import jax
import jax.numpy as jnp
from jax import lax
from jax.experimental import pallas as pl
from jax.experimental.pallas import tpu as pltpu
from jax.sharding import PartitionSpec as P


F32 = jnp.float32
BF16 = jnp.bfloat16
HIGH = lax.Precision.HIGHEST
FAR = -1e30


def nn(a, b):
    return lax.dot_general(a, b, (((1,), (0,)), ((), ())), preferred_element_type=F32)


def nt(a, b):
    return lax.dot_general(a, b, (((1,), (1,)), ((), ())), preferred_element_type=F32)


def grid_ids(size):
    rows = lax.broadcasted_iota(jnp.int32, (size, size), 0)
    cols = lax.broadcasted_iota(jnp.int32, (size, size), 1)
    return rows, cols


def exact_terms(value):
    high = value.astype(BF16)
    left = value - high.astype(F32)
    mid = left.astype(BF16)
    return high, mid, (left - mid.astype(F32)).astype(BF16)


def gates(logit, decay):
    heads, size = decay.shape
    rows, cols = grid_ids(size)
    upper = jnp.where(rows <= cols, 1.0, 0.0).astype(BF16)
    high, mid, low = exact_terms(decay)
    run = nn(high, upper) + nn(mid, upper) + nn(low, upper)
    lanes = [run, 1.0 / (1.0 + jnp.exp(-logit))]
    spare = -2 * heads % 8
    if spare:
        lanes.append(jnp.zeros((spare, size), F32))
    lanes = jnp.concatenate(lanes, axis=0)
    return lanes, lanes.T


def unit_rows(tensor):
    scale = lax.rsqrt(jnp.sum(tensor * tensor, axis=-1, keepdims=True) + 1e-06)
    return tensor * scale, scale


def unit_lower_inverse(couplings, fill):
    size = couplings[0].shape[0]
    base = size // 4
    lane_block = lax.broadcasted_iota(jnp.int32, (base, size), 1) // base
    on = [lane_block == b for b in range(4)]
    odd = lane_block % 2 == 1
    masks = [jnp.where(o, 1.0, 0.0).astype(BF16) for o in on]
    none = jnp.zeros((base, size), BF16)

    def strip(a, b):
        return a[b * base : (b + 1) * base]

    def spread(x):
        return jnp.concatenate([x * m for m in masks], axis=0)

    flat = [sum(jnp.where(on[b], strip(a, b), 0.0) for b in range(4)) for a in couplings]
    rest = [-x for x in flat]
    power = flat
    reach = 1
    while 2 * reach < base:
        narrow = [p.astype(BF16) for p in power]
        if reach == 1:
            power = [nn(p, spread(p)) for p in narrow]
            fill()
        else:
            both = [
                nn(jnp.concatenate([n.astype(BF16), p], axis=0), spread(p))
                for n, p in zip(rest, narrow)
            ]
            rest = [n + p + x[:base] for n, p, x in zip(rest, power, both)]
            power = [x[base:] for x in both]
            fill()
        reach *= 2
    if reach > 1:
        narrow = [p.astype(BF16) for p in power]
        rest = [n + p + nn(n.astype(BF16), spread(b)) for n, p, b in zip(rest, power, narrow)]
        fill()

    outer = [jnp.where(on[0], strip(a, 1), 0.0) + jnp.where(on[2], strip(a, 3), 0.0) for a in couplings]
    wide = [n.astype(BF16) for n in rest]
    half = [g + nn(g.astype(BF16), spread(n)) for g, n in zip(outer, wide)]
    half_b = [y.astype(BF16) for y in half]
    fill()
    late = [jnp.where(odd, n, 0.0) for n in rest]
    cross = [
        y + nn(l.astype(BF16), jnp.concatenate([none, b * masks[0], none, b * masks[2]], axis=0))
        for y, l, b in zip(half, late, half_b)
    ]
    fill()
    below = [l - z for l, z in zip(late, cross)]
    above = [jnp.where(odd, 0.0, n) for n in rest]
    mid = size // 2
    early = [jnp.concatenate([t[:, :mid], b[:, :mid]], axis=0).astype(BF16) for t, b in zip(above, below)]
    later = [jnp.concatenate([t[:, mid:], b[:, mid:]], axis=0).astype(BF16) for t, b in zip(above, below)]
    corner = [a[mid:, :mid] for a in couplings]
    half = [c + nn(c.astype(BF16), e) for c, e in zip(corner, early)]
    fill()
    cross = [y + nn(l, y.astype(BF16)) for y, l in zip(half, later)]
    blank = jnp.zeros((mid, mid), BF16)
    return [
        jnp.concatenate(
            [
                jnp.concatenate([e, blank], axis=1),
                jnp.concatenate([(-z).astype(BF16), l], axis=1),
            ],
            axis=0,
        )
        for e, z, l in zip(early, cross, later)
    ]


def prepare_kernel(
    half, pieces, tok_hbm, w_hbm, logit_hbm, decay_hbm, og_hbm,
    w_ref, og_ref, unit_ref, scale_ref, lane_ref, col_ref, u_ref, wk_ref, dbt_ref, ktt_ref, gt_ref,
    keep_ref, send_ref,
    tok_scr, logit_ref, decay_ref, value_scr, pay_scr, gamma_scr, pair_scr, tok_sem, w_sem, more_sem,
):
    heads, size = decay_ref.shape
    members, depth, columns = w_ref.shape
    width = columns // heads
    chunk = depth // pieces
    members_in_turn = (1, 2, 0)

    def part(i):
        return pl.ds(i * chunk, chunk)

    tok_copies = [
        pltpu.make_async_copy(tok_hbm.at[:, part(i)], tok_scr.at[:, part(i)], tok_sem.at[i])
        for i in range(pieces)
    ]
    w_copies = [
        [
            pltpu.make_async_copy(w_hbm.at[p, part(i)], w_ref.at[p, part(i)], w_sem.at[p, i])
            for i in range(pieces)
        ]
        for p in range(members)
    ]
    small = [(logit_hbm, logit_ref), (decay_hbm, decay_ref), (og_hbm, og_ref)]
    small = [pltpu.make_async_copy(a, b, more_sem.at[i]) for i, (a, b) in enumerate(small)]
    for copy in small:
        copy.start()
    for turn, p in enumerate(members_in_turn):
        for i in range(pieces):
            if turn == 0:
                tok_copies[i].start()
            w_copies[p][i].start()

    def product(p, i):
        span = slice(i * chunk, (i + 1) * chunk)
        return nn(tok_scr[:, span], w_ref[p, span])

    every = range(heads)
    spans = [slice(h * width, (h + 1) * width) for h in every]
    for copy in small:
        copy.wait()
    lanes, cols_of = gates(logit_ref[...], decay_ref[...])
    lane_ref[...] = lanes
    col_ref[...] = cols_of
    for h in every:
        gt_ref[h] = og_ref[:, spans[h]].astype(F32).T.astype(BF16)
    rows, cols = grid_ids(size)
    causal = rows >= cols
    strict = rows > cols
    run_col = [cols_of[:, h : h + 1] for h in every]
    run_row = [lanes[h : h + 1, :] for h in every]
    beta = [cols_of[:, heads + h : heads + h + 1] for h in every]

    total = None
    for i in range(pieces):
        tok_copies[i].wait()
        w_copies[1][i].wait()
        result = product(1, i)
        total = result if total is None else total + result

    def normalize(p, total):
        for h in every:
            unit, scale = unit_rows(total[:, spans[h]])
            unit_ref[p, :, spans[h]] = unit
            scale_ref[:, p * heads + h : p * heads + h + 1] = scale

    normalize(1, total)
    keys = [unit_ref[1, :, s] for s in spans]
    key_b = [k.astype(BF16) for k in keys]
    for h in every:
        gamma = jnp.exp(jnp.where(causal, run_col[h] - run_row[h], FAR))
        gamma_scr[h] = gamma
        pair_scr[h] = jnp.where(strict, beta[h] * gamma * nt(key_b[h], key_b[h]), 0.0)
    for i in range(pieces):
        w_copies[2][i].wait()
    waiting = [(p, i) for p in (2, 0) for i in range(pieces)]
    totals = {2: None, 0: None}

    def fill():
        if waiting:
            p, i = waiting.pop(0)
            if p == 0 and i == 0:
                for copy in w_copies[0]:
                    copy.wait()
            result = product(p, i)
            totals[p] = result if totals[p] is None else totals[p] + result

    inverse = unit_lower_inverse([pair_scr[h] for h in every], fill)
    while waiting:
        fill()
    value_scr[...] = totals[2]
    normalize(0, totals[0])
    queries = [unit_ref[0, :, s] for s in spans]
    scores = [(gamma_scr[h] * nt(queries[h].astype(BF16), key_b[h])).astype(BF16) for h in every]
    last = [run_col[h][size - 1 : size, :] for h in every]
    open_col = [jnp.exp(run_col[h]) for h in every]
    fade_row = [jnp.exp(last[h] - run_row[h]) for h in every]
    write_key = [beta[h] * open_col[h] * keys[h] for h in every]
    right = [
        jnp.concatenate([beta[h] * value_scr[:, spans[h]], write_key[h]], axis=1) for h in every
    ]
    solved = [right[h] + nn(inverse[h], right[h].astype(BF16)) for h in every]
    fade_t = [keys[h].T * fade_row[h] for h in every]
    left = [jnp.concatenate([nn(gt_ref[h], scores[h]), fade_t[h]], axis=0) for h in every]
    back = [left[h] + nn(left[h].astype(BF16), inverse[h]) for h in every]
    e_rows, e_cols = grid_ids(width)
    for h in every:
        fade_hi = fade_t[h].astype(BF16)
        fade_lo = (fade_t[h] - fade_hi.astype(F32)).astype(BF16)
        solved_hi = solved[h].astype(BF16)
        solved_lo = (solved[h][:, :width] - solved_hi[:, :width].astype(F32)).astype(BF16)
        state = nn(fade_hi, solved_hi)
        fill = state[:, :width] + nn(fade_lo, solved_hi[:, :width]) + nn(fade_hi, solved_lo)
        unit = jnp.where(e_rows == e_cols, jnp.exp(last[h]), 0.0)
        seed = nn(gt_ref[h], (open_col[h] * queries[h]).astype(BF16)) - nn(
            back[h][:width].astype(BF16), write_key[h].astype(BF16)
        )
        pay_scr[h, 0] = (unit - state[:, width:]).astype(BF16)
        pay_scr[h, 1] = fill.astype(BF16)
        pay_scr[h, 2] = seed.astype(BF16)
        u_ref[h] = solved[h][:, :width]
        wk_ref[h] = solved_hi[:, width:]
        dbt_ref[h] = back[h][:width]
        ktt_ref[h] = back[h][width:].astype(BF16)
    if half:
        core = lax.rem(lax.axis_index("seq"), 2)
        keep_ref[...] = pay_scr[pl.ds(core * half, half)]
        send_ref[...] = pay_scr[pl.ds((1 - core) * half, half)]
    else:
        keep_ref[...] = pay_scr[...]
        send_ref[...] = pay_scr[...]


def here():
    return pl.BlockSpec(memory_space=pltpu.VMEM)


def away():
    return pl.BlockSpec(memory_space=pltpu.HBM)


def limit(mebibytes):
    return pltpu.CompilerParams(vmem_limit_bytes=mebibytes * 2**20)


def prepare(tokens, weights, logit, decay, out_grad, half):
    heads, size = logit.shape
    members, depth, columns = weights.shape
    width = columns // heads
    part = half or heads
    pieces = 4 if depth % 512 == 0 else 1
    gate_rows = 2 * heads + -2 * heads % 8
    shapes = [
        ((members, depth, columns), BF16),
        ((size, columns), BF16),
        ((2, size, columns), F32),
        ((size, 2 * heads), F32),
        ((gate_rows, size), F32),
        ((size, gate_rows), F32),
        ((heads, size, width), F32),
        ((heads, size, width), BF16),
        ((heads, width, size), F32),
        ((heads, width, size), BF16),
        ((heads, width, size), BF16),
        ((part, 3, width, width), BF16),
        ((part, 3, width, width), BF16),
    ]
    return pl.pallas_call(
        functools.partial(prepare_kernel, half, pieces),
        in_specs=[away()] * 5,
        out_specs=[here()] * len(shapes),
        out_shape=[jax.ShapeDtypeStruct(*s) for s in shapes],
        scratch_shapes=[
            pltpu.VMEM((size, depth), BF16),
            pltpu.VMEM((heads, size), F32),
            pltpu.VMEM((heads, size), F32),
            pltpu.VMEM((size, columns), F32),
            pltpu.VMEM((heads, 3, width, width), BF16),
            pltpu.VMEM((heads, size, size), F32),
            pltpu.VMEM((heads, size, size), F32),
            pltpu.SemaphoreType.DMA((pieces,)),
            pltpu.SemaphoreType.DMA((members, pieces)),
            pltpu.SemaphoreType.DMA((3,)),
        ],
        compiler_params=limit(28),
        name="prepare",
    )(*(pltpu.with_memory_space_constraint(x, pltpu.HBM) for x in (tokens, weights, logit, decay, out_grad)))


def weigh_kernel(heads, lane_ref, col_ref, gamma_ref, turned_ref, strong_ref, strong_t_ref):
    size = lane_ref.shape[1]
    rows, cols = grid_ids(size)
    for h in range(heads):
        gap = col_ref[:, h : h + 1] - lane_ref[h : h + 1, :]
        gamma = jnp.exp(jnp.where(rows >= cols, gap, FAR))
        turned = jnp.exp(jnp.where(rows <= cols, -gap, FAR))
        gamma_ref[h] = gamma
        turned_ref[h] = turned
        beta = col_ref[:, heads + h : heads + h + 1]
        beta_row = lane_ref[heads + h : heads + h + 1, :]
        strong_ref[h] = jnp.where(rows > cols, beta * gamma, 0.0)
        strong_t_ref[h] = jnp.where(rows < cols, beta_row * turned, 0.0)


def weigh(lanes, cols, heads):
    size = lanes.shape[1]
    shape = jax.ShapeDtypeStruct((heads, size, size), F32)
    return pl.pallas_call(
        functools.partial(weigh_kernel, heads),
        in_specs=[here()] * 2,
        out_specs=[here()] * 4,
        out_shape=[shape] * 4,
        compiler_params=limit(8),
        name="weigh",
    )(lanes, cols)


def pair_kernel(levels, keep_ref, recv_ref, *pay_refs):
    place = lax.axis_index("seq")
    first = lax.rem(place, 2) == 0
    chip = place // 2

    def join(early, late):
        width = early.shape[-1]
        for h in range(keep_ref.shape[0]):
            ahead = nn(late[h, 0], jnp.concatenate([early[h, 1], early[h, 0]], axis=1))
            up = ahead[:, :width] + late[h, 1].astype(F32)
            down = nn(late[h, 2], early[h, 0]) + early[h, 2].astype(F32)
            joint = ahead[:, width:].astype(BF16)
            for level in range(levels):
                upward = lax.rem(chip // (1 << level), 2) == 0
                pay_refs[level][h, 0] = joint
                pay_refs[level][h, 1] = jnp.where(upward, up, down).astype(BF16)

    @pl.when(first)
    def _():
        join(keep_ref, recv_ref)

    @pl.when(jnp.logical_not(first))
    def _():
        join(recv_ref, keep_ref)


def join_pair(keep, recv, levels):
    half, _, width, _ = keep.shape
    shape = jax.ShapeDtypeStruct((half, 2, width, width), BF16)
    return pl.pallas_call(
        functools.partial(pair_kernel, levels),
        in_specs=[here()] * 2,
        out_specs=[here()] * levels,
        out_shape=[shape] * levels,
        compiler_params=limit(8),
        name="join_pair",
    )(keep, recv)


def two_terms(value):
    high = value.astype(BF16)
    return high, (value - high.astype(F32)).astype(BF16)


def scan_kernel(keep_ref, recv_ref, near_ref, far_ref, cross_ref, own_ref, send_ref, enter, leave):
    place = lax.axis_index("seq")
    first = lax.rem(place, 2) == 0
    chip = place // 2
    low = lax.rem(chip, 2) == 1
    high = chip // 2 == 1
    every = range(keep_ref.shape[0])

    def pairs(one, two):
        for h in every:

            @pl.when(high)
            def _():
                enter[h] = nn(two[h, 0], one[h, 1]) + two[h, 1].astype(F32)
                leave[h] = jnp.zeros_like(leave[h])

            @pl.when(jnp.logical_not(high))
            def _():
                leave[h] = nn(two[h, 1], one[h, 0]) + one[h, 1].astype(F32)
                enter[h] = jnp.zeros_like(enter[h])

    @pl.when(low)
    def _():
        pairs(cross_ref, far_ref)
        for h in every:
            top, rest = two_terms(enter[h])
            enter[h] = nn(near_ref[h, 0], top) + nn(near_ref[h, 0], rest) + near_ref[h, 1].astype(F32)

    @pl.when(jnp.logical_not(low))
    def _():
        pairs(far_ref, cross_ref)
        for h in every:
            top, rest = two_terms(leave[h])
            leave[h] = nn(top, near_ref[h, 0]) + nn(rest, near_ref[h, 0]) + near_ref[h, 1].astype(F32)

    def within(early, late, early_out, late_out):
        for h in every:
            top, rest = two_terms(enter[h])
            back, tail = two_terms(leave[h])
            middle = nn(early[h, 0], top) + nn(early[h, 0], rest) + early[h, 1].astype(F32)
            inner = nn(back, late[h, 0]) + nn(tail, late[h, 0]) + late[h, 2].astype(F32)
            early_out[h, 0] = top
            early_out[h, 1] = inner.astype(BF16)
            late_out[h, 0] = middle.astype(BF16)
            late_out[h, 1] = back

    @pl.when(first)
    def _():
        within(keep_ref, recv_ref, own_ref, send_ref)

    @pl.when(jnp.logical_not(first))
    def _():
        within(recv_ref, keep_ref, send_ref, own_ref)


def scan_chips(keep, recv, near, far, cross):
    half, _, width, _ = keep.shape
    shape = jax.ShapeDtypeStruct((half, 2, width, width), BF16)
    return pl.pallas_call(
        scan_kernel,
        in_specs=[here()] * 5,
        out_specs=[here()] * 2,
        out_shape=[shape] * 2,
        scratch_shapes=[pltpu.VMEM((half, width, width), F32)] * 2,
        compiler_params=limit(8),
        name="scan_chips",
    )(keep, recv, near, far, cross)


def part_at(slot, count):
    place = lax.axis_index("head")
    if count != 4:
        return lax.rem(place + slot + 1, count)
    if slot == 0:
        return 3 - place
    if slot == 3:
        return place
    low, high = ((2, 0), (3, 1)) if slot == 1 else ((1, 3), (0, 2))
    ends = jnp.where(place == 0, low[0], low[1])
    return jnp.where(place < 2, ends, jnp.where(place == 2, high[0], high[1]))


def early_parts(count):
    return 2 if count == 4 else 1


def grads_kernel(
    half, count, w_ref, unit_ref, scale_ref, col_ref, u_ref, wk_ref, dbt_ref, ktt_ref, gt_ref, og_ref,
    gamma_ref, turned_ref, strong_ref, strong_t_ref, own_ref, recv_ref,
    grad_ref, *rest,
):
    heads, size, width = u_ref.shape
    outs, edge_scr = rest[:-1], rest[-1]
    if half:
        core = lax.rem(lax.axis_index("seq"), 2)
        edge_scr[pl.ds(core * half, half)] = own_ref[...]
        edge_scr[pl.ds((1 - core) * half, half)] = recv_ref[...]
    else:
        edge_scr[...] = own_ref[...]
    every = range(heads)
    spans = [slice(h * width, (h + 1) * width) for h in every]
    run_col = [col_ref[:, h : h + 1] for h in every]
    beta = [col_ref[:, heads + h : heads + h + 1] for h in every]
    open_col = [jnp.exp(run_col[h]) for h in every]
    fade_col = [jnp.exp(run_col[h][size - 1 : size, :] - run_col[h]) for h in every]
    update = [(u_ref[h] - nn(wk_ref[h], edge_scr[h, 0])).astype(BF16) for h in every]
    delta_t = [dbt_ref[h] + nn(edge_scr[h, 1], ktt_ref[h]) for h in every]
    delta = [d.T for d in delta_t]
    totals = [None] * len(outs)
    group = 2 if heads % 2 == 0 else 1
    for h in every:
        span = spans[h]
        rows = jnp.concatenate([og_ref[:, span], delta[h].astype(BF16)], axis=0)
        lanes = nt(rows, update[h])
        turned = nn(update[h], jnp.concatenate([gt_ref[h], delta_t[h].astype(BF16)], axis=1))
        attend = (gamma_ref[h] * lanes[:size]).astype(BF16)
        attend_t = (turned_ref[h] * turned[:, :size]).astype(BF16)
        mix = (strong_ref[h] * lanes[size:] + strong_t_ref[h] * turned[:, size:]).astype(BF16)
        edge = nt(rows, edge_scr[h, 0])
        query = unit_ref[0, :, span]
        key = unit_ref[1, :, span]
        key_b = key.astype(BF16)
        dq = open_col[h] * edge[:size] + nn(attend, key_b)
        dk = (
            nn(attend_t, query.astype(BF16))
            - nn(mix, key_b)
            + fade_col[h] * nn(update[h], edge_scr[h, 1])
            - beta[h] * open_col[h] * edge[size:]
        )
        for slot, unit, slope in ((0, query, dq), (1, key, dk)):
            scale = scale_ref[:, slot * heads + h : slot * heads + h + 1]
            along = jnp.sum(unit * slope, axis=-1, keepdims=True)
            grad_ref[slot, :, span] = (scale * (slope - unit * along)).astype(BF16)
        grad_ref[2, :, span] = (beta[h] * delta[h]).astype(BF16)
        if h % group == group - 1:
            ready = slice((h - group + 1) * width, (h + 1) * width)
            for slot in range(len(outs)):
                part = spread_grads(grad_ref, w_ref, slot, count, ready)
                totals[slot] = part if h < group else totals[slot] + part
    for out_ref, total in zip(outs, totals):
        out_ref[...] = total.astype(out_ref.dtype)


def spread_grads(grad_ref, w_ref, slot, count, span=slice(None)):
    step = w_ref.shape[1] // count
    rows = pl.ds(pl.multiple_of(part_at(slot, count) * step, step), step)
    total = nt(grad_ref[0, :, span], w_ref[0, rows, span])
    for member in range(1, grad_ref.shape[0]):
        total = total + nt(grad_ref[member, :, span], w_ref[member, rows, span])
    return total


def grads(weights, prepared, out_grad, weighed, own, recv, half):
    unit, scale, col, u, wk, dbt, ktt, gt = prepared
    heads, size, width = u.shape
    members, depth, columns = weights.shape
    count = lax.axis_size("head")
    step = depth // count
    early = early_parts(count)
    return pl.pallas_call(
        functools.partial(grads_kernel, half, count),
        in_specs=[here()] * 16,
        out_specs=[here()] * (1 + early),
        out_shape=[jax.ShapeDtypeStruct((members, size, columns), BF16)]
        + [jax.ShapeDtypeStruct((size, step), BF16)] * early,
        scratch_shapes=[
            pltpu.VMEM((heads, 2, width, width), BF16),
        ],
        compiler_params=limit(24),
        name="grads",
    )(weights, unit, scale, col, u, wk, dbt, ktt, gt, out_grad, *weighed, own, recv)


def others_kernel(count, w_ref, grad_ref, *outs):
    for i, out_ref in enumerate(outs):
        out_ref[...] = spread_grads(grad_ref, w_ref, i + early_parts(count), count).astype(out_ref.dtype)


def others(weights, grad):
    _, depth, _ = weights.shape
    size = grad.shape[1]
    count = lax.axis_size("head")
    step = depth // count
    kinds = [F32] * 2 if count == 4 else [BF16] * (count - 2) + [F32]
    return pl.pallas_call(
        functools.partial(others_kernel, count),
        in_specs=[here()] * 2,
        out_specs=[here()] * len(kinds),
        out_shape=[jax.ShapeDtypeStruct((size, step), k) for k in kinds],
        compiler_params=limit(16),
        name="others",
    )(weights, grad)


def swap(value, axis, count, mask):
    return lax.ppermute(value, axis, [(i, i ^ mask) for i in range(count)])


def edges_by_pairs(keep, send, count):
    recv = swap(send, "seq", count, 1)
    low, high = join_pair(keep, recv, 2)
    near = swap(low, "seq", count, 2)
    far = swap(high, "seq", count, 4)
    cross = swap(high, "seq", count, 6)
    own, other = scan_chips(keep, recv, near, far, cross)
    return own, swap(other, "seq", count, 1)


def edges_by_gather(keep, count):
    place = lax.axis_index("seq")
    gathered = lax.all_gather(keep, "seq")
    product = functools.partial(jnp.einsum, "hij,hjk->hik", precision=HIGH)

    def take(j):
        return lax.dynamic_index_in_dim(gathered, j, 0, False).astype(F32)

    def forward(j, state):
        part = take(j)
        return product(part[:, 0], state) + part[:, 1]

    def backward(i, state):
        part = take(count - 1 - i)
        return product(state, part[:, 0]) + part[:, 2]

    vacant = jnp.zeros(keep.shape[:1] + keep.shape[2:], F32)
    enter = lax.fori_loop(0, place, forward, vacant)
    leave = lax.fori_loop(0, count - 1 - place, backward, vacant)
    own = jnp.stack([enter, leave], axis=1).astype(BF16)
    return own, own


def sum_on_line(blocks):
    count = lax.axis_size("head")
    right = left = None
    for turn in range(count - 1):
        onward = blocks[count - 1 - turn]
        back = blocks[turn + 1]
        if turn:
            onward = (onward.astype(F32) + right.astype(F32)).astype(BF16)
            back = (back.astype(F32) + left.astype(F32)).astype(BF16)
        right = lax.ppermute(onward, "head", [(i, i + 1) for i in range(turn + 1)])
        left = lax.ppermute(back, "head", [(count - 1 - i, count - 2 - i) for i in range(turn + 1)])
    total = blocks[0]
    if count > 1:
        total = total + right.astype(F32) + left.astype(F32)
    return total.astype(BF16)


def sum_of_four(end, first, joint, own):
    outer = lax.ppermute(end, "head", [(0, 1), (3, 2)])
    inner = lax.ppermute(end, "head", [(1, 2), (2, 1)])
    ring = lax.ppermute(first, "head", [(0, 2), (2, 3), (3, 1), (1, 0)])
    joint = (joint + outer.astype(F32)).astype(BF16)
    joint = lax.ppermute(joint, "head", [(0, 1), (1, 3), (3, 2), (2, 0)])
    total = own + inner.astype(F32) + ring.astype(F32) + joint.astype(F32)
    return total.astype(BF16)


def step_on_device(tokens, qkv_weight, beta_logit, log_decay, out_grad):
    heads = beta_logit.shape[0]
    count = lax.axis_size("seq")
    paired = heads % 2 == 0 and count == 8
    half = heads // 2 if paired else 0
    held, kept_grad, unit, scale, lanes, col, u, wk, dbt, ktt, gt, keep, send = prepare(
        tokens, qkv_weight, beta_logit, log_decay, out_grad, half
    )
    if paired:
        own, recv = edges_by_pairs(keep, send, count)
    else:
        own, recv = edges_by_gather(keep, count)
    weighed = weigh(lanes, col, heads)
    prepared = (unit, scale, col, u, wk, dbt, ktt, gt)
    grad, *early = grads(held, prepared, kept_grad, weighed, own, recv, half)
    rest = others(held, grad)
    if lax.axis_size("head") == 4:
        return sum_of_four(*early, *rest)
    return sum_on_line([rest[-1], *early, *rest[:-1]])


def solution(mesh):
    return jax.shard_map(
        step_on_device,
        mesh=mesh,
        in_specs=(
            P("seq", None),
            P(None, None, "head"),
            P("head", "seq"),
            P("head", "seq"),
            P("seq", "head"),
        ),
        out_specs=P("seq", "head"),
        check_vma=False,
    )
```

```python
import functools

import jax
import jax.numpy as jnp
from jax import lax
from jax.experimental import pallas as pl
from jax.experimental.pallas import tpu as pltpu
from jax.sharding import PartitionSpec as P


F32 = jnp.float32
BF16 = jnp.bfloat16
HIGH = lax.Precision.HIGHEST
FAR = -1e30


def nn(a, b):
    return lax.dot_general(a, b, (((1,), (0,)), ((), ())), preferred_element_type=F32)


def nt(a, b):
    return lax.dot_general(a, b, (((1,), (1,)), ((), ())), preferred_element_type=F32)


def grid_ids(size):
    rows = lax.broadcasted_iota(jnp.int32, (size, size), 0)
    cols = lax.broadcasted_iota(jnp.int32, (size, size), 1)
    return rows, cols


def exact_terms(value):
    high = value.astype(BF16)
    left = value - high.astype(F32)
    mid = left.astype(BF16)
    return high, mid, (left - mid.astype(F32)).astype(BF16)


def gates(logit, decay):
    heads, size = decay.shape
    rows, cols = grid_ids(size)
    upper = jnp.where(rows <= cols, 1.0, 0.0).astype(BF16)
    high, mid, low = exact_terms(decay)
    run = nn(high, upper) + nn(mid, upper) + nn(low, upper)
    lanes = [run, 1.0 / (1.0 + jnp.exp(-logit))]
    spare = -2 * heads % 8
    if spare:
        lanes.append(jnp.zeros((spare, size), F32))
    lanes = jnp.concatenate(lanes, axis=0)
    return lanes, lanes.T


def unit_rows(tensor):
    scale = lax.rsqrt(jnp.sum(tensor * tensor, axis=-1, keepdims=True) + 1e-06)
    return tensor * scale, scale


def unit_lower_inverse(couplings, fill):
    size = couplings[0].shape[0]
    base = size // 4
    lane_block = lax.broadcasted_iota(jnp.int32, (base, size), 1) // base
    on = [lane_block == b for b in range(4)]
    odd = lane_block % 2 == 1
    masks = [jnp.where(o, 1.0, 0.0).astype(BF16) for o in on]
    none = jnp.zeros((base, size), BF16)

    def strip(a, b):
        return a[b * base : (b + 1) * base]

    def spread(x):
        return jnp.concatenate([x * m for m in masks], axis=0)

    flat = [sum(jnp.where(on[b], strip(a, b), 0.0) for b in range(4)) for a in couplings]
    rest = [-x for x in flat]
    power = flat
    reach = 1
    while 2 * reach < base:
        narrow = [p.astype(BF16) for p in power]
        if reach == 1:
            power = [nn(p, spread(p)) for p in narrow]
            fill()
        else:
            both = [
                nn(jnp.concatenate([n.astype(BF16), p], axis=0), spread(p))
                for n, p in zip(rest, narrow)
            ]
            rest = [n + p + x[:base] for n, p, x in zip(rest, power, both)]
            power = [x[base:] for x in both]
            fill()
        reach *= 2
    if reach > 1:
        narrow = [p.astype(BF16) for p in power]
        rest = [n + p + nn(n.astype(BF16), spread(b)) for n, p, b in zip(rest, power, narrow)]
        fill()

    outer = [jnp.where(on[0], strip(a, 1), 0.0) + jnp.where(on[2], strip(a, 3), 0.0) for a in couplings]
    wide = [n.astype(BF16) for n in rest]
    half = [g + nn(g.astype(BF16), spread(n)) for g, n in zip(outer, wide)]
    half_b = [y.astype(BF16) for y in half]
    fill()
    late = [jnp.where(odd, n, 0.0) for n in rest]
    cross = [
        y + nn(l.astype(BF16), jnp.concatenate([none, b * masks[0], none, b * masks[2]], axis=0))
        for y, l, b in zip(half, late, half_b)
    ]
    fill()
    below = [l - z for l, z in zip(late, cross)]
    above = [jnp.where(odd, 0.0, n) for n in rest]
    mid = size // 2
    early = [jnp.concatenate([t[:, :mid], b[:, :mid]], axis=0).astype(BF16) for t, b in zip(above, below)]
    later = [jnp.concatenate([t[:, mid:], b[:, mid:]], axis=0).astype(BF16) for t, b in zip(above, below)]
    corner = [a[mid:, :mid] for a in couplings]
    half = [c + nn(c.astype(BF16), e) for c, e in zip(corner, early)]
    fill()
    cross = [y + nn(l, y.astype(BF16)) for y, l in zip(half, later)]
    blank = jnp.zeros((mid, mid), BF16)
    return [
        jnp.concatenate(
            [
                jnp.concatenate([e, blank], axis=1),
                jnp.concatenate([(-z).astype(BF16), l], axis=1),
            ],
            axis=0,
        )
        for e, z, l in zip(early, cross, later)
    ]


def prepare_kernel(
    half, pieces, tok_hbm, w_hbm, logit_hbm, decay_hbm, og_hbm,
    w_ref, og_ref, unit_ref, scale_ref, lane_ref, col_ref, u_ref, wk_ref, dbt_ref, ktt_ref, gt_ref,
    keep_ref, send_ref,
    tok_scr, logit_ref, decay_ref, value_scr, pay_scr, gamma_scr, pair_scr, tok_sem, w_sem, more_sem,
):
    heads, size = decay_ref.shape
    members, depth, columns = w_ref.shape
    width = columns // heads
    chunk = depth // pieces

    def part(i):
        return pl.ds(i * chunk, chunk)

    tok_copies = [
        pltpu.make_async_copy(tok_hbm.at[:, part(i)], tok_scr.at[:, part(i)], tok_sem.at[i])
        for i in range(pieces)
    ]
    w_copies = [
        [
            pltpu.make_async_copy(w_hbm.at[p, part(i)], w_ref.at[p, part(i)], w_sem.at[p, i])
            for i in range(pieces)
        ]
        for p in range(members)
    ]
    small = [(logit_hbm, logit_ref), (decay_hbm, decay_ref), (og_hbm, og_ref)]
    small = [pltpu.make_async_copy(a, b, more_sem.at[i]) for i, (a, b) in enumerate(small)]
    for copy in small[:2]:
        copy.start()
    for i in range(pieces):
        tok_copies[i].start()
        w_copies[1][i].start()
    small[2].start()

    def product(p, i):
        span = slice(i * chunk, (i + 1) * chunk)
        return nn(tok_scr[:, span], w_ref[p, span])

    every = range(heads)
    spans = [slice(h * width, (h + 1) * width) for h in every]
    for copy in small[:2]:
        copy.wait()
    lanes, cols_of = gates(logit_ref[...], decay_ref[...])
    lane_ref[...] = lanes
    col_ref[...] = cols_of
    rows, cols = grid_ids(size)
    causal = rows >= cols
    strict = rows > cols
    run_col = [cols_of[:, h : h + 1] for h in every]
    run_row = [lanes[h : h + 1, :] for h in every]
    beta = [cols_of[:, heads + h : heads + h + 1] for h in every]

    total = None
    for i in range(pieces):
        tok_copies[i].wait()
        w_copies[1][i].wait()
        if i == 0:
            for p in (2, 0):
                for copy in w_copies[p]:
                    copy.start()
        result = product(1, i)
        total = result if total is None else total + result

    def normalize(p, total):
        for h in every:
            unit, scale = unit_rows(total[:, spans[h]])
            unit_ref[p, :, spans[h]] = unit
            scale_ref[:, p * heads + h : p * heads + h + 1] = scale

    small[2].wait()
    for h in every:
        gt_ref[h] = og_ref[:, spans[h]].astype(F32).T.astype(BF16)
    normalize(1, total)
    keys = [unit_ref[1, :, s] for s in spans]
    key_b = [k.astype(BF16) for k in keys]
    for h in every:
        gamma = jnp.exp(jnp.where(causal, run_col[h] - run_row[h], FAR))
        gamma_scr[h] = gamma
        pair_scr[h] = jnp.where(strict, beta[h] * gamma * nt(key_b[h], key_b[h]), 0.0)
    for i in range(pieces):
        w_copies[2][i].wait()
    waiting = [(p, i) for p in (2, 0) for i in range(pieces)]
    totals = {2: None, 0: None}

    def fill():
        if waiting:
            p, i = waiting.pop(0)
            if p == 0 and i == 0:
                for copy in w_copies[0]:
                    copy.wait()
            result = product(p, i)
            totals[p] = result if totals[p] is None else totals[p] + result

    inverse = unit_lower_inverse([pair_scr[h] for h in every], fill)
    while waiting:
        fill()
    value_scr[...] = totals[2]
    normalize(0, totals[0])
    queries = [unit_ref[0, :, s] for s in spans]
    scores = [(gamma_scr[h] * nt(queries[h].astype(BF16), key_b[h])).astype(BF16) for h in every]
    last = [run_col[h][size - 1 : size, :] for h in every]
    open_col = [jnp.exp(run_col[h]) for h in every]
    fade_row = [jnp.exp(last[h] - run_row[h]) for h in every]
    write_key = [beta[h] * open_col[h] * keys[h] for h in every]
    right = [
        jnp.concatenate([beta[h] * value_scr[:, spans[h]], write_key[h]], axis=1) for h in every
    ]
    solved = [right[h] + nn(inverse[h], right[h].astype(BF16)) for h in every]
    fade_t = [keys[h].T * fade_row[h] for h in every]
    left = [jnp.concatenate([nn(gt_ref[h], scores[h]), fade_t[h]], axis=0) for h in every]
    back = [left[h] + nn(left[h].astype(BF16), inverse[h]) for h in every]
    e_rows, e_cols = grid_ids(width)
    for h in every:
        fade_hi = fade_t[h].astype(BF16)
        fade_lo = (fade_t[h] - fade_hi.astype(F32)).astype(BF16)
        solved_hi = solved[h].astype(BF16)
        solved_lo = (solved[h][:, :width] - solved_hi[:, :width].astype(F32)).astype(BF16)
        state = nn(fade_hi, solved_hi)
        fill = state[:, :width] + nn(fade_lo, solved_hi[:, :width]) + nn(fade_hi, solved_lo)
        unit = jnp.where(e_rows == e_cols, jnp.exp(last[h]), 0.0)
        seed = nn(gt_ref[h], (open_col[h] * queries[h]).astype(BF16)) - nn(
            back[h][:width].astype(BF16), write_key[h].astype(BF16)
        )
        pay_scr[h, 0] = (unit - state[:, width:]).astype(BF16)
        pay_scr[h, 1] = fill.astype(BF16)
        pay_scr[h, 2] = seed.astype(BF16)
        u_ref[h] = solved[h][:, :width]
        wk_ref[h] = solved_hi[:, width:]
        dbt_ref[h] = back[h][:width]
        ktt_ref[h] = back[h][width:].astype(BF16)
    if half:
        core = lax.rem(lax.axis_index("seq"), 2)
        keep_ref[...] = pay_scr[pl.ds(core * half, half)]
        send_ref[...] = pay_scr[pl.ds((1 - core) * half, half)]
    else:
        keep_ref[...] = pay_scr[...]
        send_ref[...] = pay_scr[...]


def here():
    return pl.BlockSpec(memory_space=pltpu.VMEM)


def away():
    return pl.BlockSpec(memory_space=pltpu.HBM)


def limit(mebibytes):
    return pltpu.CompilerParams(vmem_limit_bytes=mebibytes * 2**20)


def prepare(tokens, weights, logit, decay, out_grad, half):
    heads, size = logit.shape
    members, depth, columns = weights.shape
    width = columns // heads
    part = half or heads
    pieces = 4 if depth % 512 == 0 else 1
    gate_rows = 2 * heads + -2 * heads % 8
    shapes = [
        ((members, depth, columns), BF16),
        ((size, columns), BF16),
        ((2, size, columns), F32),
        ((size, 2 * heads), F32),
        ((gate_rows, size), F32),
        ((size, gate_rows), F32),
        ((heads, size, width), F32),
        ((heads, size, width), BF16),
        ((heads, width, size), F32),
        ((heads, width, size), BF16),
        ((heads, width, size), BF16),
        ((part, 3, width, width), BF16),
        ((part, 3, width, width), BF16),
    ]
    return pl.pallas_call(
        functools.partial(prepare_kernel, half, pieces),
        in_specs=[away()] * 5,
        out_specs=[here()] * len(shapes),
        out_shape=[jax.ShapeDtypeStruct(*s) for s in shapes],
        scratch_shapes=[
            pltpu.VMEM((size, depth), BF16),
            pltpu.VMEM((heads, size), F32),
            pltpu.VMEM((heads, size), F32),
            pltpu.VMEM((size, columns), F32),
            pltpu.VMEM((heads, 3, width, width), BF16),
            pltpu.VMEM((heads, size, size), F32),
            pltpu.VMEM((heads, size, size), F32),
            pltpu.SemaphoreType.DMA((pieces,)),
            pltpu.SemaphoreType.DMA((members, pieces)),
            pltpu.SemaphoreType.DMA((3,)),
        ],
        compiler_params=limit(16),
        name="prepare",
    )(*(pltpu.with_memory_space_constraint(x, pltpu.HBM) for x in (tokens, weights, logit, decay, out_grad)))


def weigh_kernel(heads, lane_ref, col_ref, gamma_ref, turned_ref, strong_ref, strong_t_ref):
    size = lane_ref.shape[1]
    rows, cols = grid_ids(size)
    for h in range(heads):
        gap = col_ref[:, h : h + 1] - lane_ref[h : h + 1, :]
        gamma = jnp.exp(jnp.where(rows >= cols, gap, FAR))
        turned = jnp.exp(jnp.where(rows <= cols, -gap, FAR))
        gamma_ref[h] = gamma
        turned_ref[h] = turned
        beta = col_ref[:, heads + h : heads + h + 1]
        beta_row = lane_ref[heads + h : heads + h + 1, :]
        strong_ref[h] = jnp.where(rows > cols, beta * gamma, 0.0)
        strong_t_ref[h] = jnp.where(rows < cols, beta_row * turned, 0.0)


def weigh(lanes, cols, heads):
    size = lanes.shape[1]
    shape = jax.ShapeDtypeStruct((heads, size, size), F32)
    return pl.pallas_call(
        functools.partial(weigh_kernel, heads),
        in_specs=[here()] * 2,
        out_specs=[here()] * 4,
        out_shape=[shape] * 4,
        compiler_params=limit(8),
        name="weigh",
    )(lanes, cols)


def pair_kernel(levels, keep_ref, recv_ref, *pay_refs):
    place = lax.axis_index("seq")
    first = lax.rem(place, 2) == 0
    chip = place // 2

    def join(early, late):
        width = early.shape[-1]
        for h in range(keep_ref.shape[0]):
            ahead = nn(late[h, 0], jnp.concatenate([early[h, 1], early[h, 0]], axis=1))
            up = ahead[:, :width] + late[h, 1].astype(F32)
            down = nn(late[h, 2], early[h, 0]) + early[h, 2].astype(F32)
            joint = ahead[:, width:].astype(BF16)
            for level in range(levels):
                upward = lax.rem(chip // (1 << level), 2) == 0
                pay_refs[level][h, 0] = joint
                pay_refs[level][h, 1] = jnp.where(upward, up, down).astype(BF16)

    @pl.when(first)
    def _():
        join(keep_ref, recv_ref)

    @pl.when(jnp.logical_not(first))
    def _():
        join(recv_ref, keep_ref)


def join_pair(keep, recv, levels):
    half, _, width, _ = keep.shape
    shape = jax.ShapeDtypeStruct((half, 2, width, width), BF16)
    return pl.pallas_call(
        functools.partial(pair_kernel, levels),
        in_specs=[here()] * 2,
        out_specs=[here()] * levels,
        out_shape=[shape] * levels,
        compiler_params=limit(8),
        name="join_pair",
    )(keep, recv)


def two_terms(value):
    high = value.astype(BF16)
    return high, (value - high.astype(F32)).astype(BF16)


def scan_kernel(keep_ref, recv_ref, near_ref, far_ref, cross_ref, own_ref, send_ref, enter, leave):
    place = lax.axis_index("seq")
    first = lax.rem(place, 2) == 0
    chip = place // 2
    low = lax.rem(chip, 2) == 1
    high = chip // 2 == 1
    every = range(keep_ref.shape[0])

    def pairs(one, two):
        for h in every:

            @pl.when(high)
            def _():
                enter[h] = nn(two[h, 0], one[h, 1]) + two[h, 1].astype(F32)
                leave[h] = jnp.zeros_like(leave[h])

            @pl.when(jnp.logical_not(high))
            def _():
                leave[h] = nn(two[h, 1], one[h, 0]) + one[h, 1].astype(F32)
                enter[h] = jnp.zeros_like(enter[h])

    @pl.when(low)
    def _():
        pairs(cross_ref, far_ref)
        for h in every:
            top, rest = two_terms(enter[h])
            enter[h] = nn(near_ref[h, 0], top) + nn(near_ref[h, 0], rest) + near_ref[h, 1].astype(F32)

    @pl.when(jnp.logical_not(low))
    def _():
        pairs(far_ref, cross_ref)
        for h in every:
            top, rest = two_terms(leave[h])
            leave[h] = nn(top, near_ref[h, 0]) + nn(rest, near_ref[h, 0]) + near_ref[h, 1].astype(F32)

    def within(early, late, early_out, late_out):
        for h in every:
            top, rest = two_terms(enter[h])
            back, tail = two_terms(leave[h])
            middle = nn(early[h, 0], top) + nn(early[h, 0], rest) + early[h, 1].astype(F32)
            inner = nn(back, late[h, 0]) + nn(tail, late[h, 0]) + late[h, 2].astype(F32)
            early_out[h, 0] = top
            early_out[h, 1] = inner.astype(BF16)
            late_out[h, 0] = middle.astype(BF16)
            late_out[h, 1] = back

    @pl.when(first)
    def _():
        within(keep_ref, recv_ref, own_ref, send_ref)

    @pl.when(jnp.logical_not(first))
    def _():
        within(recv_ref, keep_ref, send_ref, own_ref)


def scan_chips(keep, recv, near, far, cross):
    half, _, width, _ = keep.shape
    shape = jax.ShapeDtypeStruct((half, 2, width, width), BF16)
    return pl.pallas_call(
        scan_kernel,
        in_specs=[here()] * 5,
        out_specs=[here()] * 2,
        out_shape=[shape] * 2,
        scratch_shapes=[pltpu.VMEM((half, width, width), F32)] * 2,
        compiler_params=limit(8),
        name="scan_chips",
    )(keep, recv, near, far, cross)


def part_at(slot, count):
    place = lax.axis_index("head")
    if count != 4:
        return lax.rem(place + slot + 1, count)
    if slot == 0:
        return 3 - place
    if slot == 3:
        return place
    low, high = ((2, 0), (3, 1)) if slot == 1 else ((1, 3), (0, 2))
    ends = jnp.where(place == 0, low[0], low[1])
    return jnp.where(place < 2, ends, jnp.where(place == 2, high[0], high[1]))


def early_parts():
    return 1


def grads_kernel(
    half, count, w_ref, unit_ref, scale_ref, col_ref, u_ref, wk_ref, dbt_ref, ktt_ref, gt_ref, og_ref,
    gamma_ref, turned_ref, strong_ref, strong_t_ref, own_ref, recv_ref,
    grad_ref, *rest,
):
    heads, size, width = u_ref.shape
    outs, edge_scr = rest[:-1], rest[-1]
    if half:
        core = lax.rem(lax.axis_index("seq"), 2)
        edge_scr[pl.ds(core * half, half)] = own_ref[...]
        edge_scr[pl.ds((1 - core) * half, half)] = recv_ref[...]
    else:
        edge_scr[...] = own_ref[...]
    every = range(heads)
    spans = [slice(h * width, (h + 1) * width) for h in every]
    run_col = [col_ref[:, h : h + 1] for h in every]
    beta = [col_ref[:, heads + h : heads + h + 1] for h in every]
    open_col = [jnp.exp(run_col[h]) for h in every]
    fade_col = [jnp.exp(run_col[h][size - 1 : size, :] - run_col[h]) for h in every]
    update = [(u_ref[h] - nn(wk_ref[h], edge_scr[h, 0])).astype(BF16) for h in every]
    delta_t = [dbt_ref[h] + nn(edge_scr[h, 1], ktt_ref[h]) for h in every]
    delta = [d.T for d in delta_t]
    totals = [None] * len(outs)
    group = 2 if heads % 2 == 0 else 1
    for h in every:
        span = spans[h]
        rows = jnp.concatenate([og_ref[:, span], delta[h].astype(BF16)], axis=0)
        lanes = nt(rows, update[h])
        turned = nn(update[h], jnp.concatenate([gt_ref[h], delta_t[h].astype(BF16)], axis=1))
        attend = (gamma_ref[h] * lanes[:size]).astype(BF16)
        attend_t = (turned_ref[h] * turned[:, :size]).astype(BF16)
        mix = (strong_ref[h] * lanes[size:] + strong_t_ref[h] * turned[:, size:]).astype(BF16)
        edge = nt(rows, edge_scr[h, 0])
        query = unit_ref[0, :, span]
        key = unit_ref[1, :, span]
        key_b = key.astype(BF16)
        dq = open_col[h] * edge[:size] + nn(attend, key_b)
        dk = (
            nn(attend_t, query.astype(BF16))
            - nn(mix, key_b)
            + fade_col[h] * nn(update[h], edge_scr[h, 1])
            - beta[h] * open_col[h] * edge[size:]
        )
        for slot, unit, slope in ((0, query, dq), (1, key, dk)):
            scale = scale_ref[:, slot * heads + h : slot * heads + h + 1]
            along = jnp.sum(unit * slope, axis=-1, keepdims=True)
            grad_ref[slot, :, span] = (scale * (slope - unit * along)).astype(BF16)
        grad_ref[2, :, span] = (beta[h] * delta[h]).astype(BF16)
        if h % group == group - 1:
            ready = slice((h - group + 1) * width, (h + 1) * width)
            for slot in range(len(outs)):
                part = spread_grads(grad_ref, w_ref, slot, count, ready)
                totals[slot] = part if h < group else totals[slot] + part
    for out_ref, total in zip(outs, totals):
        out_ref[...] = total.astype(out_ref.dtype)


def spread_grads(grad_ref, w_ref, slot, count, span=slice(None)):
    step = w_ref.shape[1] // count
    rows = pl.ds(pl.multiple_of(part_at(slot, count) * step, step), step)
    total = nt(grad_ref[0, :, span], w_ref[0, rows, span])
    for member in range(1, grad_ref.shape[0]):
        total = total + nt(grad_ref[member, :, span], w_ref[member, rows, span])
    return total


def grads(weights, prepared, out_grad, weighed, own, recv, half):
    unit, scale, col, u, wk, dbt, ktt, gt = prepared
    heads, size, width = u.shape
    members, depth, columns = weights.shape
    count = lax.axis_size("head")
    step = depth // count
    early = early_parts()
    return pl.pallas_call(
        functools.partial(grads_kernel, half, count),
        in_specs=[here()] * 16,
        out_specs=[here()] * (1 + early),
        out_shape=[jax.ShapeDtypeStruct((members, size, columns), BF16)]
        + [jax.ShapeDtypeStruct((size, step), BF16)] * early,
        scratch_shapes=[
            pltpu.VMEM((heads, 2, width, width), BF16),
        ],
        compiler_params=limit(12),
        name="grads",
    )(weights, unit, scale, col, u, wk, dbt, ktt, gt, out_grad, *weighed, own, recv)


def others_kernel(count, w_ref, grad_ref, *outs):
    for i, out_ref in enumerate(outs):
        out_ref[...] = spread_grads(grad_ref, w_ref, i + early_parts(), count).astype(out_ref.dtype)


def others(weights, grad):
    _, depth, _ = weights.shape
    size = grad.shape[1]
    count = lax.axis_size("head")
    step = depth // count
    kinds = [BF16] + [F32] * 2 if count == 4 else [BF16] * (count - 2) + [F32]
    return pl.pallas_call(
        functools.partial(others_kernel, count),
        in_specs=[here()] * 2,
        out_specs=[here()] * len(kinds),
        out_shape=[jax.ShapeDtypeStruct((size, step), k) for k in kinds],
        compiler_params=limit(8),
        name="others",
    )(weights, grad)


def swap(value, axis, count, mask):
    return lax.ppermute(value, axis, [(i, i ^ mask) for i in range(count)])


def edges_by_pairs(keep, send, count):
    recv = swap(send, "seq", count, 1)
    low, high = join_pair(keep, recv, 2)
    far = swap(high, "seq", count, 4)
    cross = swap(high, "seq", count, 6)
    near = swap(low, "seq", count, 2)
    own, other = scan_chips(keep, recv, near, far, cross)
    return own, swap(other, "seq", count, 1)


def edges_by_gather(keep, count):
    place = lax.axis_index("seq")
    gathered = lax.all_gather(keep, "seq")
    product = functools.partial(jnp.einsum, "hij,hjk->hik", precision=HIGH)

    def take(j):
        return lax.dynamic_index_in_dim(gathered, j, 0, False).astype(F32)

    def forward(j, state):
        part = take(j)
        return product(part[:, 0], state) + part[:, 1]

    def backward(i, state):
        part = take(count - 1 - i)
        return product(state, part[:, 0]) + part[:, 2]

    vacant = jnp.zeros(keep.shape[:1] + keep.shape[2:], F32)
    enter = lax.fori_loop(0, place, forward, vacant)
    leave = lax.fori_loop(0, count - 1 - place, backward, vacant)
    own = jnp.stack([enter, leave], axis=1).astype(BF16)
    return own, own


def sum_on_line(blocks):
    count = lax.axis_size("head")
    right = left = None
    for turn in range(count - 1):
        onward = blocks[count - 1 - turn]
        back = blocks[turn + 1]
        if turn:
            onward = (onward.astype(F32) + right.astype(F32)).astype(BF16)
            back = (back.astype(F32) + left.astype(F32)).astype(BF16)
        right = lax.ppermute(onward, "head", [(i, i + 1) for i in range(turn + 1)])
        left = lax.ppermute(back, "head", [(count - 1 - i, count - 2 - i) for i in range(turn + 1)])
    total = blocks[0]
    if count > 1:
        total = total + right.astype(F32) + left.astype(F32)
    return total.astype(BF16)


def join_kernel(joint_ref, outer_ref, out_ref):
    place = lax.axis_index("head")
    inside = jnp.logical_or(place == 1, place == 2)

    @pl.when(inside)
    def _():
        out_ref[...] = (joint_ref[...] + outer_ref[...].astype(F32)).astype(BF16)

    @pl.when(jnp.logical_not(inside))
    def _():
        out_ref[...] = joint_ref[...].astype(BF16)


def join_outer(joint, outer):
    return pl.pallas_call(
        join_kernel,
        in_specs=[here()] * 2,
        out_specs=here(),
        out_shape=jax.ShapeDtypeStruct(joint.shape, BF16),
        compiler_params=limit(8),
        name="join_outer",
    )(joint, outer)


def sum_of_four(end, first, joint, own):
    outer = lax.ppermute(end, "head", [(0, 1), (1, 0), (2, 3), (3, 2)])
    inner = lax.ppermute(end, "head", [(1, 2), (2, 1)])
    joint = join_outer(joint, outer)
    joint = lax.ppermute(joint, "head", [(0, 1), (1, 3), (3, 2), (2, 0)])
    ring = lax.ppermute(first, "head", [(0, 2), (2, 3), (3, 1), (1, 0)])
    total = own + inner.astype(F32) + ring.astype(F32) + joint.astype(F32)
    return total.astype(BF16)


def step_on_device(tokens, qkv_weight, beta_logit, log_decay, out_grad):
    heads = beta_logit.shape[0]
    count = lax.axis_size("seq")
    paired = heads % 2 == 0 and count == 8
    half = heads // 2 if paired else 0
    held, kept_grad, unit, scale, lanes, col, u, wk, dbt, ktt, gt, keep, send = prepare(
        tokens, qkv_weight, beta_logit, log_decay, out_grad, half
    )
    if paired:
        own, recv = edges_by_pairs(keep, send, count)
    else:
        own, recv = edges_by_gather(keep, count)
    weighed = weigh(lanes, col, heads)
    prepared = (unit, scale, col, u, wk, dbt, ktt, gt)
    grad, *early = grads(held, prepared, kept_grad, weighed, own, recv, half)
    rest = others(held, grad)
    if lax.axis_size("head") == 4:
        return sum_of_four(*early, *rest)
    return sum_on_line([rest[-1], *early, *rest[:-1]])


def solution(mesh):
    return jax.shard_map(
        step_on_device,
        mesh=mesh,
        in_specs=(
            P("seq", None),
            P(None, None, "head"),
            P("head", "seq"),
            P("head", "seq"),
            P("seq", "head"),
        ),
        out_specs=P("seq", "head"),
        check_vma=False,
    )
```

```python
import functools

import jax
import jax.numpy as jnp
from jax import lax
from jax.experimental import pallas as pl
from jax.experimental.pallas import tpu as pltpu
from jax.sharding import PartitionSpec as P


F32 = jnp.float32
BF16 = jnp.bfloat16
HIGH = lax.Precision.HIGHEST
FAR = -1e30


def nn(a, b):
    return lax.dot_general(a, b, (((1,), (0,)), ((), ())), preferred_element_type=F32)


def nt(a, b):
    return lax.dot_general(a, b, (((1,), (1,)), ((), ())), preferred_element_type=F32)


def grid_ids(size):
    rows = lax.broadcasted_iota(jnp.int32, (size, size), 0)
    cols = lax.broadcasted_iota(jnp.int32, (size, size), 1)
    return rows, cols


def exact_terms(value):
    high = value.astype(BF16)
    left = value - high.astype(F32)
    mid = left.astype(BF16)
    return high, mid, (left - mid.astype(F32)).astype(BF16)


def gates(logit, decay):
    heads, size = decay.shape
    rows, cols = grid_ids(size)
    upper = jnp.where(rows <= cols, 1.0, 0.0).astype(BF16)
    high, mid, low = exact_terms(decay)
    run = nn(jnp.concatenate([high, mid, low], axis=0), upper)
    run = run[:heads] + run[heads : 2 * heads] + run[2 * heads :]
    lanes = [run, 1.0 / (1.0 + jnp.exp(-logit))]
    spare = -2 * heads % 8
    if spare:
        lanes.append(jnp.zeros((spare, size), F32))
    lanes = jnp.concatenate(lanes, axis=0)
    return lanes, lanes.T


def two_terms(value):
    high = value.astype(BF16)
    return high, (value - high.astype(F32)).astype(BF16)


def unit_rows(tensor):
    scale = lax.rsqrt(jnp.sum(tensor * tensor, axis=-1, keepdims=True) + 1e-06)
    scale = jnp.broadcast_to(scale, tensor.shape)
    return tensor * scale, scale


def unit_lower_inverse(couplings, fill):
    size = couplings[0].shape[0]
    base = size // 4
    lane_block = lax.broadcasted_iota(jnp.int32, (base, size), 1) // base
    on = [lane_block == b for b in range(4)]
    odd = lane_block % 2 == 1
    masks = [jnp.where(o, 1.0, 0.0).astype(BF16) for o in on]
    none = jnp.zeros((base, size), BF16)

    def strip(a, b):
        return a[b * base : (b + 1) * base]

    def spread(x):
        return jnp.concatenate([x * m for m in masks], axis=0)

    flat = [sum(jnp.where(on[b], strip(a, b), 0.0) for b in range(4)) for a in couplings]
    rest = [-x for x in flat]
    power = flat
    reach = 1
    while 2 * reach < base:
        narrow = [p.astype(BF16) for p in power]
        if reach == 1:
            power = [nn(p, spread(p)) for p in narrow]
            fill()
        else:
            both = [
                nn(jnp.concatenate([n.astype(BF16), p], axis=0), spread(p))
                for n, p in zip(rest, narrow)
            ]
            rest = [n + p + x[:base] for n, p, x in zip(rest, power, both)]
            power = [x[base:] for x in both]
            fill()
        reach *= 2
    if reach > 1:
        narrow = [p.astype(BF16) for p in power]
        rest = [n + p + nn(n.astype(BF16), spread(b)) for n, p, b in zip(rest, power, narrow)]
        fill()

    outer = [jnp.where(on[0], strip(a, 1), 0.0) + jnp.where(on[2], strip(a, 3), 0.0) for a in couplings]
    wide = [n.astype(BF16) for n in rest]
    half = [g + nn(g.astype(BF16), spread(n)) for g, n in zip(outer, wide)]
    half_b = [y.astype(BF16) for y in half]
    fill()
    late = [jnp.where(odd, n, 0.0) for n in rest]
    cross = [
        y + nn(l.astype(BF16), jnp.concatenate([none, b * masks[0], none, b * masks[2]], axis=0))
        for y, l, b in zip(half, late, half_b)
    ]
    fill()
    below = [l - z for l, z in zip(late, cross)]
    above = [jnp.where(odd, 0.0, n) for n in rest]
    mid = size // 2
    early = [jnp.concatenate([t[:, :mid], b[:, :mid]], axis=0).astype(BF16) for t, b in zip(above, below)]
    later = [jnp.concatenate([t[:, mid:], b[:, mid:]], axis=0).astype(BF16) for t, b in zip(above, below)]
    corner = [a[mid:, :mid] for a in couplings]
    half = [c + nn(c.astype(BF16), e) for c, e in zip(corner, early)]
    fill()
    cross = [y + nn(l, y.astype(BF16)) for y, l in zip(half, later)]
    blank = jnp.zeros((mid, mid), BF16)
    return [
        jnp.concatenate(
            [
                jnp.concatenate([e, blank], axis=1),
                jnp.concatenate([(-z).astype(BF16), l], axis=1),
            ],
            axis=0,
        )
        for e, z, l in zip(early, cross, later)
    ]


def prepare_kernel(
    half, pieces, tok_hbm, w_hbm, logit_hbm, decay_hbm, og_hbm,
    w_ref, og_ref, unit_ref, scale_ref, lane_ref, col_ref, u_ref, wk_ref, dbt_ref, ktt_ref, gt_ref,
    keep_ref, send_ref,
    tok_scr, logit_ref, decay_ref, value_scr, pay_scr, gamma_scr, pair_scr, tok_sem, w_sem, more_sem,
):
    heads, size = decay_ref.shape
    members, depth, columns = w_ref.shape
    width = columns // heads
    chunk = depth // pieces

    def part(i):
        return pl.ds(i * chunk, chunk)

    tok_copies = [
        pltpu.make_async_copy(tok_hbm.at[:, part(i)], tok_scr.at[:, part(i)], tok_sem.at[i])
        for i in range(pieces)
    ]
    w_copies = [
        [
            pltpu.make_async_copy(w_hbm.at[p, part(i)], w_ref.at[p, part(i)], w_sem.at[p, i])
            for i in range(pieces)
        ]
        for p in range(members)
    ]
    small = [(logit_hbm, logit_ref), (decay_hbm, decay_ref), (og_hbm, og_ref)]
    small = [pltpu.make_async_copy(a, b, more_sem.at[i]) for i, (a, b) in enumerate(small)]
    for copy in small[:2]:
        copy.start()
    for i in range(pieces):
        tok_copies[i].start()
        w_copies[1][i].start()
    small[2].start()

    def product(p, i):
        span = slice(i * chunk, (i + 1) * chunk)
        return nn(tok_scr[:, span], w_ref[p, span])

    every = range(heads)
    spans = [slice(h * width, (h + 1) * width) for h in every]
    for copy in small[:2]:
        copy.wait()
    lanes, cols_of = gates(logit_ref[...], decay_ref[...])
    lane_ref[...] = lanes
    col_ref[...] = cols_of
    rows, cols = grid_ids(size)
    causal = rows >= cols
    strict = rows > cols
    run_col = [cols_of[:, h : h + 1] for h in every]
    run_row = [lanes[h : h + 1, :] for h in every]
    beta = [cols_of[:, heads + h : heads + h + 1] for h in every]

    total = None
    for i in range(pieces):
        tok_copies[i].wait()
        w_copies[1][i].wait()
        if i == 0:
            for p in (2, 0):
                for copy in w_copies[p]:
                    copy.start()
        result = product(1, i)
        total = result if total is None else total + result

    def normalize(p, total):
        for h in every:
            unit, scale = unit_rows(total[:, spans[h]])
            unit_ref[p, :, spans[h]] = unit
            scale_ref[p, :, spans[h]] = scale

    small[2].wait()
    for h in every:
        gt_ref[h] = og_ref[:, spans[h]].astype(F32).T.astype(BF16)
    normalize(1, total)
    keys = [unit_ref[1, :, s] for s in spans]
    key_b = [k.astype(BF16) for k in keys]
    for h in every:
        gamma = jnp.exp(jnp.where(causal, run_col[h] - run_row[h], FAR))
        gamma_scr[h] = gamma
        pair_scr[h] = jnp.where(strict, beta[h] * gamma * nt(key_b[h], key_b[h]), 0.0)
    for i in range(pieces):
        w_copies[2][i].wait()
    waiting = [(p, i) for p in (2, 0) for i in range(pieces)]
    totals = {2: None, 0: None}

    def fill():
        if waiting:
            p, i = waiting.pop(0)
            if p == 0 and i == 0:
                for copy in w_copies[0]:
                    copy.wait()
            result = product(p, i)
            totals[p] = result if totals[p] is None else totals[p] + result

    inverse = unit_lower_inverse([pair_scr[h] for h in every], fill)
    while waiting:
        fill()
    value_scr[...] = totals[2]
    normalize(0, totals[0])
    queries = [unit_ref[0, :, s] for s in spans]
    scores = [(gamma_scr[h] * nt(queries[h].astype(BF16), key_b[h])).astype(BF16) for h in every]
    last = [run_col[h][size - 1 : size, :] for h in every]
    open_col = [jnp.exp(run_col[h]) for h in every]
    fade_row = [jnp.exp(last[h] - run_row[h]) for h in every]
    write_key = [beta[h] * open_col[h] * keys[h] for h in every]
    right = [
        jnp.concatenate([beta[h] * value_scr[:, spans[h]], write_key[h]], axis=1) for h in every
    ]
    solved = [right[h] + nn(inverse[h], right[h].astype(BF16)) for h in every]
    fade_t = [keys[h].T * fade_row[h] for h in every]
    left = [jnp.concatenate([nn(gt_ref[h], scores[h]), fade_t[h]], axis=0) for h in every]
    back = [left[h] + nn(left[h].astype(BF16), inverse[h]) for h in every]
    e_rows, e_cols = grid_ids(width)
    for h in every:
        fade_hi = fade_t[h].astype(BF16)
        fade_lo = (fade_t[h] - fade_hi.astype(F32)).astype(BF16)
        solved_hi = solved[h].astype(BF16)
        solved_lo = (solved[h][:, :width] - solved_hi[:, :width].astype(F32)).astype(BF16)
        state = nn(fade_hi, solved_hi)
        fill = state[:, :width] + nn(fade_lo, solved_hi[:, :width]) + nn(fade_hi, solved_lo)
        unit = jnp.where(e_rows == e_cols, jnp.exp(last[h]), 0.0)
        seed = nn(gt_ref[h], (open_col[h] * queries[h]).astype(BF16)) - nn(
            back[h][:width].astype(BF16), write_key[h].astype(BF16)
        )
        pay_scr[h, 0] = (unit - state[:, width:]).astype(BF16)
        pay_scr[h, 1] = fill.astype(BF16)
        pay_scr[h, 2] = seed.astype(BF16)
        u_ref[h] = solved[h][:, :width]
        wk_ref[h] = solved_hi[:, width:]
        dbt_ref[h] = back[h][:width]
        ktt_ref[h] = back[h][width:].astype(BF16)
    if half:
        core = lax.rem(lax.axis_index("seq"), 2)
        keep_ref[...] = pay_scr[pl.ds(core * half, half)]
        send_ref[...] = pay_scr[pl.ds((1 - core) * half, half)]
    else:
        keep_ref[...] = pay_scr[...]
        send_ref[...] = pay_scr[...]


def here():
    return pl.BlockSpec(memory_space=pltpu.VMEM)


def away():
    return pl.BlockSpec(memory_space=pltpu.HBM)


def limit(mebibytes):
    return pltpu.CompilerParams(vmem_limit_bytes=mebibytes * 2**20)


def prepare(tokens, weights, logit, decay, out_grad, half):
    heads, size = logit.shape
    members, depth, columns = weights.shape
    width = columns // heads
    part = half or heads
    pieces = 4 if depth % 512 == 0 else 1
    gate_rows = 2 * heads + -2 * heads % 8
    shapes = [
        ((members, depth, columns), BF16),
        ((size, columns), BF16),
        ((2, size, columns), F32),
        ((2, size, columns), F32),
        ((gate_rows, size), F32),
        ((size, gate_rows), F32),
        ((heads, size, width), F32),
        ((heads, size, width), BF16),
        ((heads, width, size), F32),
        ((heads, width, size), BF16),
        ((heads, width, size), BF16),
        ((part, 3, width, width), BF16),
        ((part, 3, width, width), BF16),
    ]
    return pl.pallas_call(
        functools.partial(prepare_kernel, half, pieces),
        in_specs=[away()] * 5,
        out_specs=[here()] * len(shapes),
        out_shape=[jax.ShapeDtypeStruct(*s) for s in shapes],
        scratch_shapes=[
            pltpu.VMEM((size, depth), BF16),
            pltpu.VMEM((heads, size), F32),
            pltpu.VMEM((heads, size), F32),
            pltpu.VMEM((size, columns), F32),
            pltpu.VMEM((heads, 3, width, width), BF16),
            pltpu.VMEM((heads, size, size), F32),
            pltpu.VMEM((heads, size, size), F32),
            pltpu.SemaphoreType.DMA((pieces,)),
            pltpu.SemaphoreType.DMA((members, pieces)),
            pltpu.SemaphoreType.DMA((3,)),
        ],
        compiler_params=limit(16),
        name="prepare",
    )(*(pltpu.with_memory_space_constraint(x, pltpu.HBM) for x in (tokens, weights, logit, decay, out_grad)))


def weigh_kernel(heads, lane_ref, col_ref, gamma_ref, turned_ref, strong_ref, strong_t_ref):
    size = lane_ref.shape[1]
    rows, cols = grid_ids(size)
    for h in range(heads):
        gap = col_ref[:, h : h + 1] - lane_ref[h : h + 1, :]
        gamma = jnp.exp(jnp.where(rows >= cols, gap, FAR))
        turned = jnp.exp(jnp.where(rows <= cols, -gap, FAR))
        gamma_ref[h] = gamma
        turned_ref[h] = turned
        beta = col_ref[:, heads + h : heads + h + 1]
        beta_row = lane_ref[heads + h : heads + h + 1, :]
        strong_ref[h] = jnp.where(rows > cols, beta * gamma, 0.0)
        strong_t_ref[h] = jnp.where(rows < cols, beta_row * turned, 0.0)


def weigh(lanes, cols, heads):
    size = lanes.shape[1]
    shape = jax.ShapeDtypeStruct((heads, size, size), F32)
    return pl.pallas_call(
        functools.partial(weigh_kernel, heads),
        in_specs=[here()] * 2,
        out_specs=[here()] * 4,
        out_shape=[shape] * 4,
        compiler_params=limit(8),
        name="weigh",
    )(lanes, cols)


def pair_kernel(levels, keep_ref, recv_ref, *pay_refs):
    place = lax.axis_index("seq")
    first = lax.rem(place, 2) == 0
    chip = place // 2

    def join(early, late):
        width = early.shape[-1]
        for h in range(keep_ref.shape[0]):
            ahead = nn(late[h, 0], jnp.concatenate([early[h, 1], early[h, 0]], axis=1))
            up = ahead[:, :width] + late[h, 1].astype(F32)
            down = nn(late[h, 2], early[h, 0]) + early[h, 2].astype(F32)
            joint = ahead[:, width:].astype(BF16)
            for level in range(levels):
                upward = lax.rem(chip // (1 << level), 2) == 0
                pay_refs[level][h, 0] = joint
                pay_refs[level][h, 1] = jnp.where(upward, up, down).astype(BF16)

    @pl.when(first)
    def _():
        join(keep_ref, recv_ref)

    @pl.when(jnp.logical_not(first))
    def _():
        join(recv_ref, keep_ref)


def join_pair(keep, recv, levels):
    half, _, width, _ = keep.shape
    shape = jax.ShapeDtypeStruct((half, 2, width, width), BF16)
    return pl.pallas_call(
        functools.partial(pair_kernel, levels),
        in_specs=[here()] * 2,
        out_specs=[here()] * levels,
        out_shape=[shape] * levels,
        compiler_params=limit(8),
        name="join_pair",
    )(keep, recv)


def scan_kernel(keep_ref, recv_ref, near_ref, far_ref, cross_ref, own_ref, send_ref, enter, leave):
    place = lax.axis_index("seq")
    first = lax.rem(place, 2) == 0
    chip = place // 2
    low = lax.rem(chip, 2) == 1
    high = chip // 2 == 1
    every = range(keep_ref.shape[0])

    def pairs(one, two):
        for h in every:

            @pl.when(high)
            def _():
                enter[h] = nn(two[h, 0], one[h, 1]) + two[h, 1].astype(F32)
                leave[h] = jnp.zeros_like(leave[h])

            @pl.when(jnp.logical_not(high))
            def _():
                leave[h] = nn(two[h, 1], one[h, 0]) + one[h, 1].astype(F32)
                enter[h] = jnp.zeros_like(enter[h])

    @pl.when(low)
    def _():
        pairs(cross_ref, far_ref)
        for h in every:
            top, rest = two_terms(enter[h])
            enter[h] = nn(near_ref[h, 0], top) + nn(near_ref[h, 0], rest) + near_ref[h, 1].astype(F32)

    @pl.when(jnp.logical_not(low))
    def _():
        pairs(far_ref, cross_ref)
        for h in every:
            top, rest = two_terms(leave[h])
            leave[h] = nn(top, near_ref[h, 0]) + nn(rest, near_ref[h, 0]) + near_ref[h, 1].astype(F32)

    def within(early, late, early_out, late_out):
        for h in every:
            top, rest = two_terms(enter[h])
            back, tail = two_terms(leave[h])
            middle = nn(early[h, 0], top) + nn(early[h, 0], rest) + early[h, 1].astype(F32)
            inner = nn(back, late[h, 0]) + nn(tail, late[h, 0]) + late[h, 2].astype(F32)
            early_out[h, 0] = top
            early_out[h, 1] = inner.astype(BF16)
            late_out[h, 0] = middle.astype(BF16)
            late_out[h, 1] = back

    @pl.when(first)
    def _():
        within(keep_ref, recv_ref, own_ref, send_ref)

    @pl.when(jnp.logical_not(first))
    def _():
        within(recv_ref, keep_ref, send_ref, own_ref)


def scan_chips(keep, recv, near, far, cross):
    half, _, width, _ = keep.shape
    shape = jax.ShapeDtypeStruct((half, 2, width, width), BF16)
    return pl.pallas_call(
        scan_kernel,
        in_specs=[here()] * 5,
        out_specs=[here()] * 2,
        out_shape=[shape] * 2,
        scratch_shapes=[pltpu.VMEM((half, width, width), F32)] * 2,
        compiler_params=limit(8),
        name="scan_chips",
    )(keep, recv, near, far, cross)


def part_at(slot, count):
    place = lax.axis_index("head")
    if count != 4:
        return lax.rem(place + slot + 1, count)
    if slot == 0:
        return 3 - place
    if slot == 3:
        return place
    low, high = ((2, 0), (3, 1)) if slot == 1 else ((1, 3), (0, 2))
    ends = jnp.where(place == 0, low[0], low[1])
    return jnp.where(place < 2, ends, jnp.where(place == 2, high[0], high[1]))


def early_parts():
    return 1


def grads_kernel(
    half, count, w_ref, unit_ref, scale_ref, col_ref, u_ref, wk_ref, dbt_ref, ktt_ref, gt_ref, og_ref,
    gamma_ref, turned_ref, strong_ref, strong_t_ref, own_ref, recv_ref,
    grad_ref, *rest,
):
    heads, size, width = u_ref.shape
    outs, edge_scr = rest[:-1], rest[-1]
    if half:
        core = lax.rem(lax.axis_index("seq"), 2)
        edge_scr[pl.ds(core * half, half)] = own_ref[...]
        edge_scr[pl.ds((1 - core) * half, half)] = recv_ref[...]
    else:
        edge_scr[...] = own_ref[...]
    every = range(heads)
    spans = [slice(h * width, (h + 1) * width) for h in every]
    run_col = [col_ref[:, h : h + 1] for h in every]
    beta = [col_ref[:, heads + h : heads + h + 1] for h in every]
    open_col = [jnp.exp(run_col[h]) for h in every]
    fade_col = [jnp.exp(run_col[h][size - 1 : size, :] - run_col[h]) for h in every]
    update = [(u_ref[h] - nn(wk_ref[h], edge_scr[h, 0])).astype(BF16) for h in every]
    delta_t = [dbt_ref[h] + nn(edge_scr[h, 1], ktt_ref[h]) for h in every]
    delta = [d.T for d in delta_t]
    ones = jnp.ones((width, width), BF16)
    slopes = {}

    def contract(h):
        span = spans[h]
        rows = jnp.concatenate([og_ref[:, span], delta[h].astype(BF16)], axis=0)
        lanes = nt(rows, update[h])
        turned = nn(update[h], jnp.concatenate([gt_ref[h], delta_t[h].astype(BF16)], axis=1))
        attend = (gamma_ref[h] * lanes[:size]).astype(BF16)
        attend_t = (turned_ref[h] * turned[:, :size]).astype(BF16)
        mix = (strong_ref[h] * lanes[size:] + strong_t_ref[h] * turned[:, size:]).astype(BF16)
        edge = nt(rows, edge_scr[h, 0])
        key_b = unit_ref[1, :, span].astype(BF16)
        inner = nn(jnp.concatenate([attend, mix], axis=0), key_b)
        dq = open_col[h] * edge[:size] + inner[:size]
        dk = (
            nn(attend_t, unit_ref[0, :, span].astype(BF16))
            - inner[size:]
            + fade_col[h] * nn(update[h], edge_scr[h, 1])
            - beta[h] * open_col[h] * edge[size:]
        )
        slopes[h] = (dq, dk)
        grad_ref[2, :, span] = (beta[h] * delta[h]).astype(BF16)

    def project_out(h):
        span = spans[h]
        for slot, slope in enumerate(slopes[h]):
            unit = unit_ref[slot, :, span]
            along = nn((unit * slope).astype(BF16), ones)
            grad_ref[slot, :, span] = (scale_ref[slot, :, span] * (slope - unit * along)).astype(BF16)

    totals = [None] * len(outs)

    def emit(group):
        ready = slice(group[0] * width, (group[-1] + 1) * width)
        for slot in range(len(outs)):
            part = spread_grads(grad_ref, w_ref, slot, count, ready)
            totals[slot] = part if totals[slot] is None else totals[slot] + part

    group = 2 if heads % 2 == 0 else 1
    groups = [list(range(g, g + group)) for g in range(0, heads, group)]
    for turn, members in enumerate(groups):
        for h in members:
            contract(h)
        if turn:
            emit(groups[turn - 1])
        for h in members:
            project_out(h)
    emit(groups[-1])
    for out_ref, total in zip(outs, totals):
        out_ref[...] = total.astype(out_ref.dtype)


def spread_grads(grad_ref, w_ref, slot, count, span=slice(None)):
    step = w_ref.shape[1] // count
    rows = pl.ds(pl.multiple_of(part_at(slot, count) * step, step), step)
    last = grad_ref.shape[0] - 1
    total = nt(grad_ref[last, :, span], w_ref[last, rows, span])
    for member in range(last):
        total = total + nt(grad_ref[member, :, span], w_ref[member, rows, span])
    return total


def grads(weights, prepared, out_grad, weighed, own, recv, half):
    unit, scale, col, u, wk, dbt, ktt, gt = prepared
    heads, size, width = u.shape
    members, depth, columns = weights.shape
    count = lax.axis_size("head")
    step = depth // count
    early = early_parts()
    return pl.pallas_call(
        functools.partial(grads_kernel, half, count),
        in_specs=[here()] * 16,
        out_specs=[here()] * (1 + early),
        out_shape=[jax.ShapeDtypeStruct((members, size, columns), BF16)]
        + [jax.ShapeDtypeStruct((size, step), BF16)] * early,
        scratch_shapes=[
            pltpu.VMEM((heads, 2, width, width), BF16),
        ],
        compiler_params=limit(12),
        name="grads",
    )(weights, unit, scale, col, u, wk, dbt, ktt, gt, out_grad, *weighed, own, recv)


def others_kernel(count, w_ref, grad_ref, *outs):
    for i, out_ref in enumerate(outs):
        out_ref[...] = spread_grads(grad_ref, w_ref, i + early_parts(), count).astype(out_ref.dtype)


def others(weights, grad):
    _, depth, _ = weights.shape
    size = grad.shape[1]
    count = lax.axis_size("head")
    step = depth // count
    kinds = [BF16] + [F32] * 2 if count == 4 else [BF16] * (count - 2) + [F32]
    return pl.pallas_call(
        functools.partial(others_kernel, count),
        in_specs=[here()] * 2,
        out_specs=[here()] * len(kinds),
        out_shape=[jax.ShapeDtypeStruct((size, step), k) for k in kinds],
        compiler_params=limit(8),
        name="others",
    )(weights, grad)


def swap(value, axis, count, mask):
    return lax.ppermute(value, axis, [(i, i ^ mask) for i in range(count)])


def edges_by_pairs(keep, send, count):
    recv = swap(send, "seq", count, 1)
    low, high = join_pair(keep, recv, 2)
    far = swap(high, "seq", count, 4)
    cross = swap(high, "seq", count, 6)
    near = swap(low, "seq", count, 2)
    own, other = scan_chips(keep, recv, near, far, cross)
    return own, swap(other, "seq", count, 1)


def edges_by_gather(keep, count):
    place = lax.axis_index("seq")
    gathered = lax.all_gather(keep, "seq")
    product = functools.partial(jnp.einsum, "hij,hjk->hik", precision=HIGH)

    def take(j):
        return lax.dynamic_index_in_dim(gathered, j, 0, False).astype(F32)

    def forward(j, state):
        part = take(j)
        return product(part[:, 0], state) + part[:, 1]

    def backward(i, state):
        part = take(count - 1 - i)
        return product(state, part[:, 0]) + part[:, 2]

    vacant = jnp.zeros(keep.shape[:1] + keep.shape[2:], F32)
    enter = lax.fori_loop(0, place, forward, vacant)
    leave = lax.fori_loop(0, count - 1 - place, backward, vacant)
    own = jnp.stack([enter, leave], axis=1).astype(BF16)
    return own, own


def sum_on_line(blocks):
    count = lax.axis_size("head")
    right = left = None
    for turn in range(count - 1):
        onward = blocks[count - 1 - turn]
        back = blocks[turn + 1]
        if turn:
            onward = (onward.astype(F32) + right.astype(F32)).astype(BF16)
            back = (back.astype(F32) + left.astype(F32)).astype(BF16)
        right = lax.ppermute(onward, "head", [(i, i + 1) for i in range(turn + 1)])
        left = lax.ppermute(back, "head", [(count - 1 - i, count - 2 - i) for i in range(turn + 1)])
    total = blocks[0]
    if count > 1:
        total = total + right.astype(F32) + left.astype(F32)
    return total.astype(BF16)


def join_kernel(joint_ref, outer_ref, out_ref):
    place = lax.axis_index("head")
    inside = jnp.logical_or(place == 1, place == 2)

    @pl.when(inside)
    def _():
        out_ref[...] = (joint_ref[...] + outer_ref[...].astype(F32)).astype(BF16)

    @pl.when(jnp.logical_not(inside))
    def _():
        out_ref[...] = joint_ref[...].astype(BF16)


def join_outer(joint, outer):
    return pl.pallas_call(
        join_kernel,
        in_specs=[here()] * 2,
        out_specs=here(),
        out_shape=jax.ShapeDtypeStruct(joint.shape, BF16),
        compiler_params=limit(8),
        name="join_outer",
    )(joint, outer)


def sum_of_four(end, first, joint, own):
    outer = lax.ppermute(end, "head", [(0, 1), (1, 0), (2, 3), (3, 2)])
    inner = lax.ppermute(end, "head", [(1, 2), (2, 1)])
    joint = join_outer(joint, outer)
    joint = lax.ppermute(joint, "head", [(0, 1), (1, 3), (3, 2), (2, 0)])
    ring = lax.ppermute(first, "head", [(0, 2), (2, 3), (3, 1), (1, 0)])
    total = own + inner.astype(F32) + ring.astype(F32) + joint.astype(F32)
    return total.astype(BF16)


def step_on_device(tokens, qkv_weight, beta_logit, log_decay, out_grad):
    heads = beta_logit.shape[0]
    count = lax.axis_size("seq")
    paired = heads % 2 == 0 and count == 8
    half = heads // 2 if paired else 0
    held, kept_grad, unit, scale, lanes, col, u, wk, dbt, ktt, gt, keep, send = prepare(
        tokens, qkv_weight, beta_logit, log_decay, out_grad, half
    )
    if paired:
        own, recv = edges_by_pairs(keep, send, count)
    else:
        own, recv = edges_by_gather(keep, count)
    weighed = weigh(lanes, col, heads)
    prepared = (unit, scale, col, u, wk, dbt, ktt, gt)
    grad, *early = grads(held, prepared, kept_grad, weighed, own, recv, half)
    rest = others(held, grad)
    if lax.axis_size("head") == 4:
        return sum_of_four(*early, *rest)
    return sum_on_line([rest[-1], *early, *rest[:-1]])


def solution(mesh):
    return jax.shard_map(
        step_on_device,
        mesh=mesh,
        in_specs=(
            P("seq", None),
            P(None, None, "head"),
            P("head", "seq"),
            P("head", "seq"),
            P("seq", "head"),
        ),
        out_specs=P("seq", "head"),
        check_vma=False,
    )
```

```python
import functools

import jax
import jax.numpy as jnp
from jax import lax
from jax.experimental import pallas as pl
from jax.experimental.pallas import tpu as pltpu
from jax.sharding import PartitionSpec as P


F32 = jnp.float32
BF16 = jnp.bfloat16
HIGH = lax.Precision.HIGHEST
FAR = -1e30


def nn(a, b):
    return lax.dot_general(a, b, (((1,), (0,)), ((), ())), preferred_element_type=F32)


def nt(a, b):
    return lax.dot_general(a, b, (((1,), (1,)), ((), ())), preferred_element_type=F32)


def grid_ids(size):
    rows = lax.broadcasted_iota(jnp.int32, (size, size), 0)
    cols = lax.broadcasted_iota(jnp.int32, (size, size), 1)
    return rows, cols


def exact_terms(value):
    high = value.astype(BF16)
    left = value - high.astype(F32)
    mid = left.astype(BF16)
    return high, mid, (left - mid.astype(F32)).astype(BF16)


def gates(logit, decay):
    heads, size = decay.shape
    rows, cols = grid_ids(size)
    upper = jnp.where(rows <= cols, 1.0, 0.0).astype(BF16)
    high, mid, low = exact_terms(decay)
    run = nn(jnp.concatenate([high, mid, low], axis=0), upper)
    run = run[:heads] + run[heads : 2 * heads] + run[2 * heads :]
    lanes = [run, 1.0 / (1.0 + jnp.exp(-logit))]
    spare = -2 * heads % 8
    if spare:
        lanes.append(jnp.zeros((spare, size), F32))
    lanes = jnp.concatenate(lanes, axis=0)
    return lanes, lanes.T


def two_terms(value):
    high = value.astype(BF16)
    return high, (value - high.astype(F32)).astype(BF16)


def unit_rows(tensor):
    scale = lax.rsqrt(jnp.sum(tensor * tensor, axis=-1, keepdims=True) + 1e-06)
    scale = jnp.broadcast_to(scale, tensor.shape)
    return tensor * scale, scale


def unit_lower_inverse(couplings, fill):
    size = couplings[0].shape[0]
    base = size // 4
    lane_block = lax.broadcasted_iota(jnp.int32, (base, size), 1) // base
    on = [lane_block == b for b in range(4)]
    odd = lane_block % 2 == 1
    masks = [jnp.where(o, 1.0, 0.0).astype(BF16) for o in on]
    none = jnp.zeros((base, size), BF16)

    def strip(a, b):
        return a[b * base : (b + 1) * base]

    def spread(x):
        return jnp.concatenate([x * m for m in masks], axis=0)

    flat = [sum(jnp.where(on[b], strip(a, b), 0.0) for b in range(4)) for a in couplings]
    rest = [-x for x in flat]
    power = flat
    reach = 1
    while 2 * reach < base:
        narrow = [p.astype(BF16) for p in power]
        if reach == 1:
            power = [nn(p, spread(p)) for p in narrow]
            fill()
        else:
            both = [
                nn(jnp.concatenate([n.astype(BF16), p], axis=0), spread(p))
                for n, p in zip(rest, narrow)
            ]
            rest = [n + p + x[:base] for n, p, x in zip(rest, power, both)]
            power = [x[base:] for x in both]
            fill()
        reach *= 2
    if reach > 1:
        narrow = [p.astype(BF16) for p in power]
        rest = [n + p + nn(n.astype(BF16), spread(b)) for n, p, b in zip(rest, power, narrow)]
        fill()

    outer = [jnp.where(on[0], strip(a, 1), 0.0) + jnp.where(on[2], strip(a, 3), 0.0) for a in couplings]
    wide = [n.astype(BF16) for n in rest]
    half = [g + nn(g.astype(BF16), spread(n)) for g, n in zip(outer, wide)]
    half_b = [y.astype(BF16) for y in half]
    fill()
    late = [jnp.where(odd, n, 0.0) for n in rest]
    cross = [
        y + nn(l.astype(BF16), jnp.concatenate([none, b * masks[0], none, b * masks[2]], axis=0))
        for y, l, b in zip(half, late, half_b)
    ]
    fill()
    below = [l - z for l, z in zip(late, cross)]
    above = [jnp.where(odd, 0.0, n) for n in rest]
    mid = size // 2
    early = [jnp.concatenate([t[:, :mid], b[:, :mid]], axis=0).astype(BF16) for t, b in zip(above, below)]
    later = [jnp.concatenate([t[:, mid:], b[:, mid:]], axis=0).astype(BF16) for t, b in zip(above, below)]
    corner = [a[mid:, :mid] for a in couplings]
    half = [c + nn(c.astype(BF16), e) for c, e in zip(corner, early)]
    fill()
    cross = [y + nn(l, y.astype(BF16)) for y, l in zip(half, later)]
    blank = jnp.zeros((mid, mid), BF16)
    return [
        jnp.concatenate(
            [
                jnp.concatenate([e, blank], axis=1),
                jnp.concatenate([(-z).astype(BF16), l], axis=1),
            ],
            axis=0,
        )
        for e, z, l in zip(early, cross, later)
    ]


def prepare_kernel(
    half, pieces, tok_hbm, w_hbm, logit_hbm, decay_hbm, og_hbm,
    w_ref, og_ref, unit_ref, scale_ref, lane_ref, col_ref, u_ref, wk_ref, dbt_ref, ktt_ref, gt_ref,
    keep_ref, send_ref,
    tok_scr, logit_ref, decay_ref, value_scr, pay_scr, gamma_scr, pair_scr, tok_sem, w_sem, more_sem,
):
    heads, size = decay_ref.shape
    members, depth, columns = w_ref.shape
    width = columns // heads
    chunk = depth // pieces

    def part(i):
        return pl.ds(i * chunk, chunk)

    tok_copies = [
        pltpu.make_async_copy(tok_hbm.at[:, part(i)], tok_scr.at[:, part(i)], tok_sem.at[i])
        for i in range(pieces)
    ]
    w_copies = [
        [
            pltpu.make_async_copy(w_hbm.at[p, part(i)], w_ref.at[p, part(i)], w_sem.at[p, i])
            for i in range(pieces)
        ]
        for p in range(members)
    ]
    small = [(logit_hbm, logit_ref), (decay_hbm, decay_ref), (og_hbm, og_ref)]
    small = [pltpu.make_async_copy(a, b, more_sem.at[i]) for i, (a, b) in enumerate(small)]
    for copy in small[:2]:
        copy.start()
    for i in range(pieces):
        tok_copies[i].start()
        w_copies[1][i].start()
    small[2].start()

    def product(p, i):
        span = slice(i * chunk, (i + 1) * chunk)
        return nn(tok_scr[:, span], w_ref[p, span])

    every = range(heads)
    spans = [slice(h * width, (h + 1) * width) for h in every]
    for copy in small[:2]:
        copy.wait()
    lanes, cols_of = gates(logit_ref[...], decay_ref[...])
    lane_ref[...] = lanes
    col_ref[...] = cols_of
    rows, cols = grid_ids(size)
    causal = rows >= cols
    strict = rows > cols
    run_col = [cols_of[:, h : h + 1] for h in every]
    run_row = [lanes[h : h + 1, :] for h in every]
    beta = [cols_of[:, heads + h : heads + h + 1] for h in every]

    total = None
    for i in range(pieces):
        tok_copies[i].wait()
        w_copies[1][i].wait()
        if i == 0:
            for p in (2, 0):
                for copy in w_copies[p]:
                    copy.start()
        result = product(1, i)
        total = result if total is None else total + result

    def normalize(p, total):
        for h in every:
            unit, scale = unit_rows(total[:, spans[h]])
            unit_ref[p, :, spans[h]] = unit
            scale_ref[p, :, spans[h]] = scale

    small[2].wait()
    for h in every:
        gt_ref[h] = og_ref[:, spans[h]].astype(F32).T.astype(BF16)
    normalize(1, total)
    keys = [unit_ref[1, :, s] for s in spans]
    key_b = [k.astype(BF16) for k in keys]
    for h in every:
        gamma = jnp.exp(jnp.where(causal, run_col[h] - run_row[h], FAR))
        gamma_scr[h] = gamma
        pair_scr[h] = jnp.where(strict, beta[h] * gamma * nt(key_b[h], key_b[h]), 0.0)
    for i in range(pieces):
        w_copies[2][i].wait()
    waiting = [(p, i) for p in (2, 0) for i in range(pieces)]
    totals = {2: None, 0: None}

    def fill():
        if waiting:
            p, i = waiting.pop(0)
            if p == 0 and i == 0:
                for copy in w_copies[0]:
                    copy.wait()
            result = product(p, i)
            totals[p] = result if totals[p] is None else totals[p] + result

    inverse = unit_lower_inverse([pair_scr[h] for h in every], fill)
    while waiting:
        fill()
    value_scr[...] = totals[2]
    normalize(0, totals[0])
    queries = [unit_ref[0, :, s] for s in spans]
    scores = [(gamma_scr[h] * nt(queries[h].astype(BF16), key_b[h])).astype(BF16) for h in every]
    last = [run_col[h][size - 1 : size, :] for h in every]
    open_col = [jnp.exp(run_col[h]) for h in every]
    fade_row = [jnp.exp(last[h] - run_row[h]) for h in every]
    write_key = [beta[h] * open_col[h] * keys[h] for h in every]
    right = [
        jnp.concatenate([beta[h] * value_scr[:, spans[h]], write_key[h]], axis=1) for h in every
    ]
    solved = [right[h] + nn(inverse[h], right[h].astype(BF16)) for h in every]
    fade_t = [keys[h].T * fade_row[h] for h in every]
    left = [jnp.concatenate([nn(gt_ref[h], scores[h]), fade_t[h]], axis=0) for h in every]
    back = [left[h] + nn(left[h].astype(BF16), inverse[h]) for h in every]
    e_rows, e_cols = grid_ids(width)
    for h in every:
        fade_hi = fade_t[h].astype(BF16)
        fade_lo = (fade_t[h] - fade_hi.astype(F32)).astype(BF16)
        solved_hi = solved[h].astype(BF16)
        solved_lo = (solved[h][:, :width] - solved_hi[:, :width].astype(F32)).astype(BF16)
        state = nn(fade_hi, solved_hi)
        fill = state[:, :width] + nn(fade_lo, solved_hi[:, :width]) + nn(fade_hi, solved_lo)
        unit = jnp.where(e_rows == e_cols, jnp.exp(last[h]), 0.0)
        seed = nn(gt_ref[h], (open_col[h] * queries[h]).astype(BF16)) - nn(
            back[h][:width].astype(BF16), write_key[h].astype(BF16)
        )
        pay_scr[h, 0] = (unit - state[:, width:]).astype(BF16)
        pay_scr[h, 1] = fill.astype(BF16)
        pay_scr[h, 2] = seed.astype(BF16)
        u_ref[h] = solved[h][:, :width]
        wk_ref[h] = solved_hi[:, width:]
        dbt_ref[h] = back[h][:width]
        ktt_ref[h] = back[h][width:].astype(BF16)
    if half:
        core = lax.rem(lax.axis_index("seq"), 2)
        keep_ref[...] = pay_scr[pl.ds(core * half, half)]
        send_ref[...] = pay_scr[pl.ds((1 - core) * half, half)]
    else:
        keep_ref[...] = pay_scr[...]
        send_ref[...] = pay_scr[...]


def here():
    return pl.BlockSpec(memory_space=pltpu.VMEM)


def away():
    return pl.BlockSpec(memory_space=pltpu.HBM)


def limit(mebibytes):
    return pltpu.CompilerParams(vmem_limit_bytes=mebibytes * 2**20)


def prepare(tokens, weights, logit, decay, out_grad, half):
    heads, size = logit.shape
    members, depth, columns = weights.shape
    width = columns // heads
    part = half or heads
    pieces = 4 if depth % 512 == 0 else 1
    gate_rows = 2 * heads + -2 * heads % 8
    shapes = [
        ((members, depth, columns), BF16),
        ((size, columns), BF16),
        ((2, size, columns), F32),
        ((2, size, columns), F32),
        ((gate_rows, size), F32),
        ((size, gate_rows), F32),
        ((heads, size, width), F32),
        ((heads, size, width), BF16),
        ((heads, width, size), F32),
        ((heads, width, size), BF16),
        ((heads, width, size), BF16),
        ((part, 3, width, width), BF16),
        ((part, 3, width, width), BF16),
    ]
    return pl.pallas_call(
        functools.partial(prepare_kernel, half, pieces),
        in_specs=[away()] * 5,
        out_specs=[here()] * len(shapes),
        out_shape=[jax.ShapeDtypeStruct(*s) for s in shapes],
        scratch_shapes=[
            pltpu.VMEM((size, depth), BF16),
            pltpu.VMEM((heads, size), F32),
            pltpu.VMEM((heads, size), F32),
            pltpu.VMEM((size, columns), F32),
            pltpu.VMEM((heads, 3, width, width), BF16),
            pltpu.VMEM((heads, size, size), F32),
            pltpu.VMEM((heads, size, size), F32),
            pltpu.SemaphoreType.DMA((pieces,)),
            pltpu.SemaphoreType.DMA((members, pieces)),
            pltpu.SemaphoreType.DMA((3,)),
        ],
        compiler_params=limit(16),
        name="prepare",
    )(*(pltpu.with_memory_space_constraint(x, pltpu.HBM) for x in (tokens, weights, logit, decay, out_grad)))


def weigh_kernel(
    heads, lane_ref, col_ref,
    gamma_ref, turned_ref, strong_ref, strong_t_ref, open_ref, fade_ref, beta_ref,
):
    size = lane_ref.shape[1]
    width = open_ref.shape[2]
    rows, cols = grid_ids(size)
    for h in range(heads):
        run = col_ref[:, h : h + 1]
        gap = run - lane_ref[h : h + 1, :]
        gamma = jnp.exp(jnp.where(rows >= cols, gap, FAR))
        turned = jnp.exp(jnp.where(rows <= cols, -gap, FAR))
        gamma_ref[h] = gamma
        turned_ref[h] = turned
        beta = col_ref[:, heads + h : heads + h + 1]
        beta_row = lane_ref[heads + h : heads + h + 1, :]
        strong_ref[h] = jnp.where(rows > cols, beta * gamma, 0.0)
        strong_t_ref[h] = jnp.where(rows < cols, beta_row * turned, 0.0)
        open_ref[h] = jnp.broadcast_to(jnp.exp(run), (size, width))
        fade_ref[h] = jnp.broadcast_to(jnp.exp(run[size - 1 :, :] - run), (size, width))
        beta_ref[h] = jnp.broadcast_to(beta, (size, width))


def weigh(lanes, cols, heads, width):
    size = lanes.shape[1]
    shapes = [jax.ShapeDtypeStruct((heads, size, size), F32)] * 4
    shapes += [jax.ShapeDtypeStruct((heads, size, width), F32)] * 3
    return pl.pallas_call(
        functools.partial(weigh_kernel, heads),
        in_specs=[here()] * 2,
        out_specs=[here()] * len(shapes),
        out_shape=shapes,
        compiler_params=limit(8),
        name="weigh",
    )(lanes, cols)


def pair_kernel(levels, keep_ref, recv_ref, *pay_refs):
    place = lax.axis_index("seq")
    first = lax.rem(place, 2) == 0
    chip = place // 2

    def join(early, late):
        width = early.shape[-1]
        for h in range(keep_ref.shape[0]):
            ahead = nn(late[h, 0], jnp.concatenate([early[h, 1], early[h, 0]], axis=1))
            up = ahead[:, :width] + late[h, 1].astype(F32)
            down = nn(late[h, 2], early[h, 0]) + early[h, 2].astype(F32)
            joint = ahead[:, width:].astype(BF16)
            for level in range(levels):
                upward = lax.rem(chip // (1 << level), 2) == 0
                pay_refs[level][h, 0] = joint
                pay_refs[level][h, 1] = jnp.where(upward, up, down).astype(BF16)

    @pl.when(first)
    def _():
        join(keep_ref, recv_ref)

    @pl.when(jnp.logical_not(first))
    def _():
        join(recv_ref, keep_ref)


def join_pair(keep, recv, levels):
    half, _, width, _ = keep.shape
    shape = jax.ShapeDtypeStruct((half, 2, width, width), BF16)
    return pl.pallas_call(
        functools.partial(pair_kernel, levels),
        in_specs=[here()] * 2,
        out_specs=[here()] * levels,
        out_shape=[shape] * levels,
        compiler_params=limit(8),
        name="join_pair",
    )(keep, recv)


def scan_kernel(keep_ref, recv_ref, near_ref, far_ref, cross_ref, own_ref, send_ref, enter, leave):
    place = lax.axis_index("seq")
    first = lax.rem(place, 2) == 0
    chip = place // 2
    low = lax.rem(chip, 2) == 1
    high = chip // 2 == 1
    every = range(keep_ref.shape[0])

    def pairs(one, two):
        for h in every:

            @pl.when(high)
            def _():
                enter[h] = nn(two[h, 0], one[h, 1]) + two[h, 1].astype(F32)
                leave[h] = jnp.zeros_like(leave[h])

            @pl.when(jnp.logical_not(high))
            def _():
                leave[h] = nn(two[h, 1], one[h, 0]) + one[h, 1].astype(F32)
                enter[h] = jnp.zeros_like(enter[h])

    @pl.when(low)
    def _():
        pairs(cross_ref, far_ref)
        for h in every:
            top, rest = two_terms(enter[h])
            enter[h] = nn(near_ref[h, 0], top) + nn(near_ref[h, 0], rest) + near_ref[h, 1].astype(F32)

    @pl.when(jnp.logical_not(low))
    def _():
        pairs(far_ref, cross_ref)
        for h in every:
            top, rest = two_terms(leave[h])
            leave[h] = nn(top, near_ref[h, 0]) + nn(rest, near_ref[h, 0]) + near_ref[h, 1].astype(F32)

    def within(early, late, early_out, late_out):
        for h in every:
            top, rest = two_terms(enter[h])
            back, tail = two_terms(leave[h])
            middle = nn(early[h, 0], top) + nn(early[h, 0], rest) + early[h, 1].astype(F32)
            inner = nn(back, late[h, 0]) + nn(tail, late[h, 0]) + late[h, 2].astype(F32)
            early_out[h, 0] = top
            early_out[h, 1] = inner.astype(BF16)
            late_out[h, 0] = middle.astype(BF16)
            late_out[h, 1] = back

    @pl.when(first)
    def _():
        within(keep_ref, recv_ref, own_ref, send_ref)

    @pl.when(jnp.logical_not(first))
    def _():
        within(recv_ref, keep_ref, send_ref, own_ref)


def scan_chips(keep, recv, near, far, cross):
    half, _, width, _ = keep.shape
    shape = jax.ShapeDtypeStruct((half, 2, width, width), BF16)
    return pl.pallas_call(
        scan_kernel,
        in_specs=[here()] * 5,
        out_specs=[here()] * 2,
        out_shape=[shape] * 2,
        scratch_shapes=[pltpu.VMEM((half, width, width), F32)] * 2,
        compiler_params=limit(8),
        name="scan_chips",
    )(keep, recv, near, far, cross)


def part_at(slot, count):
    place = lax.axis_index("head")
    if count != 4:
        return lax.rem(place + slot + 1, count)
    if slot == 0:
        return 3 - place
    if slot == 3:
        return place
    low, high = ((2, 0), (3, 1)) if slot == 1 else ((1, 3), (0, 2))
    ends = jnp.where(place == 0, low[0], low[1])
    return jnp.where(place < 2, ends, jnp.where(place == 2, high[0], high[1]))


def base_of(part, many):
    if part is None:
        return 0
    core = lax.rem(lax.axis_index("seq"), 2)
    return many * (core if part == 0 else 1 - core)


def lanes_from(head, width, many=1):
    if isinstance(head, int):
        return slice(head * width, (head + many) * width)
    return pl.ds(pl.multiple_of(head * width, width * many), many * width)


def contract(base, refs, edge_ref, grad_ref):
    (unit_ref, u_ref, wk_ref, dbt_ref, ktt_ref, gt_ref, og_ref) = refs[:7]
    (gamma_ref, turned_ref, strong_ref, strong_t_ref, open_ref, fade_ref, beta_ref) = refs[7:]
    _, size, width = u_ref.shape
    every = range(edge_ref.shape[0])
    update = [(u_ref[base + i] - nn(wk_ref[base + i], edge_ref[i, 0])).astype(BF16) for i in every]
    delta_t = [dbt_ref[base + i] + nn(edge_ref[i, 1], ktt_ref[base + i]) for i in every]
    delta = [d.T for d in delta_t]
    slopes = []
    for i in every:
        h = base + i
        span = lanes_from(h, width)
        rows = jnp.concatenate([og_ref[:, span], delta[i].astype(BF16)], axis=0)
        lanes = nt(rows, update[i])
        turned = nn(update[i], jnp.concatenate([gt_ref[h], delta_t[i].astype(BF16)], axis=1))
        attend = (gamma_ref[h] * lanes[:size]).astype(BF16)
        attend_t = (turned_ref[h] * turned[:, :size]).astype(BF16)
        mix = (strong_ref[h] * lanes[size:] + strong_t_ref[h] * turned[:, size:]).astype(BF16)
        edge = nt(rows, edge_ref[i, 0])
        key_b = unit_ref[1, :, span].astype(BF16)
        inner = nn(jnp.concatenate([attend, mix], axis=0), key_b)
        dq = open_ref[h] * edge[:size] + inner[:size]
        dk = (
            nn(attend_t, unit_ref[0, :, span].astype(BF16))
            - inner[size:]
            + fade_ref[h] * nn(update[i], edge_ref[i, 1])
            - beta_ref[h] * open_ref[h] * edge[size:]
        )
        grad_ref[2, :, lanes_from(i, width)] = (beta_ref[h] * delta[i]).astype(BF16)
        slopes.append((dq, dk))
    return slopes


def project_out(base, slopes, unit_ref, scale_ref, grad_ref):
    width = slopes[0][0].shape[1]
    ones = jnp.ones((width, width), BF16)
    for i, pair in enumerate(slopes):
        span = lanes_from(base + i, width)
        for slot, slope in enumerate(pair):
            unit = unit_ref[slot, :, span]
            along = nn((unit * slope).astype(BF16), ones)
            change = scale_ref[slot, :, span] * (slope - unit * along)
            grad_ref[slot, :, lanes_from(i, width)] = change.astype(BF16)


def spread_grads(groups, w_ref, slot, count):
    step = w_ref.shape[1] // count
    rows = pl.ds(pl.multiple_of(part_at(slot, count) * step, step), step)
    total = None
    for base, width, grad_ref in groups:
        span = lanes_from(base, width, grad_ref.shape[2] // width)
        for member in (2, 0, 1):
            part = nt(grad_ref[member], w_ref[member, rows, span])
            total = part if total is None else total + part
    return total


def own_kernel(edge_ref, scale_ref, *refs):
    refs, grad_ref = refs[:-1], refs[-1]
    base = base_of(0, edge_ref.shape[0])
    slopes = contract(base, refs, edge_ref, grad_ref)
    project_out(base, slopes, refs[0], scale_ref, grad_ref)


def own_grads(edge, scale, prepared):
    many, _, width, _ = edge.shape
    size = scale.shape[1]
    return pl.pallas_call(
        own_kernel,
        in_specs=[here()] * (2 + len(prepared)),
        out_specs=here(),
        out_shape=jax.ShapeDtypeStruct((3, size, many * width), BF16),
        compiler_params=limit(12),
        name="own_grads",
    )(edge, scale, *prepared)


def grads_kernel(part, count, w_ref, edge_ref, scale_ref, *refs):
    refs, (grad_ref, out_ref) = refs[:-2], refs[-2:]
    done = []
    many, _, width, _ = edge_ref.shape
    base = base_of(part, many)
    if part is not None:
        refs, done = refs[:-1], [(base_of(0, many), width, refs[-1])]
    slopes = contract(base, refs, edge_ref, grad_ref)
    total = spread_grads(done, w_ref, 0, count)
    project_out(base, slopes, refs[0], scale_ref, grad_ref)
    last = spread_grads([(base, width, grad_ref)], w_ref, 0, count)
    out_ref[...] = (last if total is None else total + last).astype(out_ref.dtype)


def grads(weights, edge, scale, prepared, own):
    many, _, width, _ = edge.shape
    size = scale.shape[1]
    depth = weights.shape[1]
    count = lax.axis_size("head")
    more = [] if own is None else [own]
    return pl.pallas_call(
        functools.partial(grads_kernel, None if own is None else 1, count),
        in_specs=[here()] * (3 + len(prepared) + len(more)),
        out_specs=[here()] * 2,
        out_shape=[
            jax.ShapeDtypeStruct((3, size, many * width), BF16),
            jax.ShapeDtypeStruct((size, depth // count), BF16),
        ],
        compiler_params=limit(12),
        name="grads",
    )(weights, edge, scale, *prepared, *more)


def others_kernel(count, width, parts, w_ref, *refs):
    grad_refs, outs = refs[: len(parts)], refs[len(parts) :]
    groups = [
        (base_of(part, ref.shape[2] // width), width, ref) for part, ref in zip(parts, grad_refs)
    ]
    for i, out_ref in enumerate(outs):
        out_ref[...] = spread_grads(groups, w_ref, i + 1, count).astype(out_ref.dtype)


def others(weights, groups, width):
    size = groups[0].shape[1]
    count = lax.axis_size("head")
    step = weights.shape[1] // count
    kinds = [BF16] + [F32] * 2 if count == 4 else [BF16] * (count - 2) + [F32]
    parts = (None,) if len(groups) == 1 else (0, 1)
    return pl.pallas_call(
        functools.partial(others_kernel, count, width, parts),
        in_specs=[here()] * (1 + len(groups)),
        out_specs=[here()] * len(kinds),
        out_shape=[jax.ShapeDtypeStruct((size, step), k) for k in kinds],
        compiler_params=limit(8),
        name="others",
    )(weights, *groups)


def swap(value, axis, count, mask):
    return lax.ppermute(value, axis, [(i, i ^ mask) for i in range(count)])


def edges_by_pairs(keep, send, count):
    recv = swap(send, "seq", count, 1)
    low, high = join_pair(keep, recv, 2)
    far = swap(high, "seq", count, 4)
    cross = swap(high, "seq", count, 6)
    near = swap(low, "seq", count, 2)
    own, other = scan_chips(keep, recv, near, far, cross)
    return own, swap(other, "seq", count, 1)


def edges_by_gather(keep, count):
    place = lax.axis_index("seq")
    gathered = lax.all_gather(keep, "seq")
    product = functools.partial(jnp.einsum, "hij,hjk->hik", precision=HIGH)

    def take(j):
        return lax.dynamic_index_in_dim(gathered, j, 0, False).astype(F32)

    def forward(j, state):
        part = take(j)
        return product(part[:, 0], state) + part[:, 1]

    def backward(i, state):
        part = take(count - 1 - i)
        return product(state, part[:, 0]) + part[:, 2]

    vacant = jnp.zeros(keep.shape[:1] + keep.shape[2:], F32)
    enter = lax.fori_loop(0, place, forward, vacant)
    leave = lax.fori_loop(0, count - 1 - place, backward, vacant)
    own = jnp.stack([enter, leave], axis=1).astype(BF16)
    return own, own


def sum_on_line(blocks):
    count = lax.axis_size("head")
    right = left = None
    for turn in range(count - 1):
        onward = blocks[count - 1 - turn]
        back = blocks[turn + 1]
        if turn:
            onward = (onward.astype(F32) + right.astype(F32)).astype(BF16)
            back = (back.astype(F32) + left.astype(F32)).astype(BF16)
        right = lax.ppermute(onward, "head", [(i, i + 1) for i in range(turn + 1)])
        left = lax.ppermute(back, "head", [(count - 1 - i, count - 2 - i) for i in range(turn + 1)])
    total = blocks[0]
    if count > 1:
        total = total + right.astype(F32) + left.astype(F32)
    return total.astype(BF16)


def join_kernel(joint_ref, outer_ref, out_ref):
    place = lax.axis_index("head")
    inside = jnp.logical_or(place == 1, place == 2)

    @pl.when(inside)
    def _():
        out_ref[...] = (joint_ref[...] + outer_ref[...].astype(F32)).astype(BF16)

    @pl.when(jnp.logical_not(inside))
    def _():
        out_ref[...] = joint_ref[...].astype(BF16)


def join_outer(joint, outer):
    return pl.pallas_call(
        join_kernel,
        in_specs=[here()] * 2,
        out_specs=here(),
        out_shape=jax.ShapeDtypeStruct(joint.shape, BF16),
        compiler_params=limit(8),
        name="join_outer",
    )(joint, outer)


def sum_of_four(end, first, joint, own):
    outer = lax.ppermute(end, "head", [(0, 1), (1, 0), (2, 3), (3, 2)])
    inner = lax.ppermute(end, "head", [(1, 2), (2, 1)])
    joint = join_outer(joint, outer)
    joint = lax.ppermute(joint, "head", [(0, 1), (1, 3), (3, 2), (2, 0)])
    ring = lax.ppermute(first, "head", [(0, 2), (2, 3), (3, 1), (1, 0)])
    total = own + inner.astype(F32) + ring.astype(F32) + joint.astype(F32)
    return total.astype(BF16)


def step_on_device(tokens, qkv_weight, beta_logit, log_decay, out_grad):
    heads = beta_logit.shape[0]
    count = lax.axis_size("seq")
    paired = heads % 2 == 0 and count == 8
    half = heads // 2 if paired else 0
    held, kept_grad, unit, scale, lanes, col, u, wk, dbt, ktt, gt, keep, send = prepare(
        tokens, qkv_weight, beta_logit, log_decay, out_grad, half
    )
    if paired:
        own, recv = edges_by_pairs(keep, send, count)
    else:
        own, recv = edges_by_gather(keep, count)
    width = qkv_weight.shape[2] // heads
    prepared = (unit, u, wk, dbt, ktt, gt, kept_grad, *weigh(lanes, col, heads, width))
    if paired:
        own_part = own_grads(own, scale, prepared)
        grad, end = grads(held, recv, scale, prepared, own_part)
        groups = [own_part, grad]
    else:
        grad, end = grads(held, own, scale, prepared, None)
        groups = [grad]
    rest = others(held, groups, width)
    if lax.axis_size("head") == 4:
        return sum_of_four(end, *rest)
    return sum_on_line([rest[-1], end, *rest[:-1]])


def solution(mesh):
    return jax.shard_map(
        step_on_device,
        mesh=mesh,
        in_specs=(
            P("seq", None),
            P(None, None, "head"),
            P("head", "seq"),
            P("head", "seq"),
            P("seq", "head"),
        ),
        out_specs=P("seq", "head"),
        check_vma=False,
    )
```

```python
import functools

import jax
import jax.numpy as jnp
from jax import lax
from jax.experimental import pallas as pl
from jax.experimental.pallas import tpu as pltpu
from jax.sharding import PartitionSpec as P


F32 = jnp.float32
BF16 = jnp.bfloat16
HIGH = lax.Precision.HIGHEST
FAR = -1e30


def nn(a, b):
    return lax.dot_general(a, b, (((1,), (0,)), ((), ())), preferred_element_type=F32)


def nt(a, b):
    return lax.dot_general(a, b, (((1,), (1,)), ((), ())), preferred_element_type=F32)


def grid_ids(size):
    rows = lax.broadcasted_iota(jnp.int32, (size, size), 0)
    cols = lax.broadcasted_iota(jnp.int32, (size, size), 1)
    return rows, cols


def exact_terms(value):
    high = value.astype(BF16)
    left = value - high.astype(F32)
    mid = left.astype(BF16)
    return high, mid, (left - mid.astype(F32)).astype(BF16)


def gates(logit, decay):
    heads, size = decay.shape
    rows, cols = grid_ids(size)
    upper = jnp.where(rows <= cols, 1.0, 0.0).astype(BF16)
    high, mid, low = exact_terms(decay)
    run = nn(jnp.concatenate([high, mid, low], axis=0), upper)
    run = run[:heads] + run[heads : 2 * heads] + run[2 * heads :]
    lanes = [run, 1.0 / (1.0 + jnp.exp(-logit))]
    spare = -2 * heads % 8
    if spare:
        lanes.append(jnp.zeros((spare, size), F32))
    lanes = jnp.concatenate(lanes, axis=0)
    return lanes, lanes.T


def two_terms(value):
    high = value.astype(BF16)
    return high, (value - high.astype(F32)).astype(BF16)


def unit_rows(tensor):
    scale = lax.rsqrt(jnp.sum(tensor * tensor, axis=-1, keepdims=True) + 1e-06)
    scale = jnp.broadcast_to(scale, tensor.shape)
    return tensor * scale, scale


def unit_lower_inverse(couplings, fill):
    size = couplings[0].shape[0]
    base = size // 4
    lane_block = lax.broadcasted_iota(jnp.int32, (base, size), 1) // base
    on = [lane_block == b for b in range(4)]
    odd = lane_block % 2 == 1
    masks = [jnp.where(o, 1.0, 0.0).astype(BF16) for o in on]
    none = jnp.zeros((base, size), BF16)

    def strip(a, b):
        return a[b * base : (b + 1) * base]

    def spread(x):
        return jnp.concatenate([x * m for m in masks], axis=0)

    flat = [sum(jnp.where(on[b], strip(a, b), 0.0) for b in range(4)) for a in couplings]
    rest = [-x for x in flat]
    power = flat
    reach = 1
    while 2 * reach < base:
        narrow = [p.astype(BF16) for p in power]
        if reach == 1:
            power = [nn(p, spread(p)) for p in narrow]
            fill()
        else:
            both = [
                nn(jnp.concatenate([n.astype(BF16), p], axis=0), spread(p))
                for n, p in zip(rest, narrow)
            ]
            rest = [n + p + x[:base] for n, p, x in zip(rest, power, both)]
            power = [x[base:] for x in both]
            fill()
        reach *= 2
    if reach > 1:
        narrow = [p.astype(BF16) for p in power]
        rest = [n + p + nn(n.astype(BF16), spread(b)) for n, p, b in zip(rest, power, narrow)]
        fill()

    outer = [jnp.where(on[0], strip(a, 1), 0.0) + jnp.where(on[2], strip(a, 3), 0.0) for a in couplings]
    wide = [n.astype(BF16) for n in rest]
    half = [g + nn(g.astype(BF16), spread(n)) for g, n in zip(outer, wide)]
    half_b = [y.astype(BF16) for y in half]
    fill()
    late = [jnp.where(odd, n, 0.0) for n in rest]
    cross = [
        y + nn(l.astype(BF16), jnp.concatenate([none, b * masks[0], none, b * masks[2]], axis=0))
        for y, l, b in zip(half, late, half_b)
    ]
    fill()
    below = [l - z for l, z in zip(late, cross)]
    above = [jnp.where(odd, 0.0, n) for n in rest]
    mid = size // 2
    early = [jnp.concatenate([t[:, :mid], b[:, :mid]], axis=0).astype(BF16) for t, b in zip(above, below)]
    later = [jnp.concatenate([t[:, mid:], b[:, mid:]], axis=0).astype(BF16) for t, b in zip(above, below)]
    corner = [a[mid:, :mid] for a in couplings]
    half = [c + nn(c.astype(BF16), e) for c, e in zip(corner, early)]
    fill()
    cross = [y + nn(l, y.astype(BF16)) for y, l in zip(half, later)]
    blank = jnp.zeros((mid, mid), BF16)
    return [
        jnp.concatenate(
            [
                jnp.concatenate([e, blank], axis=1),
                jnp.concatenate([(-z).astype(BF16), l], axis=1),
            ],
            axis=0,
        )
        for e, z, l in zip(early, cross, later)
    ]


def prepare_kernel(
    part, many, pieces, tok_hbm, w_hbm, logit_hbm, decay_hbm, og_hbm,
    w_ref, og_ref, unit_ref, scale_ref, lane_ref, col_ref, gt_ref, value_scr, gamma_scr, inv_ref, open_ref, beta_ref,
    *more,
):
    out_refs, (tok_scr, logit_ref, decay_ref, pair_scr, tok_sem, w_sem, more_sem) = more[:5], more[5:]
    heads, size = decay_ref.shape
    members, depth, columns = w_ref.shape
    width = columns // heads
    chunk = depth // pieces

    def part(i):
        return pl.ds(i * chunk, chunk)

    tok_copies = [
        pltpu.make_async_copy(tok_hbm.at[:, part(i)], tok_scr.at[:, part(i)], tok_sem.at[i])
        for i in range(pieces)
    ]
    w_copies = [
        [
            pltpu.make_async_copy(w_hbm.at[p, part(i)], w_ref.at[p, part(i)], w_sem.at[p, i])
            for i in range(pieces)
        ]
        for p in range(members)
    ]
    small = [(logit_hbm, logit_ref), (decay_hbm, decay_ref), (og_hbm, og_ref)]
    small = [pltpu.make_async_copy(a, b, more_sem.at[i]) for i, (a, b) in enumerate(small)]
    for copy in small[:2]:
        copy.start()
    for i in range(pieces):
        tok_copies[i].start()
        w_copies[1][i].start()
    small[2].start()

    def product(p, i):
        span = slice(i * chunk, (i + 1) * chunk)
        return nn(tok_scr[:, span], w_ref[p, span])

    every = range(heads)
    spans = [slice(h * width, (h + 1) * width) for h in every]
    for copy in small[:2]:
        copy.wait()
    lanes, cols_of = gates(logit_ref[...], decay_ref[...])
    lane_ref[...] = lanes
    col_ref[...] = cols_of
    rows, cols = grid_ids(size)
    causal = rows >= cols
    strict = rows > cols
    run_col = [cols_of[:, h : h + 1] for h in every]
    run_row = [lanes[h : h + 1, :] for h in every]
    beta = [cols_of[:, heads + h : heads + h + 1] for h in every]

    total = None
    for i in range(pieces):
        tok_copies[i].wait()
        w_copies[1][i].wait()
        if i == 0:
            for p in (2, 0):
                for copy in w_copies[p]:
                    copy.start()
        result = product(1, i)
        total = result if total is None else total + result

    def normalize(p, total):
        for h in every:
            unit, scale = unit_rows(total[:, spans[h]])
            unit_ref[p, :, spans[h]] = unit
            scale_ref[p, :, spans[h]] = scale

    small[2].wait()
    for h in every:
        gt_ref[h] = og_ref[:, spans[h]].astype(F32).T.astype(BF16)
    normalize(1, total)
    keys = [unit_ref[1, :, s] for s in spans]
    key_b = [k.astype(BF16) for k in keys]
    for h in every:
        gamma = jnp.exp(jnp.where(causal, run_col[h] - run_row[h], FAR))
        gamma_scr[h] = gamma
        pair_scr[h] = jnp.where(strict, beta[h] * gamma * nt(key_b[h], key_b[h]), 0.0)
    for i in range(pieces):
        w_copies[2][i].wait()
    waiting = [(p, i) for p in (2, 0) for i in range(pieces)]
    totals = {2: None, 0: None}

    def fill():
        if waiting:
            p, i = waiting.pop(0)
            if p == 0 and i == 0:
                for copy in w_copies[0]:
                    copy.wait()
            result = product(p, i)
            totals[p] = result if totals[p] is None else totals[p] + result

    inverse = unit_lower_inverse([pair_scr[h] for h in every], fill)
    while waiting:
        fill()
    value_scr[...] = totals[2]
    normalize(0, totals[0])
    for h in every:
        inv_ref[h] = inverse[h]
        open_ref[h] = jnp.broadcast_to(jnp.exp(run_col[h]), (size, width))
        beta_ref[h] = jnp.broadcast_to(beta[h], (size, width))
    solve_heads(base_of(part, many), (unit_ref, value_scr, lane_ref, gamma_scr, inv_ref, open_ref, beta_ref, gt_ref), out_refs)


def solve_heads(base, refs, out_refs):
    unit_ref, value_ref, lane_ref, gamma_ref, inv_ref, open_ref, beta_ref, gt_ref = refs
    u_ref, wk_ref, dbt_ref, fade_ref, pay_ref = out_refs
    many, size, width = u_ref.shape
    every = range(many)
    heads = [base + i for i in every]
    spans = [lanes_from(h, width) for h in heads]
    keys = [unit_ref[1, :, s] for s in spans]
    queries = [unit_ref[0, :, s] for s in spans]
    inverse = [inv_ref[h] for h in heads]
    scores = [
        (gamma_ref[h] * nt(q.astype(BF16), k.astype(BF16))).astype(BF16)
        for h, q, k in zip(heads, queries, keys)
    ]
    run_row = [lane_ref[pl.ds(h, 1), :] for h in heads]
    last = [r[:, size - 1 :] for r in run_row]
    fade_row = [jnp.exp(a - r) for a, r in zip(last, run_row)]
    write_key = [beta_ref[h] * open_ref[h] * k for h, k in zip(heads, keys)]
    right = [
        jnp.concatenate([beta_ref[h] * value_ref[:, s], w], axis=1)
        for h, s, w in zip(heads, spans, write_key)
    ]
    solved = [r + nn(n, r.astype(BF16)) for r, n in zip(right, inverse)]
    fade_t = [k.T * f for k, f in zip(keys, fade_row)]
    left = [nn(gt_ref[h], p) for h, p in zip(heads, scores)]
    back = [x + nn(x.astype(BF16), n) for x, n in zip(left, inverse)]
    e_rows, e_cols = grid_ids(width)
    for i, h in enumerate(heads):
        fade_hi, fade_lo = two_terms(fade_t[i])
        solved_hi = solved[i].astype(BF16)
        solved_lo = (solved[i][:, :width] - solved_hi[:, :width].astype(F32)).astype(BF16)
        state = nn(fade_hi, solved_hi)
        fill = state[:, :width] + nn(fade_lo, solved_hi[:, :width]) + nn(fade_hi, solved_lo)
        unit = jnp.where(e_rows == e_cols, jnp.exp(last[i]), 0.0)
        seed = nn(gt_ref[h], (open_ref[h] * queries[i]).astype(BF16)) - nn(
            back[i].astype(BF16), write_key[i].astype(BF16)
        )
        pay_ref[i, 0] = (unit - state[:, width:]).astype(BF16)
        pay_ref[i, 1] = fill.astype(BF16)
        pay_ref[i, 2] = seed.astype(BF16)
        u_ref[i] = solved[i][:, :width]
        wk_ref[i] = solved_hi[:, width:]
        dbt_ref[i] = back[i]
        fade_ref[i] = fade_t[i]


def here():
    return pl.BlockSpec(memory_space=pltpu.VMEM)


def away():
    return pl.BlockSpec(memory_space=pltpu.HBM)


def limit(mebibytes):
    return pltpu.CompilerParams(vmem_limit_bytes=mebibytes * 2**20)


def solved_shapes(many, size, width):
    return [
        jax.ShapeDtypeStruct((many, size, width), F32),
        jax.ShapeDtypeStruct((many, size, width), BF16),
        jax.ShapeDtypeStruct((many, width, size), F32),
        jax.ShapeDtypeStruct((many, width, size), F32),
        jax.ShapeDtypeStruct((many, 3, width, width), BF16),
    ]


def prepare(tokens, weights, logit, decay, out_grad, half):
    heads, size = logit.shape
    members, depth, columns = weights.shape
    width = columns // heads
    pieces = 4 if depth % 512 == 0 else 1
    gate_rows = 2 * heads + -2 * heads % 8
    shapes = [
        ((members, depth, columns), BF16),
        ((size, columns), BF16),
        ((2, size, columns), F32),
        ((2, size, columns), F32),
        ((gate_rows, size), F32),
        ((size, gate_rows), F32),
        ((heads, width, size), BF16),
        ((size, columns), F32),
        ((heads, size, size), F32),
        ((heads, size, size), BF16),
        ((heads, size, width), F32),
        ((heads, size, width), F32),
    ]
    shapes = [jax.ShapeDtypeStruct(*s) for s in shapes]
    shapes += solved_shapes(half or heads, size, width)
    args = (tokens, weights, logit, decay, out_grad)
    return pl.pallas_call(
        functools.partial(prepare_kernel, 1 if half else None, half or heads, pieces),
        in_specs=[away()] * 5,
        out_specs=[here()] * len(shapes),
        out_shape=shapes,
        scratch_shapes=[
            pltpu.VMEM((size, depth), BF16),
            pltpu.VMEM((heads, size), F32),
            pltpu.VMEM((heads, size), F32),
            pltpu.VMEM((heads, size, size), F32),
            pltpu.SemaphoreType.DMA((pieces,)),
            pltpu.SemaphoreType.DMA((members, pieces)),
            pltpu.SemaphoreType.DMA((3,)),
        ],
        compiler_params=limit(16),
        name="prepare",
    )(*(pltpu.with_memory_space_constraint(x, pltpu.HBM) for x in args))


def solve_own_kernel(*refs):
    solve_heads(base_of(0, refs[8].shape[0]), refs[:8], refs[8:])


def solve_own(half, unit, value, lanes, gamma, inverse, opened, beta, gt):
    _, width, size = gt.shape
    shapes = solved_shapes(half, size, width)
    return pl.pallas_call(
        solve_own_kernel,
        in_specs=[here()] * 8,
        out_specs=[here()] * len(shapes),
        out_shape=shapes,
        compiler_params=limit(12),
        name="solve_own",
    )(unit, value, lanes, gamma, inverse, opened, beta, gt)


def weigh_kernel(heads, parts, lane_ref, col_ref, gamma_ref, inv_ref, *refs):
    fades, ktts = refs[: len(parts)], refs[len(parts) : 2 * len(parts)]
    turned_ref, strong_ref, strong_t_ref, fade_ref = refs[2 * len(parts) :]
    size = lane_ref.shape[1]
    width = fade_ref.shape[2]
    for part, fade_t_ref, ktt_ref in zip(parts, fades, ktts):
        many = fade_t_ref.shape[0]
        base = base_of(part, many)
        for i in range(many):
            fade_t = fade_t_ref[i]
            ktt_ref[i] = (fade_t + nn(fade_t.astype(BF16), inv_ref[base + i])).astype(BF16)
    rows, cols = grid_ids(size)
    for h in range(heads):
        run = col_ref[:, h : h + 1]
        gap = run - lane_ref[h : h + 1, :]
        turned = jnp.exp(jnp.where(rows <= cols, -gap, FAR))
        turned_ref[h] = turned
        beta = col_ref[:, heads + h : heads + h + 1]
        beta_row = lane_ref[heads + h : heads + h + 1, :]
        strong_ref[h] = jnp.where(rows > cols, beta * gamma_ref[h], 0.0)
        strong_t_ref[h] = jnp.where(rows < cols, beta_row * turned, 0.0)
        fade_ref[h] = jnp.broadcast_to(jnp.exp(run[size - 1 :, :] - run), (size, width))


def weigh(lanes, cols, gamma, inverse, fades):
    heads, size, _ = gamma.shape
    width = fades[0].shape[1]
    shapes = [jax.ShapeDtypeStruct(f.shape, BF16) for f in fades]
    shapes += [jax.ShapeDtypeStruct((heads, size, size), F32)] * 3
    shapes += [jax.ShapeDtypeStruct((heads, size, width), F32)]
    return pl.pallas_call(
        functools.partial(weigh_kernel, heads, (None,) if len(fades) == 1 else (0, 1)),
        in_specs=[here()] * (4 + len(fades)),
        out_specs=[here()] * len(shapes),
        out_shape=shapes,
        compiler_params=limit(8),
        name="weigh",
    )(lanes, cols, gamma, inverse, *fades)


def pair_kernel(levels, keep_ref, recv_ref, *pay_refs):
    place = lax.axis_index("seq")
    first = lax.rem(place, 2) == 0
    chip = place // 2

    def join(early, late):
        width = early.shape[-1]
        for h in range(keep_ref.shape[0]):
            ahead = nn(late[h, 0], jnp.concatenate([early[h, 1], early[h, 0]], axis=1))
            up = ahead[:, :width] + late[h, 1].astype(F32)
            down = nn(late[h, 2], early[h, 0]) + early[h, 2].astype(F32)
            joint = ahead[:, width:].astype(BF16)
            for level in range(levels):
                upward = lax.rem(chip // (1 << level), 2) == 0
                pay_refs[level][h, 0] = joint
                pay_refs[level][h, 1] = jnp.where(upward, up, down).astype(BF16)

    @pl.when(first)
    def _():
        join(keep_ref, recv_ref)

    @pl.when(jnp.logical_not(first))
    def _():
        join(recv_ref, keep_ref)


def join_pair(keep, recv, levels):
    half, _, width, _ = keep.shape
    shape = jax.ShapeDtypeStruct((half, 2, width, width), BF16)
    return pl.pallas_call(
        functools.partial(pair_kernel, levels),
        in_specs=[here()] * 2,
        out_specs=[here()] * levels,
        out_shape=[shape] * levels,
        compiler_params=limit(8),
        name="join_pair",
    )(keep, recv)


def scan_kernel(keep_ref, recv_ref, near_ref, far_ref, cross_ref, own_ref, send_ref, enter, leave):
    place = lax.axis_index("seq")
    first = lax.rem(place, 2) == 0
    chip = place // 2
    low = lax.rem(chip, 2) == 1
    high = chip // 2 == 1
    every = range(keep_ref.shape[0])

    def pairs(one, two):
        for h in every:

            @pl.when(high)
            def _():
                enter[h] = nn(two[h, 0], one[h, 1]) + two[h, 1].astype(F32)
                leave[h] = jnp.zeros_like(leave[h])

            @pl.when(jnp.logical_not(high))
            def _():
                leave[h] = nn(two[h, 1], one[h, 0]) + one[h, 1].astype(F32)
                enter[h] = jnp.zeros_like(enter[h])

    @pl.when(low)
    def _():
        pairs(cross_ref, far_ref)
        for h in every:
            top, rest = two_terms(enter[h])
            enter[h] = nn(near_ref[h, 0], top) + nn(near_ref[h, 0], rest) + near_ref[h, 1].astype(F32)

    @pl.when(jnp.logical_not(low))
    def _():
        pairs(far_ref, cross_ref)
        for h in every:
            top, rest = two_terms(leave[h])
            leave[h] = nn(top, near_ref[h, 0]) + nn(rest, near_ref[h, 0]) + near_ref[h, 1].astype(F32)

    def within(early, late, early_out, late_out):
        for h in every:
            top, rest = two_terms(enter[h])
            back, tail = two_terms(leave[h])
            middle = nn(early[h, 0], top) + nn(early[h, 0], rest) + early[h, 1].astype(F32)
            inner = nn(back, late[h, 0]) + nn(tail, late[h, 0]) + late[h, 2].astype(F32)
            early_out[h, 0] = top
            early_out[h, 1] = inner.astype(BF16)
            late_out[h, 0] = middle.astype(BF16)
            late_out[h, 1] = back

    @pl.when(first)
    def _():
        within(keep_ref, recv_ref, own_ref, send_ref)

    @pl.when(jnp.logical_not(first))
    def _():
        within(recv_ref, keep_ref, send_ref, own_ref)


def scan_chips(keep, recv, near, far, cross):
    half, _, width, _ = keep.shape
    shape = jax.ShapeDtypeStruct((half, 2, width, width), BF16)
    return pl.pallas_call(
        scan_kernel,
        in_specs=[here()] * 5,
        out_specs=[here()] * 2,
        out_shape=[shape] * 2,
        scratch_shapes=[pltpu.VMEM((half, width, width), F32)] * 2,
        compiler_params=limit(8),
        name="scan_chips",
    )(keep, recv, near, far, cross)


def part_at(slot, count):
    place = lax.axis_index("head")
    if count != 4:
        return lax.rem(place + slot + 1, count)
    if slot == 0:
        return 3 - place
    if slot == 3:
        return place
    low, high = ((2, 0), (3, 1)) if slot == 1 else ((1, 3), (0, 2))
    ends = jnp.where(place == 0, low[0], low[1])
    return jnp.where(place < 2, ends, jnp.where(place == 2, high[0], high[1]))


def base_of(part, many):
    if part is None:
        return 0
    core = lax.rem(lax.axis_index("seq"), 2)
    return many * (core if part == 0 else 1 - core)


def lanes_from(head, width, many=1):
    if isinstance(head, int):
        return slice(head * width, (head + many) * width)
    return pl.ds(pl.multiple_of(head * width, width * many), many * width)


def contract(base, refs, edge_ref, grad_ref):
    (unit_ref, u_ref, wk_ref, dbt_ref, ktt_ref, gt_ref, og_ref) = refs[:7]
    (gamma_ref, open_ref, beta_ref, turned_ref, strong_ref, strong_t_ref, fade_ref) = refs[7:]
    _, size, width = u_ref.shape
    every = range(edge_ref.shape[0])
    update = [(u_ref[i] - nn(wk_ref[i], edge_ref[i, 0])).astype(BF16) for i in every]
    delta_t = [dbt_ref[i] + nn(edge_ref[i, 1], ktt_ref[i]) for i in every]
    delta = [d.T for d in delta_t]
    slopes = []
    for i in every:
        h = base + i
        span = lanes_from(h, width)
        rows = jnp.concatenate([og_ref[:, span], delta[i].astype(BF16)], axis=0)
        lanes = nt(rows, update[i])
        turned = nn(update[i], jnp.concatenate([gt_ref[h], delta_t[i].astype(BF16)], axis=1))
        attend = (gamma_ref[h] * lanes[:size]).astype(BF16)
        attend_t = (turned_ref[h] * turned[:, :size]).astype(BF16)
        mix = (strong_ref[h] * lanes[size:] + strong_t_ref[h] * turned[:, size:]).astype(BF16)
        edge = nt(rows, edge_ref[i, 0])
        key_b = unit_ref[1, :, span].astype(BF16)
        inner = nn(jnp.concatenate([attend, mix], axis=0), key_b)
        dq = open_ref[h] * edge[:size] + inner[:size]
        dk = (
            nn(attend_t, unit_ref[0, :, span].astype(BF16))
            - inner[size:]
            + fade_ref[h] * nn(update[i], edge_ref[i, 1])
            - beta_ref[h] * open_ref[h] * edge[size:]
        )
        grad_ref[2, :, lanes_from(i, width)] = (beta_ref[h] * delta[i]).astype(BF16)
        slopes.append((dq, dk))
    return slopes


def project_out(base, slopes, unit_ref, scale_ref, grad_ref):
    width = slopes[0][0].shape[1]
    ones = jnp.ones((width, width), BF16)
    for i, pair in enumerate(slopes):
        span = lanes_from(base + i, width)
        for slot, slope in enumerate(pair):
            unit = unit_ref[slot, :, span]
            along = nn((unit * slope).astype(BF16), ones)
            change = scale_ref[slot, :, span] * (slope - unit * along)
            grad_ref[slot, :, lanes_from(i, width)] = change.astype(BF16)


def spread_grads(groups, w_ref, slot, count):
    step = w_ref.shape[1] // count
    rows = pl.ds(pl.multiple_of(part_at(slot, count) * step, step), step)
    total = None
    for base, width, grad_ref in groups:
        span = lanes_from(base, width, grad_ref.shape[2] // width)
        for member in (2, 0, 1):
            part = nt(grad_ref[member], w_ref[member, rows, span])
            total = part if total is None else total + part
    return total


def own_kernel(count, w_ref, edge_ref, scale_ref, *refs):
    refs, (grad_ref, out_ref) = refs[:-2], refs[-2:]
    many, _, width, _ = edge_ref.shape
    base = base_of(0, many)
    slopes = contract(base, refs, edge_ref, grad_ref)
    project_out(base, slopes, refs[0], scale_ref, grad_ref)
    out_ref[...] = spread_grads([(base, width, grad_ref)], w_ref, 0, count)


def own_grads(weights, edge, scale, prepared):
    many, _, width, _ = edge.shape
    size = scale.shape[1]
    count = lax.axis_size("head")
    return pl.pallas_call(
        functools.partial(own_kernel, count),
        in_specs=[here()] * (3 + len(prepared)),
        out_specs=[here()] * 2,
        out_shape=[
            jax.ShapeDtypeStruct((3, size, many * width), BF16),
            jax.ShapeDtypeStruct((size, weights.shape[1] // count), F32),
        ],
        compiler_params=limit(12),
        name="own_grads",
    )(weights, edge, scale, *prepared)


def grads_kernel(part, count, w_ref, edge_ref, scale_ref, *refs):
    refs, (grad_ref, out_ref) = refs[:-2], refs[-2:]
    many, _, width, _ = edge_ref.shape
    base = base_of(part, many)
    if part is not None:
        refs, done_ref = refs[:-1], refs[-1]
    slopes = contract(base, refs, edge_ref, grad_ref)
    project_out(base, slopes, refs[0], scale_ref, grad_ref)
    total = spread_grads([(base, width, grad_ref)], w_ref, 0, count)
    if part is not None:
        total = total + done_ref[...]
    out_ref[...] = total.astype(out_ref.dtype)


def grads(weights, edge, scale, prepared, own):
    many, _, width, _ = edge.shape
    size = scale.shape[1]
    depth = weights.shape[1]
    count = lax.axis_size("head")
    more = [] if own is None else [own]
    return pl.pallas_call(
        functools.partial(grads_kernel, None if own is None else 1, count),
        in_specs=[here()] * (3 + len(prepared) + len(more)),
        out_specs=[here()] * 2,
        out_shape=[
            jax.ShapeDtypeStruct((3, size, many * width), BF16),
            jax.ShapeDtypeStruct((size, depth // count), BF16),
        ],
        compiler_params=limit(12),
        name="grads",
    )(weights, edge, scale, *prepared, *more)


def others_kernel(count, width, parts, w_ref, *refs):
    grad_refs, outs = refs[: len(parts)], refs[len(parts) :]
    groups = [
        (base_of(part, ref.shape[2] // width), width, ref) for part, ref in zip(parts, grad_refs)
    ]
    for i, out_ref in enumerate(outs):
        out_ref[...] = spread_grads(groups, w_ref, i + 1, count).astype(out_ref.dtype)


def others(weights, groups, width):
    size = groups[0].shape[1]
    count = lax.axis_size("head")
    step = weights.shape[1] // count
    kinds = [BF16] + [F32] * 2 if count == 4 else [BF16] * (count - 2) + [F32]
    parts = (None,) if len(groups) == 1 else (0, 1)
    return pl.pallas_call(
        functools.partial(others_kernel, count, width, parts),
        in_specs=[here()] * (1 + len(groups)),
        out_specs=[here()] * len(kinds),
        out_shape=[jax.ShapeDtypeStruct((size, step), k) for k in kinds],
        compiler_params=limit(8),
        name="others",
    )(weights, *groups)


def swap(value, axis, count, mask):
    return lax.ppermute(value, axis, [(i, i ^ mask) for i in range(count)])


def swap_pay(pay, count):
    return swap(pay, "seq", count, 1)


def edges_by_pairs(keep, recv, count):
    low, high = join_pair(keep, recv, 2)
    far = swap(high, "seq", count, 4)
    cross = swap(high, "seq", count, 6)
    near = swap(low, "seq", count, 2)
    own, other = scan_chips(keep, recv, near, far, cross)
    return own, other


def edges_by_gather(keep, count):
    place = lax.axis_index("seq")
    gathered = lax.all_gather(keep, "seq")
    product = functools.partial(jnp.einsum, "hij,hjk->hik", precision=HIGH)

    def take(j):
        return lax.dynamic_index_in_dim(gathered, j, 0, False).astype(F32)

    def forward(j, state):
        part = take(j)
        return product(part[:, 0], state) + part[:, 1]

    def backward(i, state):
        part = take(count - 1 - i)
        return product(state, part[:, 0]) + part[:, 2]

    vacant = jnp.zeros(keep.shape[:1] + keep.shape[2:], F32)
    enter = lax.fori_loop(0, place, forward, vacant)
    leave = lax.fori_loop(0, count - 1 - place, backward, vacant)
    own = jnp.stack([enter, leave], axis=1).astype(BF16)
    return own, own


def sum_on_line(blocks):
    count = lax.axis_size("head")
    right = left = None
    for turn in range(count - 1):
        onward = blocks[count - 1 - turn]
        back = blocks[turn + 1]
        if turn:
            onward = (onward.astype(F32) + right.astype(F32)).astype(BF16)
            back = (back.astype(F32) + left.astype(F32)).astype(BF16)
        right = lax.ppermute(onward, "head", [(i, i + 1) for i in range(turn + 1)])
        left = lax.ppermute(back, "head", [(count - 1 - i, count - 2 - i) for i in range(turn + 1)])
    total = blocks[0]
    if count > 1:
        total = total + right.astype(F32) + left.astype(F32)
    return total.astype(BF16)


def join_kernel(joint_ref, outer_ref, out_ref):
    place = lax.axis_index("head")
    inside = jnp.logical_or(place == 1, place == 2)

    @pl.when(inside)
    def _():
        out_ref[...] = (joint_ref[...] + outer_ref[...].astype(F32)).astype(BF16)

    @pl.when(jnp.logical_not(inside))
    def _():
        out_ref[...] = joint_ref[...].astype(BF16)


def join_outer(joint, outer):
    return pl.pallas_call(
        join_kernel,
        in_specs=[here()] * 2,
        out_specs=here(),
        out_shape=jax.ShapeDtypeStruct(joint.shape, BF16),
        compiler_params=limit(8),
        name="join_outer",
    )(joint, outer)


def sum_of_four(end, first, joint, own):
    outer = lax.ppermute(end, "head", [(0, 1), (1, 0), (2, 3), (3, 2)])
    inner = lax.ppermute(end, "head", [(1, 2), (2, 1)])
    joint = join_outer(joint, outer)
    joint = lax.ppermute(joint, "head", [(0, 1), (1, 3), (3, 2), (2, 0)])
    ring = lax.ppermute(first, "head", [(0, 2), (2, 3), (3, 1), (1, 0)])
    total = own + inner.astype(F32) + ring.astype(F32) + joint.astype(F32)
    return total.astype(BF16)


def step_on_device(tokens, qkv_weight, beta_logit, log_decay, out_grad):
    heads = beta_logit.shape[0]
    count = lax.axis_size("seq")
    paired = heads % 2 == 0 and count == 8
    half = heads // 2 if paired else 0
    held, kept_grad, unit, scale, lanes, col, gt, value, gamma, inverse, opened, beta, *first = prepare(
        tokens, qkv_weight, beta_logit, log_decay, out_grad, half
    )
    solved = [first]
    if paired:
        recv = swap_pay(first[4], count)
        mine = solve_own(half, unit, value, lanes, gamma, inverse, opened, beta, gt)
        solved = [mine, first]
        own, other = edges_by_pairs(mine[4], recv, count)
    else:
        own, _ = edges_by_gather(first[4], count)
    weighed = weigh(lanes, col, gamma, inverse, [x[3] for x in solved])
    ktts, weighed = weighed[: len(solved)], weighed[len(solved) :]

    def group(i):
        u, wk, dbt = solved[i][:3]
        return (unit, u, wk, dbt, ktts[i], gt, kept_grad, gamma, opened, beta, *weighed)

    width = qkv_weight.shape[2] // heads
    if paired:
        recv = swap(other, "seq", count, 1)
        own_part, own_end = own_grads(held, own, scale, group(0))
        grad, end = grads(held, recv, scale, group(1), own_end)
        groups = [own_part, grad]
    else:
        grad, end = grads(held, own, scale, group(0), None)
        groups = [grad]
    rest = others(held, groups, width)
    if lax.axis_size("head") == 4:
        return sum_of_four(end, *rest)
    return sum_on_line([rest[-1], end, *rest[:-1]])


def solution(mesh):
    return jax.shard_map(
        step_on_device,
        mesh=mesh,
        in_specs=(
            P("seq", None),
            P(None, None, "head"),
            P("head", "seq"),
            P("head", "seq"),
            P("seq", "head"),
        ),
        out_specs=P("seq", "head"),
        check_vma=False,
    )
```

```python
import functools

import jax
import jax.numpy as jnp
from jax import lax
from jax.experimental import pallas as pl
from jax.experimental.pallas import tpu as pltpu
from jax.sharding import PartitionSpec as P


F32 = jnp.float32
BF16 = jnp.bfloat16
HIGH = lax.Precision.HIGHEST
FAR = -1e30


def nn(a, b):
    return lax.dot_general(a, b, (((1,), (0,)), ((), ())), preferred_element_type=F32)


def nt(a, b):
    return lax.dot_general(a, b, (((1,), (1,)), ((), ())), preferred_element_type=F32)


def grid_ids(size):
    rows = lax.broadcasted_iota(jnp.int32, (size, size), 0)
    cols = lax.broadcasted_iota(jnp.int32, (size, size), 1)
    return rows, cols


def exact_terms(value):
    high = value.astype(BF16)
    left = value - high.astype(F32)
    mid = left.astype(BF16)
    return high, mid, (left - mid.astype(F32)).astype(BF16)


def gates(logit, decay):
    heads, size = decay.shape
    rows, cols = grid_ids(size)
    upper = jnp.where(rows <= cols, 1.0, 0.0).astype(BF16)
    high, mid, low = exact_terms(decay)
    run = nn(jnp.concatenate([high, mid, low], axis=0), upper)
    run = run[:heads] + run[heads : 2 * heads] + run[2 * heads :]
    lanes = [run, 1.0 / (1.0 + jnp.exp(-logit))]
    spare = -2 * heads % 8
    if spare:
        lanes.append(jnp.zeros((spare, size), F32))
    lanes = jnp.concatenate(lanes, axis=0)
    return lanes, lanes.T


def two_terms(value):
    high = value.astype(BF16)
    return high, (value - high.astype(F32)).astype(BF16)


def unit_rows(tensor):
    scale = lax.rsqrt(jnp.sum(tensor * tensor, axis=-1, keepdims=True) + 1e-06)
    scale = jnp.broadcast_to(scale, tensor.shape)
    return tensor * scale, scale


def unit_lower_inverse(couplings, fill):
    size = couplings[0].shape[0]
    base = size // 4
    lane_block = lax.broadcasted_iota(jnp.int32, (base, size), 1) // base
    on = [lane_block == b for b in range(4)]
    odd = lane_block % 2 == 1
    masks = [jnp.where(o, 1.0, 0.0).astype(BF16) for o in on]
    none = jnp.zeros((base, size), BF16)

    def strip(a, b):
        return a[b * base : (b + 1) * base]

    def spread(x):
        return jnp.concatenate([x * m for m in masks], axis=0)

    flat = [sum(jnp.where(on[b], strip(a, b), 0.0) for b in range(4)) for a in couplings]
    rest = [-x for x in flat]
    power = flat
    reach = 1
    while 2 * reach < base:
        narrow = [p.astype(BF16) for p in power]
        if reach == 1:
            power = [nn(p, spread(p)) for p in narrow]
            fill()
        else:
            both = [
                nn(jnp.concatenate([n.astype(BF16), p], axis=0), spread(p))
                for n, p in zip(rest, narrow)
            ]
            rest = [n + p + x[:base] for n, p, x in zip(rest, power, both)]
            power = [x[base:] for x in both]
            fill()
        reach *= 2
    if reach > 1:
        narrow = [p.astype(BF16) for p in power]
        rest = [n + p + nn(n.astype(BF16), spread(b)) for n, p, b in zip(rest, power, narrow)]
        fill()

    outer = [jnp.where(on[0], strip(a, 1), 0.0) + jnp.where(on[2], strip(a, 3), 0.0) for a in couplings]
    wide = [n.astype(BF16) for n in rest]
    half = [g + nn(g.astype(BF16), spread(n)) for g, n in zip(outer, wide)]
    half_b = [y.astype(BF16) for y in half]
    fill()
    late = [jnp.where(odd, n, 0.0) for n in rest]
    cross = [
        y + nn(l.astype(BF16), jnp.concatenate([none, b * masks[0], none, b * masks[2]], axis=0))
        for y, l, b in zip(half, late, half_b)
    ]
    fill()
    below = [l - z for l, z in zip(late, cross)]
    above = [jnp.where(odd, 0.0, n) for n in rest]
    mid = size // 2
    early = [jnp.concatenate([t[:, :mid], b[:, :mid]], axis=0).astype(BF16) for t, b in zip(above, below)]
    later = [jnp.concatenate([t[:, mid:], b[:, mid:]], axis=0).astype(BF16) for t, b in zip(above, below)]
    corner = [a[mid:, :mid] for a in couplings]
    half = [c + nn(c.astype(BF16), e) for c, e in zip(corner, early)]
    fill()
    cross = [y + nn(l, y.astype(BF16)) for y, l in zip(half, later)]
    blank = jnp.zeros((mid, mid), BF16)
    return [
        jnp.concatenate(
            [
                jnp.concatenate([e, blank], axis=1),
                jnp.concatenate([(-z).astype(BF16), l], axis=1),
            ],
            axis=0,
        )
        for e, z, l in zip(early, cross, later)
    ]


def prepare_kernel(
    part, many, pieces, tok_hbm, w_hbm, logit_hbm, decay_hbm, og_hbm,
    w_ref, og_ref, unit_ref, scale_ref, lane_ref, col_ref, gt_ref, value_scr, gamma_scr, inv_ref, open_ref, beta_ref,
    *more,
):
    out_refs, (tok_scr, logit_ref, decay_ref, pair_scr, tok_sem, w_sem, more_sem) = more[:5], more[5:]
    heads, size = decay_ref.shape
    members, depth, columns = w_ref.shape
    width = columns // heads
    chunk = depth // pieces

    def piece(i):
        return pl.ds(i * chunk, chunk)

    tok_copies = [
        pltpu.make_async_copy(tok_hbm.at[:, piece(i)], tok_scr.at[:, piece(i)], tok_sem.at[i])
        for i in range(pieces)
    ]
    w_copies = [
        [
            pltpu.make_async_copy(w_hbm.at[p, piece(i)], w_ref.at[p, piece(i)], w_sem.at[p, i])
            for i in range(pieces)
        ]
        for p in range(members)
    ]
    small = [(logit_hbm, logit_ref), (decay_hbm, decay_ref), (og_hbm, og_ref)]
    small = [pltpu.make_async_copy(a, b, more_sem.at[i]) for i, (a, b) in enumerate(small)]
    for copy in small[:2]:
        copy.start()
    for i in range(pieces):
        tok_copies[i].start()
        w_copies[1][i].start()
    small[2].start()

    def product(p, i):
        span = slice(i * chunk, (i + 1) * chunk)
        return nn(tok_scr[:, span], w_ref[p, span])

    every = range(heads)
    spans = [slice(h * width, (h + 1) * width) for h in every]
    for copy in small[:2]:
        copy.wait()
    lanes, cols_of = gates(logit_ref[...], decay_ref[...])
    lane_ref[...] = lanes
    col_ref[...] = cols_of
    rows, cols = grid_ids(size)
    causal = rows >= cols
    strict = rows > cols
    run_col = [cols_of[:, h : h + 1] for h in every]
    run_row = [lanes[h : h + 1, :] for h in every]
    beta = [cols_of[:, heads + h : heads + h + 1] for h in every]

    total = None
    for i in range(pieces):
        tok_copies[i].wait()
        w_copies[1][i].wait()
        if i == 0:
            for p in (2, 0):
                for copy in w_copies[p]:
                    copy.start()
        result = product(1, i)
        total = result if total is None else total + result

    def normalize(p, total):
        for h in every:
            unit, scale = unit_rows(total[:, spans[h]])
            unit_ref[p, :, spans[h]] = unit
            scale_ref[p, :, spans[h]] = scale

    small[2].wait()
    for h in every:
        gt_ref[h] = og_ref[:, spans[h]].astype(F32).T.astype(BF16)
    normalize(1, total)
    keys = [unit_ref[1, :, s] for s in spans]
    key_b = [k.astype(BF16) for k in keys]
    for h in every:
        gamma = jnp.exp(jnp.where(causal, run_col[h] - run_row[h], FAR))
        gamma_scr[h] = gamma
        pair_scr[h] = jnp.where(strict, beta[h] * gamma * nt(key_b[h], key_b[h]), 0.0)
    for i in range(pieces):
        w_copies[2][i].wait()
    waiting = [(p, i) for p in (2, 0) for i in range(pieces)]
    totals = {2: None, 0: None}

    def fill():
        if waiting:
            p, i = waiting.pop(0)
            if p == 0 and i == 0:
                for copy in w_copies[0]:
                    copy.wait()
            result = product(p, i)
            totals[p] = result if totals[p] is None else totals[p] + result

    inverse = unit_lower_inverse([pair_scr[h] for h in every], fill)
    while waiting:
        fill()
    value_scr[...] = totals[2]
    normalize(0, totals[0])
    for h in every:
        inv_ref[h] = inverse[h]
        open_ref[h] = jnp.broadcast_to(jnp.exp(run_col[h]), (size, width))
        beta_ref[h] = jnp.broadcast_to(beta[h], (size, width))
    solve_heads(base_of(part, many), (unit_ref, value_scr, lane_ref, gamma_scr, inv_ref, open_ref, beta_ref, gt_ref), out_refs)


def solve_heads(base, refs, out_refs):
    unit_ref, value_ref, lane_ref, gamma_ref, inv_ref, open_ref, beta_ref, gt_ref = refs
    u_ref, wk_ref, dbt_ref, fade_ref, pay_ref = out_refs
    many, size, width = u_ref.shape
    every = range(many)
    heads = [base + i for i in every]
    spans = [lanes_from(h, width) for h in heads]
    keys = [unit_ref[1, :, s] for s in spans]
    queries = [unit_ref[0, :, s] for s in spans]
    inverse = [inv_ref[h] for h in heads]
    scores = [
        (gamma_ref[h] * nt(q.astype(BF16), k.astype(BF16))).astype(BF16)
        for h, q, k in zip(heads, queries, keys)
    ]
    run_row = [lane_ref[pl.ds(h, 1), :] for h in heads]
    last = [r[:, size - 1 :] for r in run_row]
    fade_row = [jnp.exp(a - r) for a, r in zip(last, run_row)]
    write_key = [beta_ref[h] * open_ref[h] * k for h, k in zip(heads, keys)]
    right = [
        jnp.concatenate([beta_ref[h] * value_ref[:, s], w], axis=1)
        for h, s, w in zip(heads, spans, write_key)
    ]
    solved = [r + nn(n, r.astype(BF16)) for r, n in zip(right, inverse)]
    fade_t = [k.T * f for k, f in zip(keys, fade_row)]
    left = [nn(gt_ref[h], p) for h, p in zip(heads, scores)]
    back = [x + nn(x.astype(BF16), n) for x, n in zip(left, inverse)]
    e_rows, e_cols = grid_ids(width)
    for i, h in enumerate(heads):
        fade_hi, fade_lo = two_terms(fade_t[i])
        solved_hi = solved[i].astype(BF16)
        solved_lo = (solved[i][:, :width] - solved_hi[:, :width].astype(F32)).astype(BF16)
        state = nn(fade_hi, solved_hi)
        fill = state[:, :width] + nn(fade_lo, solved_hi[:, :width]) + nn(fade_hi, solved_lo)
        unit = jnp.where(e_rows == e_cols, jnp.exp(last[i]), 0.0)
        seed = nn(gt_ref[h], (open_ref[h] * queries[i]).astype(BF16)) - nn(
            back[i].astype(BF16), write_key[i].astype(BF16)
        )
        pay_ref[i, 0] = (unit - state[:, width:]).astype(BF16)
        pay_ref[i, 1] = fill.astype(BF16)
        pay_ref[i, 2] = seed.astype(BF16)
        u_ref[i] = solved[i][:, :width]
        wk_ref[i] = solved_hi[:, width:]
        dbt_ref[i] = back[i]
        fade_ref[i] = fade_t[i]


def here():
    return pl.BlockSpec(memory_space=pltpu.VMEM)


def away():
    return pl.BlockSpec(memory_space=pltpu.HBM)


def limit(mebibytes):
    return pltpu.CompilerParams(vmem_limit_bytes=mebibytes * 2**20)


def solved_shapes(many, size, width):
    return [
        jax.ShapeDtypeStruct((many, size, width), F32),
        jax.ShapeDtypeStruct((many, size, width), BF16),
        jax.ShapeDtypeStruct((many, width, size), F32),
        jax.ShapeDtypeStruct((many, width, size), F32),
        jax.ShapeDtypeStruct((many, 3, width, width), BF16),
    ]


def prepare(tokens, weights, logit, decay, out_grad, half):
    heads, size = logit.shape
    members, depth, columns = weights.shape
    width = columns // heads
    pieces = 4 if depth % 512 == 0 else 1
    gate_rows = 2 * heads + -2 * heads % 8
    shapes = [
        ((members, depth, columns), BF16),
        ((size, columns), BF16),
        ((2, size, columns), F32),
        ((2, size, columns), F32),
        ((gate_rows, size), F32),
        ((size, gate_rows), F32),
        ((heads, width, size), BF16),
        ((size, columns), F32),
        ((heads, size, size), F32),
        ((heads, size, size), BF16),
        ((heads, size, width), F32),
        ((heads, size, width), F32),
    ]
    shapes = [jax.ShapeDtypeStruct(*s) for s in shapes]
    shapes += solved_shapes(half or heads, size, width)
    args = (tokens, weights, logit, decay, out_grad)
    return pl.pallas_call(
        functools.partial(prepare_kernel, 1 if half else None, half or heads, pieces),
        in_specs=[away()] * 5,
        out_specs=[here()] * len(shapes),
        out_shape=shapes,
        scratch_shapes=[
            pltpu.VMEM((size, depth), BF16),
            pltpu.VMEM((heads, size), F32),
            pltpu.VMEM((heads, size), F32),
            pltpu.VMEM((heads, size, size), F32),
            pltpu.SemaphoreType.DMA((pieces,)),
            pltpu.SemaphoreType.DMA((members, pieces)),
            pltpu.SemaphoreType.DMA((3,)),
        ],
        compiler_params=limit(16),
        name="prepare",
    )(*(pltpu.with_memory_space_constraint(x, pltpu.HBM) for x in args))


def solve_own_kernel(*refs):
    solve_heads(base_of(0, refs[8].shape[0]), refs[:8], refs[8:])


def solve_own(half, unit, value, lanes, gamma, inverse, opened, beta, gt):
    _, width, size = gt.shape
    shapes = solved_shapes(half, size, width)
    return pl.pallas_call(
        solve_own_kernel,
        in_specs=[here()] * 8,
        out_specs=[here()] * len(shapes),
        out_shape=shapes,
        compiler_params=limit(12),
        name="solve_own",
    )(unit, value, lanes, gamma, inverse, opened, beta, gt)


def weigh_kernel(heads, parts, lane_ref, col_ref, gamma_ref, inv_ref, *refs):
    fades, ktts = refs[: len(parts)], refs[len(parts) : 2 * len(parts)]
    turned_ref, strong_ref, strong_t_ref, fade_ref = refs[2 * len(parts) :]
    size = lane_ref.shape[1]
    width = fade_ref.shape[2]
    for part, fade_t_ref, ktt_ref in zip(parts, fades, ktts):
        many = fade_t_ref.shape[0]
        base = base_of(part, many)
        for i in range(many):
            fade_t = fade_t_ref[i]
            ktt_ref[i] = (fade_t + nn(fade_t.astype(BF16), inv_ref[base + i])).astype(BF16)
    rows, cols = grid_ids(size)
    for h in range(heads):
        run = col_ref[:, h : h + 1]
        gap = run - lane_ref[h : h + 1, :]
        turned = jnp.exp(jnp.where(rows <= cols, -gap, FAR))
        turned_ref[h] = turned
        beta = col_ref[:, heads + h : heads + h + 1]
        beta_row = lane_ref[heads + h : heads + h + 1, :]
        strong_ref[h] = jnp.where(rows > cols, beta * gamma_ref[h], 0.0)
        strong_t_ref[h] = jnp.where(rows < cols, beta_row * turned, 0.0)
        fade_ref[h] = jnp.broadcast_to(jnp.exp(run[size - 1 :, :] - run), (size, width))


def weigh(lanes, cols, gamma, inverse, fades):
    heads, size, _ = gamma.shape
    width = fades[0].shape[1]
    shapes = [jax.ShapeDtypeStruct(f.shape, BF16) for f in fades]
    shapes += [jax.ShapeDtypeStruct((heads, size, size), F32)] * 3
    shapes += [jax.ShapeDtypeStruct((heads, size, width), F32)]
    return pl.pallas_call(
        functools.partial(weigh_kernel, heads, (None,) if len(fades) == 1 else (0, 1)),
        in_specs=[here()] * (4 + len(fades)),
        out_specs=[here()] * len(shapes),
        out_shape=shapes,
        compiler_params=limit(8),
        name="weigh",
    )(lanes, cols, gamma, inverse, *fades)


def pair_kernel(levels, keep_ref, recv_ref, *pay_refs):
    place = lax.axis_index("seq")
    first = lax.rem(place, 2) == 0
    chip = place // 2

    def join(early, late):
        width = early.shape[-1]
        for h in range(keep_ref.shape[0]):
            ahead = nn(late[h, 0], jnp.concatenate([early[h, 1], early[h, 0]], axis=1))
            up = ahead[:, :width] + late[h, 1].astype(F32)
            down = nn(late[h, 2], early[h, 0]) + early[h, 2].astype(F32)
            joint = ahead[:, width:].astype(BF16)
            for level in range(levels):
                upward = lax.rem(chip // (1 << level), 2) == 0
                pay_refs[level][h, 0] = joint
                pay_refs[level][h, 1] = jnp.where(upward, up, down).astype(BF16)

    @pl.when(first)
    def _():
        join(keep_ref, recv_ref)

    @pl.when(jnp.logical_not(first))
    def _():
        join(recv_ref, keep_ref)


def join_pair(keep, recv, levels):
    half, _, width, _ = keep.shape
    shape = jax.ShapeDtypeStruct((half, 2, width, width), BF16)
    return pl.pallas_call(
        functools.partial(pair_kernel, levels),
        in_specs=[here()] * 2,
        out_specs=[here()] * levels,
        out_shape=[shape] * levels,
        compiler_params=limit(8),
        name="join_pair",
    )(keep, recv)


def scan_kernel(keep_ref, recv_ref, near_ref, far_ref, cross_ref, own_ref, send_ref, enter, leave):
    place = lax.axis_index("seq")
    first = lax.rem(place, 2) == 0
    chip = place // 2
    low = lax.rem(chip, 2) == 1
    high = chip // 2 == 1
    every = range(keep_ref.shape[0])

    def pairs(one, two):
        for h in every:

            @pl.when(high)
            def _():
                enter[h] = nn(two[h, 0], one[h, 1]) + two[h, 1].astype(F32)
                leave[h] = jnp.zeros_like(leave[h])

            @pl.when(jnp.logical_not(high))
            def _():
                leave[h] = nn(two[h, 1], one[h, 0]) + one[h, 1].astype(F32)
                enter[h] = jnp.zeros_like(enter[h])

    @pl.when(low)
    def _():
        pairs(cross_ref, far_ref)
        for h in every:
            top, rest = two_terms(enter[h])
            enter[h] = nn(near_ref[h, 0], top) + nn(near_ref[h, 0], rest) + near_ref[h, 1].astype(F32)

    @pl.when(jnp.logical_not(low))
    def _():
        pairs(far_ref, cross_ref)
        for h in every:
            top, rest = two_terms(leave[h])
            leave[h] = nn(top, near_ref[h, 0]) + nn(rest, near_ref[h, 0]) + near_ref[h, 1].astype(F32)

    def within(early, late, early_out, late_out):
        for h in every:
            top, rest = two_terms(enter[h])
            back, tail = two_terms(leave[h])
            middle = nn(early[h, 0], top) + nn(early[h, 0], rest) + early[h, 1].astype(F32)
            inner = nn(back, late[h, 0]) + nn(tail, late[h, 0]) + late[h, 2].astype(F32)
            early_out[h, 0] = top
            early_out[h, 1] = inner.astype(BF16)
            late_out[h, 0] = middle.astype(BF16)
            late_out[h, 1] = back

    @pl.when(first)
    def _():
        within(keep_ref, recv_ref, own_ref, send_ref)

    @pl.when(jnp.logical_not(first))
    def _():
        within(recv_ref, keep_ref, send_ref, own_ref)


def scan_chips(keep, recv, near, far, cross):
    half, _, width, _ = keep.shape
    shape = jax.ShapeDtypeStruct((half, 2, width, width), BF16)
    return pl.pallas_call(
        scan_kernel,
        in_specs=[here()] * 5,
        out_specs=[here()] * 2,
        out_shape=[shape] * 2,
        scratch_shapes=[pltpu.VMEM((half, width, width), F32)] * 2,
        compiler_params=limit(8),
        name="scan_chips",
    )(keep, recv, near, far, cross)


def part_at(slot, count):
    place = lax.axis_index("head")
    if count != 4:
        return lax.rem(place + slot + 1, count)
    if slot == 0:
        return 3 - place
    if slot == 3:
        return place
    low, high = ((2, 0), (3, 1)) if slot == 1 else ((1, 3), (0, 2))
    ends = jnp.where(place == 0, low[0], low[1])
    return jnp.where(place < 2, ends, jnp.where(place == 2, high[0], high[1]))


def base_of(part, many):
    if part is None:
        return 0
    core = lax.rem(lax.axis_index("seq"), 2)
    return many * (core if part == 0 else 1 - core)


def lanes_from(head, width, many=1):
    if isinstance(head, int):
        return slice(head * width, (head + many) * width)
    return pl.ds(pl.multiple_of(head * width, width * many), many * width)


def contract(base, refs, edge_ref, grad_ref):
    (unit_ref, u_ref, wk_ref, dbt_ref, ktt_ref, gt_ref, og_ref) = refs[:7]
    (gamma_ref, open_ref, beta_ref, turned_ref, strong_ref, strong_t_ref, fade_ref) = refs[7:]
    _, size, width = u_ref.shape
    every = range(edge_ref.shape[0])
    update = [(u_ref[i] - nn(wk_ref[i], edge_ref[i, 0])).astype(BF16) for i in every]
    delta_t = [dbt_ref[i] + nn(edge_ref[i, 1], ktt_ref[i]) for i in every]
    delta = [d.T for d in delta_t]
    slopes = []
    for i in every:
        h = base + i
        span = lanes_from(h, width)
        rows = jnp.concatenate([og_ref[:, span], delta[i].astype(BF16)], axis=0)
        lanes = nt(rows, update[i])
        turned = nn(update[i], jnp.concatenate([gt_ref[h], delta_t[i].astype(BF16)], axis=1))
        attend = (gamma_ref[h] * lanes[:size]).astype(BF16)
        attend_t = (turned_ref[h] * turned[:, :size]).astype(BF16)
        mix = (strong_ref[h] * lanes[size:] + strong_t_ref[h] * turned[:, size:]).astype(BF16)
        edge = nt(rows, edge_ref[i, 0])
        key_b = unit_ref[1, :, span].astype(BF16)
        inner = nn(jnp.concatenate([attend, mix], axis=0), key_b)
        dq = open_ref[h] * edge[:size] + inner[:size]
        dk = (
            nn(attend_t, unit_ref[0, :, span].astype(BF16))
            - inner[size:]
            + fade_ref[h] * nn(update[i], edge_ref[i, 1])
            - beta_ref[h] * open_ref[h] * edge[size:]
        )
        grad_ref[2, :, lanes_from(i, width)] = (beta_ref[h] * delta[i]).astype(BF16)
        slopes.append((dq, dk))
    return slopes


def project_out(base, slopes, unit_ref, scale_ref, grad_ref):
    width = slopes[0][0].shape[1]
    ones = jnp.ones((width, width), BF16)
    for i, pair in enumerate(slopes):
        span = lanes_from(base + i, width)
        for slot, slope in enumerate(pair):
            unit = unit_ref[slot, :, span]
            along = nn((unit * slope).astype(BF16), ones)
            change = scale_ref[slot, :, span] * (slope - unit * along)
            grad_ref[slot, :, lanes_from(i, width)] = change.astype(BF16)


def spread_grads(groups, w_ref, slot, count):
    step = w_ref.shape[1] // count
    rows = pl.ds(pl.multiple_of(part_at(slot, count) * step, step), step)
    total = None
    for base, width, grad_ref in groups:
        span = lanes_from(base, width, grad_ref.shape[2] // width)
        for member in (2, 0, 1):
            part = nt(grad_ref[member], w_ref[member, rows, span])
            total = part if total is None else total + part
    return total


def own_kernel(count, w_ref, edge_ref, scale_ref, *refs):
    refs, (grad_ref, out_ref) = refs[:-2], refs[-2:]
    many, _, width, _ = edge_ref.shape
    base = base_of(0, many)
    slopes = contract(base, refs, edge_ref, grad_ref)
    project_out(base, slopes, refs[0], scale_ref, grad_ref)
    out_ref[...] = spread_grads([(base, width, grad_ref)], w_ref, 0, count)


def own_grads(weights, edge, scale, prepared):
    many, _, width, _ = edge.shape
    size = scale.shape[1]
    count = lax.axis_size("head")
    return pl.pallas_call(
        functools.partial(own_kernel, count),
        in_specs=[here()] * (3 + len(prepared)),
        out_specs=[here()] * 2,
        out_shape=[
            jax.ShapeDtypeStruct((3, size, many * width), BF16),
            jax.ShapeDtypeStruct((size, weights.shape[1] // count), F32),
        ],
        compiler_params=limit(12),
        name="own_grads",
    )(weights, edge, scale, *prepared)


def grads_kernel(part, count, w_ref, edge_ref, scale_ref, *refs):
    refs, (grad_ref, out_ref) = refs[:-2], refs[-2:]
    many, _, width, _ = edge_ref.shape
    base = base_of(part, many)
    if part is not None:
        refs, done_ref = refs[:-1], refs[-1]
    slopes = contract(base, refs, edge_ref, grad_ref)
    project_out(base, slopes, refs[0], scale_ref, grad_ref)
    total = spread_grads([(base, width, grad_ref)], w_ref, 0, count)
    if part is not None:
        total = total + done_ref[...]
    out_ref[...] = total.astype(out_ref.dtype)


def grads(weights, edge, scale, prepared, own):
    many, _, width, _ = edge.shape
    size = scale.shape[1]
    depth = weights.shape[1]
    count = lax.axis_size("head")
    more = [] if own is None else [own]
    return pl.pallas_call(
        functools.partial(grads_kernel, None if own is None else 1, count),
        in_specs=[here()] * (3 + len(prepared) + len(more)),
        out_specs=[here()] * 2,
        out_shape=[
            jax.ShapeDtypeStruct((3, size, many * width), BF16),
            jax.ShapeDtypeStruct((size, depth // count), BF16),
        ],
        compiler_params=limit(12),
        name="grads",
    )(weights, edge, scale, *prepared, *more)


def others_kernel(count, width, parts, w_ref, *refs):
    grad_refs, outs = refs[: len(parts)], refs[len(parts) :]
    groups = [
        (base_of(part, ref.shape[2] // width), width, ref) for part, ref in zip(parts, grad_refs)
    ]
    for i, out_ref in enumerate(outs):
        out_ref[...] = spread_grads(groups, w_ref, i + 1, count).astype(out_ref.dtype)


def others(weights, groups, width):
    size = groups[0].shape[1]
    count = lax.axis_size("head")
    step = weights.shape[1] // count
    kinds = [BF16] + [F32] * 2 if count == 4 else [BF16] * (count - 2) + [F32]
    parts = (None,) if len(groups) == 1 else (0, 1)
    return pl.pallas_call(
        functools.partial(others_kernel, count, width, parts),
        in_specs=[here()] * (1 + len(groups)),
        out_specs=[here()] * len(kinds),
        out_shape=[jax.ShapeDtypeStruct((size, step), k) for k in kinds],
        compiler_params=limit(8),
        name="others",
    )(weights, *groups)


def swap(value, axis, count, mask):
    return lax.ppermute(value, axis, [(i, i ^ mask) for i in range(count)])


def swap_pay(pay, count):
    return swap(pay, "seq", count, 1)


def edges_by_pairs(keep, recv, count):
    low, high = join_pair(keep, recv, 2)
    far = swap(high, "seq", count, 4)
    cross = swap(high, "seq", count, 6)
    near = swap(low, "seq", count, 2)
    own, other = scan_chips(keep, recv, near, far, cross)
    return own, other


def edges_by_gather(keep, count):
    place = lax.axis_index("seq")
    gathered = lax.all_gather(keep, "seq")
    product = functools.partial(jnp.einsum, "hij,hjk->hik", precision=HIGH)

    def take(j):
        return lax.dynamic_index_in_dim(gathered, j, 0, False).astype(F32)

    def forward(j, state):
        part = take(j)
        return product(part[:, 0], state) + part[:, 1]

    def backward(i, state):
        part = take(count - 1 - i)
        return product(state, part[:, 0]) + part[:, 2]

    vacant = jnp.zeros(keep.shape[:1] + keep.shape[2:], F32)
    enter = lax.fori_loop(0, place, forward, vacant)
    leave = lax.fori_loop(0, count - 1 - place, backward, vacant)
    own = jnp.stack([enter, leave], axis=1).astype(BF16)
    return own, own


def sum_on_line(blocks):
    count = lax.axis_size("head")
    right = left = None
    for turn in range(count - 1):
        onward = blocks[count - 1 - turn]
        back = blocks[turn + 1]
        if turn:
            onward = (onward.astype(F32) + right.astype(F32)).astype(BF16)
            back = (back.astype(F32) + left.astype(F32)).astype(BF16)
        right = lax.ppermute(onward, "head", [(i, i + 1) for i in range(turn + 1)])
        left = lax.ppermute(back, "head", [(count - 1 - i, count - 2 - i) for i in range(turn + 1)])
    total = blocks[0]
    if count > 1:
        total = total + right.astype(F32) + left.astype(F32)
    return total.astype(BF16)


def join_kernel(joint_ref, outer_ref, out_ref):
    place = lax.axis_index("head")
    inside = jnp.logical_or(place == 1, place == 2)

    @pl.when(inside)
    def _():
        out_ref[...] = (joint_ref[...] + outer_ref[...].astype(F32)).astype(BF16)

    @pl.when(jnp.logical_not(inside))
    def _():
        out_ref[...] = joint_ref[...].astype(BF16)


def join_outer(joint, outer):
    return pl.pallas_call(
        join_kernel,
        in_specs=[here()] * 2,
        out_specs=here(),
        out_shape=jax.ShapeDtypeStruct(joint.shape, BF16),
        compiler_params=limit(8),
        name="join_outer",
    )(joint, outer)


def sum_of_four(end, first, joint, own):
    outer = lax.ppermute(end, "head", [(0, 1), (1, 0), (2, 3), (3, 2)])
    inner = lax.ppermute(end, "head", [(1, 2), (2, 1)])
    joint = join_outer(joint, outer)
    joint = lax.ppermute(joint, "head", [(0, 1), (1, 3), (3, 2), (2, 0)])
    ring = lax.ppermute(first, "head", [(0, 2), (2, 3), (3, 1), (1, 0)])
    total = own + inner.astype(F32) + ring.astype(F32) + joint.astype(F32)
    return total.astype(BF16)


def step_on_device(tokens, qkv_weight, beta_logit, log_decay, out_grad):
    heads = beta_logit.shape[0]
    count = lax.axis_size("seq")
    paired = heads % 2 == 0 and count == 8
    half = heads // 2 if paired else 0
    held, kept_grad, unit, scale, lanes, col, gt, value, gamma, inverse, opened, beta, *first = prepare(
        tokens, qkv_weight, beta_logit, log_decay, out_grad, half
    )
    solved = [first]
    if paired:
        recv = swap_pay(first[4], count)
        mine = solve_own(half, unit, value, lanes, gamma, inverse, opened, beta, gt)
        solved = [mine, first]
        own, other = edges_by_pairs(mine[4], recv, count)
    else:
        own, _ = edges_by_gather(first[4], count)
    weighed = weigh(lanes, col, gamma, inverse, [x[3] for x in solved])
    ktts, weighed = weighed[: len(solved)], weighed[len(solved) :]

    def group(i):
        u, wk, dbt = solved[i][:3]
        return (unit, u, wk, dbt, ktts[i], gt, kept_grad, gamma, opened, beta, *weighed)

    width = qkv_weight.shape[2] // heads
    if paired:
        recv = swap(other, "seq", count, 1)
        own_part, own_end = own_grads(held, own, scale, group(0))
        grad, end = grads(held, recv, scale, group(1), own_end)
        groups = [own_part, grad]
    else:
        grad, end = grads(held, own, scale, group(0), None)
        groups = [grad]
    rest = others(held, groups, width)
    if lax.axis_size("head") == 4:
        return sum_of_four(end, *rest)
    return sum_on_line([rest[-1], end, *rest[:-1]])


def solution(mesh):
    return jax.shard_map(
        step_on_device,
        mesh=mesh,
        in_specs=(
            P("seq", None),
            P(None, None, "head"),
            P("head", "seq"),
            P("head", "seq"),
            P("seq", "head"),
        ),
        out_specs=P("seq", "head"),
        check_vma=False,
    )
```
